32 devices in a mesh: dp: 8 (over z, y), seq: 4 (over x, core).
Axes of the slice: x: 2, y: 2, z: 4, core: 2. Of those that a mesh axis runs over, the one named last changes fastest.
Arguments:
- hidden: bfloat16 [16, 2048, 768], P('dp', 'seq'), may hold values from -6 to 6
- lengths: int32 [16], P('dp'), may hold values from 512 to 2048
- norm_gain: float32 [768], P(('dp', 'seq')), may hold values from 0.5 to 1.5
- in_weight: float32 [768, 3352], P(('dp', 'seq')), may hold values from -0.21875 to 0.21875
- conv_weight: float32 [4, 1792], P(None, ('dp', 'seq')), may hold values from -3 to 3
- conv_bias: float32 [1792], P(('dp', 'seq')), may hold values from -2.5 to 2.5
- step_bias: float32 [24], replicated, may hold values from -10 to -5
- decay_log: float32 [24], replicated, may hold values from 0 to 1
- skip_gain: float32 [24], replicated, may hold values from 0.5 to 1.5
- gate_gain: float32 [1536], P(('dp', 'seq')), may hold values from 0.5 to 1.5
- out_weight: float32 [1536, 768], P(('dp', 'seq')), may hold values from -0.15625 to 0.15625
- cotangent: bfloat16 [16, 2048, 768], P('dp', 'seq'), may hold values from -6 to 6
Outputs:
- output: bfloat16 [16, 2048, 768], P('dp', 'seq')
- grad_hidden: bfloat16 [16, 2048, 768], P('dp', 'seq')
- grad_norm_gain: float32 [768], P(('dp', 'seq'))
- grad_in_weight: float32 [768, 3352], P(('dp', 'seq'))
- grad_conv_weight: float32 [4, 1792], P(None, ('dp', 'seq'))
- grad_conv_bias: float32 [1792], P(('dp', 'seq'))
- grad_step_bias: float32 [24], replicated
- grad_decay_log: float32 [24], replicated
- grad_skip_gain: float32 [24], replicated
- grad_gate_gain: float32 [1536], P(('dp', 'seq'))
- grad_out_weight: float32 [1536, 768], P(('dp', 'seq'))
The draws below stay inside these ranges and needn't reach their ends.
All inputs are finite; a program needn't handle non-finite values.
Results may differ from the reference program's by a relative error of at most 0.00435.
The reference program's roundings to bfloat16 on the way count: a program that leaves them out, or rounds other values in their place, can miss the bound.
Values may be sent and summed in bfloat16 or wider, within the bound.
No kernel may reach another device: no remote copies, remote signals or barrier semaphores. Data moves between devices by JAX's collectives and lax.ppermute only.
A program may use at most 192 MiB of HBM per device.

```python
import jax
import jax.numpy as jnp
from jax import lax

D = 768
H = 24
P_SIZE = 64
N = 128
KW = 4
Q = 256
DI = 1536
CD = 1792
E = 3352
PIECE = 512
L = 2048
SEQS = 16


def plant(result, stream_key, least, high):
    shape = result.shape
    place = [jax.random.randint(jax.random.fold_in(stream_key, axis), (), 0, shape[axis]) for axis in range(len(shape))]
    result = result.at[tuple(place)].set(least)
    longest = shape.index(max(shape))
    place[longest] = (place[longest] + 1) % shape[longest]
    return result.at[tuple(place)].set(high)


def raised(array, rng, source, target, parts, factor):
    def block_of(axis_at):
        return (jnp.arange(array.shape[axis_at]) // (array.shape[axis_at] // parts)).reshape((-1,) + (1,) * (array.ndim - 1 - axis_at))

    first = jax.random.permutation(rng, parts)[block_of(target)]
    second = (block_of(target) + parts // 2) % parts
    return jnp.where((block_of(source) == first) | (block_of(source) == second), factor * array, array)


def shard_levels(key, extent, shards, low, top_value):
    def one(position, blocks):
        draws = jax.random.uniform(jax.random.fold_in(jax.random.fold_in(key, 6), position), (blocks,), jnp.float32, low / len(shards), top_value / len(shards))
        return jnp.repeat(jnp.exp(draws), extent[position] // blocks).reshape((-1,) + (1,) * (len(extent) - position - 1))

    gain = one(*shards[0])
    for cut in shards[1:]:
        gain = gain * one(*cut)
    return gain


def normal_values(own_key, dims, scale, most, pieces=(), kind=jnp.bfloat16):
    array = scale * jax.random.normal(own_key, dims, jnp.float32)
    if pieces:
        array = array * shard_levels(own_key, dims, pieces, -0.22, 0.18)
    return jnp.clip(array, -most, most).astype(kind)


def bell_draw_with(own_key, dims, scale, bound, split, heavy, held_as=jnp.bfloat16):
    drawn = scale * jax.random.normal(own_key, dims, jnp.float32)
    if split:
        drawn = drawn * shard_levels(own_key, dims, split, -0.22, 0.18)
    return jnp.clip(raised(drawn, jax.random.fold_in(own_key, 3), *heavy), -bound, bound).astype(held_as)


def setup_inputs(seed: int = 0) -> dict:
    key_list = jax.random.split(jax.random.key(seed), 13)
    hidden = bell_draw_with(key_list[0], (SEQS, L, D), 1.0, 6.0, ((0, 8), (1, 4)), (0, 2, 8, 2.0))
    lengths = plant(jax.random.randint(key_list[1], (SEQS,), PIECE, L + 1), jax.random.fold_in(key_list[1], 1), PIECE, L).astype(jnp.int32)
    norm_gain = jnp.clip(1.0 + 0.1 * jax.random.normal(key_list[2], (D,), jnp.float32), 0.5, 1.5)
    in_weight = normal_values(key_list[3], (D, E), D ** -0.5, 0.21875, ((0, 32),), jnp.float32)
    conv_weight = normal_values(key_list[4], (KW, CD), KW ** -0.5, 3.0, ((1, 32),), jnp.float32)
    conv_bias = normal_values(key_list[5], (CD,), 0.5, 2.5, ((0, 32),), jnp.float32)
    step_bias = jnp.clip(jax.random.uniform(key_list[6], (H,), jnp.float32, -10.0, -5.0), -10.0, -5.0)
    decay_log = jnp.clip(jax.random.uniform(key_list[7], (H,), jnp.float32, 0.0, 1.0), 0.0, 1.0)
    skip_gain = jnp.clip(jax.random.uniform(key_list[8], (H,), jnp.float32, 0.5, 1.5), 0.5, 1.5)
    gate_gain = jnp.clip(1.0 + 0.1 * jax.random.normal(key_list[9], (DI,), jnp.float32), 0.5, 1.5)
    out_weight = normal_values(key_list[10], (DI, D), DI ** -0.5, 0.15625, ((0, 32),), jnp.float32)
    cotangent = normal_values(key_list[11], (SEQS, L, D), 1.0, 6.0, ((0, 8), (1, 4)))
    return dict(hidden=hidden, lengths=lengths, norm_gain=norm_gain, in_weight=in_weight, conv_weight=conv_weight, conv_bias=conv_bias, step_bias=step_bias, decay_log=decay_log, skip_gain=skip_gain, gate_gain=gate_gain, out_weight=out_weight, cotangent=cotangent)


@jax.custom_vjp
def low(v):
    return lax.optimization_barrier(v.astype(jnp.bfloat16)).astype(jnp.float32)

@jax.custom_vjp
def low_back(v):
    return v

def low_keep(v):
    return (low(v), None)

def low_pass(kept, grad):
    return (grad,)

def back_keep(v):
    return (v, None)

def back_low(kept, grad):
    return (low(grad),)
low.defvjp(low_keep, low_pass)
low_back.defvjp(back_keep, back_low)
epsilon = 1e-05
highest = lax.Precision.HIGHEST

def rms_scale(values):
    return lax.rsqrt(lax.optimization_barrier(jnp.mean(values * values, axis=-1, keepdims=True)) + epsilon)

def decay_matrix(cum_group):
    width_q = cum_group.shape[-1]
    lower = jnp.arange(width_q)[:, None] >= jnp.arange(width_q)[None, :]
    gap = jnp.where(lower[None], cum_group[:, :, None] - cum_group[:, None, :], 0.0)
    return jnp.where(lower[None], jnp.exp(gap), 0.0)

def group_step(state, block_item):
    x_group, b_group, c_group, step_group, decay_group = block_item
    cum_decay = jnp.cumsum(decay_group, axis=0).T
    step_heads = step_group.T
    scores = low_back(jnp.dot(c_group, b_group.T, precision=highest))
    mixing = low(scores[None] * decay_matrix(cum_decay) * step_heads[:, None, :])
    intra_out = jnp.einsum('hqr,rhp->qhp', mixing, x_group, precision=highest)
    tail_weight = jnp.exp(cum_decay[:, -1:] - cum_decay) * step_heads
    b_scaled = low(b_group[None] * tail_weight[:, :, None])
    local_state = low_back(jnp.einsum('hqn,qhp->hnp', b_scaled, x_group, precision=highest))
    c_scaled = low(c_group[None] * jnp.exp(cum_decay)[:, :, None])
    inter_out = jnp.einsum('hqn,hnp->qhp', c_scaled, low(state), precision=highest)
    new_state = jnp.exp(cum_decay[:, -1])[:, None, None] * state + local_state
    return (new_state, intra_out + inter_out)

def block_forward(x_seq, valid_mask, weight_set):
    norm_gain, in_weight, conv_weight, conv_bias, step_bias, decay_log, skip_gain, gate_gain, out_weight = weight_set
    seq_len = x_seq.shape[0]
    normed = low(x_seq * rms_scale(x_seq) * low(norm_gain))
    projected = low_back(jnp.dot(normed, low(in_weight), precision=highest))
    gate_z = projected[:, :DI]
    conv_in = low(projected[:, DI:DI + CD])
    dt_raw = projected[:, DI + CD:]
    padded = jnp.pad(conv_in, ((KW - 1, 0), (0, 0)))
    kernel = low(conv_weight)
    pre_act = low(conv_bias) + sum((kernel[offset] * padded[offset:offset + seq_len] for offset in range(KW)))
    conv_out = jax.nn.silu(pre_act)
    x_heads = low(conv_out[:, :DI]).reshape(seq_len, H, P_SIZE)
    b_rows = low(conv_out[:, DI:DI + N])
    c_rows = low(conv_out[:, DI + N:])
    step_size = jax.nn.softplus(dt_raw + step_bias)
    log_decay = -step_size * jnp.exp(decay_log)
    group_count = seq_len // Q
    blocks = (x_heads.reshape(group_count, Q, H, P_SIZE), b_rows.reshape(group_count, Q, N), c_rows.reshape(group_count, Q, N), step_size.reshape(group_count, Q, H), log_decay.reshape(group_count, Q, H))
    first_state = jnp.zeros((H, N, P_SIZE), jnp.float32)
    final_state, mixed = lax.scan(jax.checkpoint(group_step), first_state, blocks)
    ssm_out = low_back(mixed.reshape(seq_len, H, P_SIZE) + skip_gain[None, :, None] * x_heads)
    gated_out = ssm_out.reshape(seq_len, DI) * jax.nn.silu(gate_z)
    gated_norm = low(gated_out * rms_scale(gated_out) * low(gate_gain))
    branch = jnp.dot(gated_norm, low(out_weight), precision=highest)
    return x_seq + valid_mask[:, None] * branch

def reference(hidden, lengths, norm_gain, in_weight, conv_weight, conv_bias, step_bias, decay_log, skip_gain, gate_gain, out_weight, cotangent):
    weight_set = (norm_gain, in_weight, conv_weight, conv_bias, step_bias, decay_log, skip_gain, gate_gain, out_weight)
    positions = jnp.arange(hidden.shape[1], dtype=jnp.int32)

    def one_sequence(totals, seq_item):
        x_seq, seq_len, cot_seq = seq_item
        valid_mask = (positions < seq_len).astype(jnp.float32)

        def forward(x_in, weight_args):
            return block_forward(x_in, valid_mask, weight_args)
        out_seq, pullback = jax.vjp(forward, x_seq.astype(jnp.float32), weight_set)
        grad_x, grad_weights = pullback(cot_seq.astype(jnp.float32))
        totals = jax.tree.map(lambda running_sum, addend: running_sum + addend, totals, grad_weights)
        return (totals, (out_seq.astype(jnp.bfloat16), grad_x.astype(jnp.bfloat16)))
    zeros = jax.tree.map(jnp.zeros_like, weight_set)
    totals, outs_pair = lax.scan(one_sequence, zeros, (hidden, lengths, cotangent))
    return (outs_pair[0], outs_pair[1], totals[0], totals[1], totals[2], totals[3], totals[4], totals[5], totals[6], totals[7], totals[8])
```

```python
import functools

import jax
import jax.numpy as jnp
from jax import lax
from jax.experimental import pallas as pl
from jax.experimental.pallas import tpu as pltpu
from jax.sharding import PartitionSpec as P

H = 24
P_SIZE = 64
N = 128
KW = 4
Q = 256
DI = 1536
CD = 1792
HL = 128
CW = CD + HL
CH = 256
HALF = 128
RIM = 16
PIECES = 32
NEG = -1e30

epsilon = 1e-05
low = jnp.bfloat16
f32 = jnp.float32
axes = ("dp", "seq")


def dot(left, right, dims):
    return lax.dot_general(left, right, (dims, ((), ())), preferred_element_type=f32)


def nn(left, right):
    return dot(left, right, ((1,), (0,)))


def nt(left, right):
    return dot(left, right, ((1,), (1,)))


def tn(left, right):
    return dot(left, right, ((0,), (0,)))


def split(value):
    top = value.astype(low)
    return top, (value - top.astype(f32)).astype(low)


def spread(parts, table):
    return nn(parts[0], table) + nn(parts[1], table)


def gather_heads(value, table):
    return spread(split(value), table)


def running_sum(value, reverse):
    rows = value.shape[0]
    at = lax.broadcasted_iota(jnp.int32, value.shape, 0)
    step = 1
    while step < rows:
        if reverse:
            value = value + jnp.where(at < rows - step, pltpu.roll(value, rows - step, 0), 0.0)
        else:
            value = value + jnp.where(at >= step, pltpu.roll(value, step, 0), 0.0)
        step *= 2
    return value


def softplus(value):
    tail = jnp.exp(-jnp.abs(value))
    series = tail * (1.0 - tail * (0.5 - tail * (1.0 / 3.0 - tail * (0.25 - tail * 0.2))))
    return jnp.maximum(value, 0.0) + jnp.where(tail < 0.03125, series, jnp.log(1.0 + tail))


def fold8(value):
    return jnp.sum(value.reshape(value.shape[0] // 8, 8, value.shape[1]), axis=0)


def pair_rows(me, own, other):
    first = (me & 1) == 0
    return jnp.concatenate([jnp.where(first, own, other), jnp.where(first, other, own)], axis=0)


def source_of(me, place):
    return me ^ ((place // 4) * 2) ^ ((place % 4) * 8)


def place_of(piece):
    return ((piece >> 1) & 3) * 4 + (piece >> 3)


def conv_kernel(
    groups, scal, x, halo, wa, wb, gain, cw, cb, sb, rate, e,
    nrm_o, nrmt_o, cie_o, xh_o, xs_o, wx_o, bc_o, step_o, cum_o, dtb_o, cumt_o,
    sloc_o, pre_o, r_o, tot_o, wc_o,
    nrm, cs, run, dec,
):
    block = pl.program_id(0)
    fresh = block % groups == 0

    @pl.when(block == 0)
    def assemble():
        me = scal[0]

        def one(place, carry):
            chip = source_of(me, place) >> 1
            own, other = wa[place].astype(f32), wb[place].astype(f32)
            wc_o[pl.ds(pl.multiple_of(chip * 48, 16), 48), :] = pair_rows(me, own, other).astype(low)
            return carry

        lax.fori_loop(0, PIECES // 2, one, 0)

    def normed(rows):
        wide = rows.astype(f32)
        scale = lax.rsqrt(jnp.mean(wide * wide, axis=-1, keepdims=True) + epsilon)
        return (wide * scale * gain[...]).astype(low)

    nrm[0:RIM, :] = normed(halo[...])
    for r in range(0, Q, 32):
        nrm[RIM + r : RIM + r + 32, :] = normed(x[r : r + 32, :])
    nrm_o[...] = nrm[RIM:, :]
    nrmt_o[...] = nrm[RIM:, :].T

    for c in range(0, CD, CH):
        cols = slice(c, c + CH)
        conv_in = nn(nrm[...], wc_o[:, cols]).astype(low)
        cie_o[:, cols] = conv_in
        cs[...] = conv_in.astype(f32)
        for r in range(0, Q, 32):
            taps = cw[0:1, cols] * cs[RIM - 3 + r : RIM + 29 + r, :]
            for k in range(1, KW):
                taps = taps + cw[k : k + 1, cols] * cs[RIM - 3 + k + r : RIM + 29 + k + r, :]
            pre = cb[:, cols] + taps
            act = (pre * jax.nn.sigmoid(pre)).astype(low)
            if c < DI:
                xh_o[r : r + 32, cols] = act
            else:
                bc_o[r : r + 32, :] = act

    dtb = nn(nrm[RIM:, :], wc_o[:, CD:CW]) + sb[...]
    step = softplus(dtb)
    cum = running_sum(-step * rate[...], False)
    step_o[...] = step
    cum_o[...] = cum
    dtb_o[...] = dtb
    cumt_o[...] = cum.T[0:H, :]
    last = cum[Q - 1 : Q, :]
    steps = split(step)
    tails = split(jnp.exp(last - cum) * step)
    decays = split(jnp.broadcast_to(jnp.exp(last), (8, HL)))
    for c in range(0, DI, CH):
        cols = slice(c, c + CH)
        table = e[:, cols]
        wide = xh_o[:, cols].astype(f32)
        xs_o[:, cols] = (spread(steps, table) * wide).astype(low)
        weighted = (spread(tails, table) * wide).astype(low)
        wx_o[:, cols] = weighted
        local = tn(bc_o[:, 0:N], weighted)
        decay = spread(decays, table)
        before = jnp.where(fresh, 0.0, run[:, cols])
        sloc_o[:, cols] = before
        after = decay[0:1, :] * before + local
        run[:, cols] = after
        r_o[:, cols] = after
        product = jnp.where(fresh, 1.0, dec[:, cols])
        pre_o[:, cols] = product
        product = product * decay
        dec[:, cols] = product
        tot_o[:, cols] = product


def intra_kernel(bc, xs, cum, cumt, o, sc):
    sc[...] = nt(bc[:, N : 2 * N], bc[:, 0:N])
    at = lax.broadcasted_iota(jnp.int32, (HALF, HALF), 0)
    to = lax.broadcasted_iota(jnp.int32, (HALF, HALF), 1)
    lower = at >= to
    left = lax.broadcasted_iota(jnp.int32, (Q, HALF), 1) < P_SIZE
    for pair in range(H // 2):
        cols = slice(pair * HALF, (pair + 1) * HALF)
        x_pair = xs[:, cols]
        tops, bottoms = [], []
        for h in (2 * pair, 2 * pair + 1):
            row = cumt[h : h + 1, :]
            upper_col, lower_col = cum[0:HALF, h : h + 1], cum[HALF:, h : h + 1]
            m00 = sc[0:HALF, 0:HALF] * jnp.exp(jnp.where(lower, upper_col - row[:, 0:HALF], NEG))
            m10 = sc[HALF:, 0:HALF] * jnp.exp(lower_col - row[:, 0:HALF])
            m11 = sc[HALF:, HALF:] * jnp.exp(jnp.where(lower, lower_col - row[:, HALF:], NEG))
            tops.append(nn(m00.astype(low), x_pair[0:HALF, :]))
            bottoms.append(nn(jnp.concatenate([m10.astype(low), m11.astype(low)], axis=1), x_pair))
        o[0:HALF, cols] = jnp.where(left[0:HALF], tops[0], tops[1])
        o[HALF:, cols] = jnp.where(left[0:HALF], bottoms[0], bottoms[1])


def valid_column(scal, groups, block):
    seq, group = block // groups, block % groups
    at = scal[1] * (groups * Q) + group * Q + lax.broadcasted_iota(jnp.int32, (Q, 1), 0)
    return (at < scal[2 + seq]).astype(f32)


def project_kernel(groups, scal, nrm, cot, wa, wb, z_o, dn_o, db_o, wz_o, wo_o):
    block = pl.program_id(0)

    @pl.when(block == 0)
    def assemble():
        me = scal[0]

        def halves(packed):
            return jnp.concatenate([packed[:, 0 : DI // 2], packed[:, DI // 2 :]], axis=0)

        def one(place, carry):
            chip = source_of(me, place) >> 1
            own, other = wa[place, 0].astype(f32), wb[place, 0].astype(f32)
            wz_o[pl.ds(pl.multiple_of(chip * 48, 16), 48), :] = pair_rows(me, own, other).astype(low)
            own, other = halves(wa[place, 1].astype(f32)), halves(wb[place, 1].astype(f32))
            wo_o[pl.ds(pl.multiple_of(chip * 96, 16), 96), :] = pair_rows(me, own, other).astype(low)
            return carry

        lax.fori_loop(0, PIECES // 2, one, 0)

    db_o[...] = (cot[...].astype(f32) * valid_column(scal, groups, block)).astype(low)
    for c in range(0, DI, CH):
        z_o[:, c : c + CH] = nn(nrm[...], wz_o[:, c : c + CH])
        dn_o[:, c : c + CH] = nt(db_o[...], wo_o[c : c + CH, :])


def gate_kernel(
    groups, scal, intra, xh, bc, cum, sloc, pre, inc, z, dn, hid, wo, gg, skip, e, et,
    out_o, dz_o, dy_o, gdy_o, gn_o, sbf_o, rs_o, dloc_o, suf_o, rd_o, tot_o, gacc_o, kacc_o,
    yi_s, ge_s, pr_s, y_s, sg_s, gt_s, run, dec,
):
    at = pl.program_id(0)
    fresh = at % groups == 0
    block = (at // groups) * groups + groups - 1 - at % groups

    @pl.when(at == 0)
    def start():
        gacc_o[...] = jnp.zeros_like(gacc_o)
        kacc_o[...] = jnp.zeros_like(kacc_o)

    c_rows = bc[:, N : 2 * N]
    growth = split(jnp.exp(cum[...]))
    for c in range(0, DI, CH):
        cols = slice(c, c + CH)
        begin = (sloc[:, cols] + pre[0:1, cols] * inc[:, cols].astype(f32)).astype(low)
        sbf_o[:, cols] = begin
        wide = spread(growth, e[:, cols])
        ge_s[:, cols] = wide
        yi_s[:, cols] = intra[:, cols] + wide * nn(c_rows, begin)

    def body(i, carry):
        rows = pl.ds(pl.multiple_of(i * 16, 16), 16)
        squares = jnp.zeros((16, HALF), f32)
        crosses = jnp.zeros((16, HALF), f32)
        for c in range(0, DI, HALF):
            cols = slice(c, c + HALF)
            zv = z[rows, cols]
            y = yi_s[rows, cols] + skip[:, cols] * xh[rows, cols].astype(f32)
            sig = jax.nn.sigmoid(zv)
            gated = y * (zv * sig)
            squares = squares + gated * gated
            crosses = crosses + (dn[rows, cols] * gg[:, cols]) * gated
            y_s[:, cols] = y
            sg_s[:, cols] = sig
            gt_s[:, cols] = gated
        scale = lax.rsqrt(jnp.sum(squares, axis=1, keepdims=True) / DI + epsilon)
        shift = scale * scale * scale * (jnp.sum(crosses, axis=1, keepdims=True) / DI)
        for c in range(0, DI, HALF):
            cols = slice(c, c + HALF)
            zv, y, sig, gated = z[rows, cols], y_s[:, cols], sg_s[:, cols], gt_s[:, cols]
            wide = dn[rows, cols]
            normal = gated * scale
            gn_o[rows, cols] = (normal * gg[:, cols]).astype(low)
            gacc_o[:, cols] += wide * normal
            d_gated = scale * (wide * gg[:, cols]) - gated * shift
            d_sig = d_gated * sig
            dz_o[rows, cols] = (d_sig * y * (1.0 + zv * (1.0 - sig))).astype(low)
            d_low = (d_sig * zv).astype(low)
            dy_o[rows, cols] = d_low
            d_y = d_low.astype(f32)
            kacc_o[:, cols] += d_y * xh[rows, cols].astype(f32)
            gdy_o[rows, cols] = (ge_s[rows, cols] * d_y).astype(low)
            pr_s[rows, cols] = d_y * yi_s[rows, cols]
        return carry

    lax.fori_loop(0, Q // 16, body, 0)

    valid = valid_column(scal, groups, block)
    for c in range(0, DI // 2, CH):
        branch = nn(gn_o[...], wo[:, c : c + CH])
        out_o[:, c : c + CH] = (hid[:, c : c + CH].astype(f32) + valid * branch).astype(low)
    decays = split(jnp.broadcast_to(jnp.exp(cum[Q - 1 : Q, :]), (8, HL)))
    sums = jnp.zeros((Q, HL), f32)
    for c in range(0, DI, CH):
        cols = slice(c, c + CH)
        sums = sums + gather_heads(pr_s[:, cols], et[cols, :])
        decay = spread(decays, e[:, cols])
        before = jnp.where(fresh, 0.0, run[:, cols])
        dloc_o[:, cols] = before
        after = decay[0:1, :] * before + tn(c_rows, gdy_o[:, cols])
        run[:, cols] = after
        rd_o[:, cols] = after
        product = jnp.where(fresh, 1.0, dec[:, cols])
        suf_o[:, cols] = product
        product = product * decay
        dec[:, cols] = product
        tot_o[:, cols] = product
    rs_o[...] = sums


def intra_back_kernel(bc, xs, xh, dy, step, cum, cumt, skip, e, et, dx_o, dbc_o, rs_o, sc, acc):
    sc[...] = nt(bc[:, 0:N], bc[:, N : 2 * N])
    acc[...] = jnp.zeros_like(acc)
    at = lax.broadcasted_iota(jnp.int32, (HALF, HALF), 0)
    to = lax.broadcasted_iota(jnp.int32, (HALF, HALF), 1)
    upper = at <= to
    left = lax.broadcasted_iota(jnp.int32, (Q, HALF), 1) < P_SIZE
    steps = split(step[...])
    sums = jnp.zeros((Q, HL), f32)
    for pair in range(H // 2):
        cols = slice(pair * HALF, (pair + 1) * HALF)
        dy_pair = dy[:, cols]
        x_pair = xs[:, cols]
        tops, bottoms = [], []
        for h in (2 * pair, 2 * pair + 1):
            keep = left if h % 2 == 0 else jnp.logical_not(left)
            x_half = jnp.where(keep, x_pair, jnp.zeros_like(x_pair))
            row = cumt[h : h + 1, :]
            first_col, second_col = cum[0:HALF, h : h + 1], cum[HALF:, h : h + 1]
            l00 = jnp.exp(jnp.where(upper, row[:, 0:HALF] - first_col, NEG))
            l01 = jnp.exp(row[:, HALF:] - first_col)
            l11 = jnp.exp(jnp.where(upper, row[:, HALF:] - second_col, NEG))
            m00 = (sc[0:HALF, 0:HALF] * l00).astype(low)
            m01 = (sc[0:HALF, HALF:] * l01).astype(low)
            m11 = (sc[HALF:, HALF:] * l11).astype(low)
            tops.append(nn(jnp.concatenate([m00, m01], axis=1), dy_pair))
            bottoms.append(nn(m11, dy_pair[HALF:, :]))
            grown = nt(x_half[0:HALF, :], dy_pair)
            acc[0:HALF, 0:HALF] += grown[:, 0:HALF] * l00
            acc[0:HALF, HALF:] += grown[:, HALF:] * l01
            acc[HALF:, HALF:] += nt(x_half[HALF:, :], dy_pair[HALF:, :]) * l11
        flow = jnp.concatenate(
            [
                jnp.where(left[0:HALF], tops[0], tops[1]),
                jnp.where(left[0:HALF], bottoms[0], bottoms[1]),
            ],
            axis=0,
        )
        sums = sums + gather_heads(flow * xh[:, cols].astype(f32), et[cols, :])
        dx_o[:, cols] = spread(steps, e[:, cols]) * flow + skip[:, cols] * dy_pair.astype(f32)
    rs_o[...] = sums
    scores = acc[...].astype(low)
    dbc_o[:, 0:N] = nn(scores, bc[:, N : 2 * N])
    dbc_o[:, N : 2 * N] = tn(scores, bc[:, 0:N])


def conv_back_kernel(
    groups, dloc, suf, inc, sbf, xh, wx, gdy, dx, dbc, bc, cum, step, dtb, rs1, rs2,
    cie, cw, cb, rate, e, et,
    dcv_o, kacc_o, hacc_o, head_o, tail_o,
    cs, ds, nxt,
):
    at = pl.program_id(0)
    fresh = at % groups == 0

    @pl.when(at == 0)
    def start():
        kacc_o[...] = jnp.zeros_like(kacc_o)
        hacc_o[...] = jnp.zeros_like(hacc_o)

    def conv_back(flow, c):
        cols = slice(c, c + CH)
        cs[...] = cie[:, cols].astype(f32)
        ds[0:8, :] = jnp.zeros((8, CH), f32)
        ds[8 + Q :, :] = jnp.where(fresh, 0.0, nxt[:, cols])
        taps = [cw[k : k + 1, cols] for k in range(KW)]
        sums = [jnp.zeros((8, CH), f32) for _ in range(KW + 1)]
        for r in range(0, Q, 32):
            views = [cs[RIM - 3 + k + r : RIM + 29 + k + r, :] for k in range(KW)]
            pre = taps[0] * views[0]
            for k in range(1, KW):
                pre = pre + taps[k] * views[k]
            pre = cb[:, cols] + pre
            sig = jax.nn.sigmoid(pre)
            d_pre = flow[r : r + 32, :] * (sig * (1.0 + pre * (1.0 - sig)))
            ds[8 + r : 40 + r, :] = d_pre
            for k in range(KW):
                sums[k] = sums[k] + fold8(d_pre * views[k])
            sums[KW] = sums[KW] + fold8(d_pre)
        nxt[:, cols] = ds[8:16, :]
        for k in range(KW + 1):
            kacc_o[8 * k : 8 * k + 8, cols] += sums[k]

        def back(begin, count):
            total = taps[0] * ds[begin + 11 : begin + 11 + count, :]
            for k in range(1, KW):
                total = total + taps[k] * ds[begin + 11 - k : begin + 11 - k + count, :]
            return total

        for r in range(0, Q, 32):
            dcv_o[r : r + 32, cols] = back(r, 32).astype(low)
        head_o[:, cols] = back(-8, 8)

        @pl.when(fresh)
        def keep():
            tail_o[:, cols] = back(Q - 16, 16)

    cumv = cum[...]
    stepv = step[...]
    last = cumv[Q - 1 : Q, :]
    fade = jnp.exp(last - cumv)
    tail = fade * stepv
    tails = split(tail)
    b_rows = bc[:, 0:N]
    d_b = dbc[:, 0:N]
    d_c = dbc[:, N : 2 * N]
    sums = jnp.zeros((Q, HL), f32)
    lasts = jnp.zeros((8, HL), f32)
    for c in range(0, DI, CH):
        cols = slice(c, c + CH)
        end = dloc[:, cols] + suf[0:1, cols] * inc[:, cols].astype(f32)
        end_low = end.astype(low)
        begin = sbf[:, cols]
        lasts = lasts + gather_heads(fold8(end * begin.astype(f32)), et[cols, :])
        reach = nn(b_rows, end_low)
        sums = sums + gather_heads(reach * xh[:, cols].astype(f32), et[cols, :])
        d_b = d_b + nt(wx[:, cols], end_low)
        d_c = d_c + nt(gdy[:, cols], begin)
        conv_back(dx[:, cols] + spread(tails, e[:, cols]) * reach, c)
    conv_back(jnp.concatenate([d_b, d_c], axis=1), DI)

    flow = sums * tail
    d_cum = rs1[...] - stepv * rs2[...] - flow
    d_last = jnp.exp(last) * jnp.sum(lasts, axis=0, keepdims=True)
    d_last = d_last + jnp.sum(flow, axis=0, keepdims=True)
    d_log = running_sum(d_cum, True) + d_last
    d_step = rs2[...] + sums * fade - d_log * rate[...]
    d_dt = d_step * jax.nn.sigmoid(dtb[...])
    dcv_o[:, CD:CW] = d_dt.astype(low)
    hacc_o[0:8, :] += fold8(d_dt)
    hacc_o[8:16, :] += fold8(d_log * stepv)


def store_pieces(me, total, first, count, height, write):
    for i in range(count):
        piece = (first + i) ^ me
        value = total[i * height : (i + 1) * height, :]
        place = place_of(piece)

        @pl.when((piece & 1) == 0)
        def mine():
            write(0, place, value)

        @pl.when((piece & 1) == 1)
        def sent():
            write(1, place, value)


def early_grad_kernel(scal, nrmt, dz, dzr, gn, db, wz, g0_o, g1_o, dn_o, part, wide):
    at = pl.program_id(0)
    me = scal[0]
    refs = (g0_o, g1_o)
    quarter = DI // 4
    cols = pl.ds(pl.multiple_of(at * quarter, HALF), quarter)
    part[...] = nn(nrmt[...], dz[...])

    def put_in(which, place, value):
        refs[which][place, 0, :, cols] = value.astype(low)

    store_pieces(me, part, 0, PIECES, 24, put_in)
    wide[...] = tn(gn[...], db[...])

    def put_out(which, place, value):
        packed = jnp.concatenate([value[0:24, :], value[24:48, :]], axis=1)
        refs[which][place, 1, :, :] = packed.astype(low)

    store_pieces(me, wide, at * 8, 8, 48, put_out)
    dn_o[...] = nt(dzr[...], wz[...])


def late_grad_kernel(scal, nrmt, dcv, g0_o, g1_o, part):
    refs = (g0_o, g1_o)
    part[...] = nn(nrmt[...], dcv[...])

    def put_in(which, place, value):
        refs[which][place, :, :] = value.astype(low)

    store_pieces(scal[0], part, 0, PIECES, 24, put_in)


def input_kernel(dcv, dnz, wc, x, cot, gain, gh_o, acc_o, total):
    @pl.when(pl.program_id(0) == 0)
    def start():
        acc_o[...] = jnp.zeros_like(acc_o)

    total[...] = dnz[...] + nt(dcv[...], wc[...])
    width = x.shape[1]
    for r in range(0, Q, 16):
        rows = slice(r, r + 16)
        wide = x[rows, :].astype(f32)
        scale = lax.rsqrt(jnp.mean(wide * wide, axis=-1, keepdims=True) + epsilon)
        flow = total[rows, :]
        acc_o[...] += fold8(flow * wide * scale)
        scaled = flow * gain[...]
        mean = jnp.sum(scaled * wide, axis=-1, keepdims=True) / width
        d_x = scale * scaled - wide * (scale * scale * scale * mean)
        gh_o[rows, :] = (cot[rows, :].astype(f32) + d_x).astype(low)


def call(kernel, grid, inputs, outputs, scratch, flops, name):
    in_specs = [spec for spec, _ in inputs]
    out_specs = [spec for spec, _, _ in outputs]
    out_shape = [jax.ShapeDtypeStruct(shape, kind) for _, shape, kind in outputs]
    moved = sum(value.size * value.dtype.itemsize for _, value in inputs)
    return pl.pallas_call(
        kernel,
        grid=(grid,),
        in_specs=in_specs,
        out_specs=out_specs,
        out_shape=out_shape,
        scratch_shapes=scratch,
        cost_estimate=pl.CostEstimate(flops=int(flops), transcendentals=0, bytes_accessed=moved),
        compiler_params=pltpu.CompilerParams(
            dimension_semantics=("arbitrary",), vmem_limit_bytes=56 * 1024 * 1024
        ),
        name=name,
    )(*[value for _, value in inputs])


def swap(value, mask):
    return lax.ppermute(value, axes, [(i, i ^ mask) for i in range(PIECES)])


def weave(value):
    line = jnp.stack([value] + [swap(value, mask) for mask in (8, 16, 24)])
    plane = jnp.stack([line] + [swap(line, mask) for mask in (2, 4, 6)])
    other = swap(plane, 1)
    flat = (PIECES // 2,) + value.shape
    return plane.reshape(flat), other.reshape(flat)


def canonical(pieces_own, pieces_other, me):
    both = jnp.concatenate([pieces_own, pieces_other])
    piece = jnp.arange(PIECES, dtype=jnp.int32) ^ me
    return both[(piece & 1) * (PIECES // 2) + place_of(piece)]


def unweave(kept, sent):
    shape = (4, 4) + kept.shape[1:]
    total = (kept.astype(f32) + swap(sent, 1).astype(f32)).reshape(shape)
    lows = total.astype(low)
    got = [swap(lows[j], mask).astype(f32) for j, mask in ((1, 2), (2, 4), (3, 6))]
    total = (total[0] + got[0]) + (got[1] + got[2])
    lows = total.astype(low)
    got = [swap(lows[j], mask).astype(f32) for j, mask in ((1, 8), (2, 16), (3, 24))]
    return (total[0] + got[0]) + (got[1] + got[2])


def total_over(value):
    value = value + swap(value, 1)
    for masks in ((2, 4, 6), (8, 16, 24)):
        got = [swap(value, mask) for mask in masks]
        value = (value + got[0]) + (got[1] + got[2])
    return value


def order_of_pieces():
    return [(j << 1) | (k << 3) for j in range(4) for k in range(4)]


def relay(ends, totals, forward):
    count = lax.axis_size("seq")
    incoming = jnp.zeros(ends.shape, f32)
    for hop in range(1, count):
        value = (totals[:, 0:1, :] * incoming + ends).astype(low)
        route = [(hop - 1, hop)] if forward else [(count - hop, count - hop - 1)]
        incoming = incoming + lax.ppermute(value, "seq", route).astype(f32)
    return incoming.astype(low)


def per_device(
    hidden,
    lengths,
    norm_gain,
    in_weight,
    conv_weight,
    conv_bias,
    step_bias,
    decay_log,
    skip_gain,
    gate_gain,
    out_weight,
    cotangent,
):
    seqs, piece_len, width = hidden.shape
    groups = piece_len // Q
    blocks = seqs * groups
    rows = seqs * piece_len
    devices = lax.axis_size(axes)
    quick = devices == PIECES
    place = lax.axis_index(axes).astype(jnp.int32)
    me = place if quick else jnp.zeros((), jnp.int32)
    seq_at = lax.axis_index("seq").astype(jnp.int32)
    scal = jnp.concatenate([me[None], seq_at[None], lengths.astype(jnp.int32)])

    rims = hidden[:, piece_len - RIM :, :]
    seq_size = lax.axis_size("seq")
    rim_in = lax.ppermute(rims, "seq", [(i, i + 1) for i in range(seq_size - 1)])
    inner = hidden.reshape(seqs, groups, Q, width)[:, : groups - 1, Q - RIM :, :]
    halo = jnp.concatenate([rim_in[:, None], inner], axis=1).reshape(blocks, RIM, width)

    small = jnp.concatenate(
        [norm_gain, conv_weight.reshape(-1), conv_bias, gate_gain]
    ).astype(low)
    w_low = in_weight.astype(low)
    o_low = out_weight.astype(low)
    first = jnp.concatenate(
        [w_low[:, DI:], jnp.zeros((w_low.shape[0], CW - (w_low.shape[1] - DI)), low)], axis=1
    )
    if quick:
        half = o_low.shape[0] // 2
        packed = jnp.concatenate([o_low[:half], o_low[half:]], axis=1)
        second = jnp.stack([w_low[:, :DI], packed])
        size = small.shape[0]
        padded = jnp.pad(small, (0, -size % HALF)).reshape(1, -1)
        smalls = canonical(*weave(padded), me)[:, 0, :size]
        ca, cb_pieces = weave(first)
        second, _ = lax.optimization_barrier((second, ca))
        za, zb = weave(second)
    else:
        smalls = lax.all_gather(small, axes, axis=0, tiled=False)
        order = jnp.array(order_of_pieces(), jnp.int32)
        whole = lax.all_gather(first, axes, axis=0, tiled=True).reshape(PIECES, -1, CW)
        ca, cb_pieces = whole[order], whole[order + 1]
        whole = lax.all_gather(w_low[:, :DI], axes, axis=0, tiled=True).reshape(PIECES, -1, DI)
        outs = lax.all_gather(o_low, axes, axis=0, tiled=True)
        outs = outs.reshape(PIECES, 2, -1, width).transpose(0, 2, 1, 3).reshape(PIECES, -1, DI)
        whole = jnp.stack([whole, outs], axis=1)
        za, zb = whole[order], whole[order + 1]
    smalls = smalls.astype(f32)
    cuts = [norm_gain.shape[0], KW * conv_weight.shape[1], conv_bias.shape[0], gate_gain.shape[0]]
    edges = [0, cuts[0], cuts[0] + cuts[1], cuts[0] + cuts[1] + cuts[2], sum(cuts)]
    gain_in = smalls[:, edges[0] : edges[1]].reshape(1, width)
    taps = smalls[:, edges[1] : edges[2]].reshape(devices, KW, -1)
    taps = taps.transpose(1, 0, 2).reshape(KW, CD)
    bias = smalls[:, edges[2] : edges[3]].reshape(1, CD)
    gain_gate = smalls[:, edges[3] : edges[4]].reshape(1, DI)

    rate = jnp.exp(decay_log)
    sb = jnp.pad(step_bias, (0, HL - H)).reshape(1, HL)
    rate_row = jnp.pad(rate, (0, HL - H)).reshape(1, HL)
    skip = jnp.repeat(skip_gain, P_SIZE).reshape(1, DI)
    heads = lax.broadcasted_iota(jnp.int32, (HL, DI), 0)
    e = (heads == lax.broadcasted_iota(jnp.int32, (HL, DI), 1) // P_SIZE).astype(low)
    heads = lax.broadcasted_iota(jnp.int32, (DI, HL), 1)
    et = (heads == lax.broadcasted_iota(jnp.int32, (DI, HL), 0) // P_SIZE).astype(low)

    def forth(i):
        return i

    def back(i):
        return (i // groups) * groups + groups - 1 - i % groups

    def tokens(cols, order):
        return pl.BlockSpec((Q, cols), lambda i: (order(i), 0))

    def per_block(height, cols, order):
        return pl.BlockSpec((None, height, cols), lambda i: (order(i), 0, 0))

    def per_seq(height, cols):
        return pl.BlockSpec((None, height, cols), lambda i: (i // groups, 0, 0))

    def fixed(*shape):
        zeros = (0,) * len(shape)
        return pl.BlockSpec(shape, lambda i: zeros, pipeline_mode=pl.Buffered(1))

    def kept(*shape):
        zeros = (0,) * len(shape)
        return pl.BlockSpec(shape, lambda i: zeros)

    scalars = pl.BlockSpec(memory_space=pltpu.SMEM)
    flat_hidden = hidden.reshape(rows, width)
    flat_cot = cotangent.reshape(rows, width)

    (nrm, nrmt, cie, xh, xs, wx, bc, step, cum, dtb, cumt, sloc, pre, ends, totals, wc) = call(
        functools.partial(conv_kernel, groups),
        blocks,
        [
            (scalars, scal),
            (tokens(width, forth), flat_hidden),
            (per_block(RIM, width, forth), halo),
            (fixed(*ca.shape), ca),
            (fixed(*ca.shape), cb_pieces),
            (fixed(1, width), gain_in),
            (fixed(KW, CD), taps),
            (fixed(1, CD), bias),
            (fixed(1, HL), sb),
            (fixed(1, HL), rate_row),
            (fixed(HL, DI), e),
        ],
        [
            (tokens(width, forth), (rows, width), low),
            (pl.BlockSpec((width, Q), lambda i: (0, i)), (width, rows), low),
            (per_block(Q + RIM, CD, forth), (blocks, Q + RIM, CD), low),
            (tokens(DI, forth), (rows, DI), low),
            (tokens(DI, forth), (rows, DI), low),
            (tokens(DI, forth), (rows, DI), low),
            (tokens(2 * N, forth), (rows, 2 * N), low),
            (tokens(HL, forth), (rows, HL), f32),
            (tokens(HL, forth), (rows, HL), f32),
            (tokens(HL, forth), (rows, HL), f32),
            (per_block(H, Q, forth), (blocks, H, Q), f32),
            (per_block(N, DI, forth), (blocks, N, DI), f32),
            (per_block(8, DI, forth), (blocks, 8, DI), f32),
            (per_seq(N, DI), (seqs, N, DI), f32),
            (per_seq(8, DI), (seqs, 8, DI), f32),
            (kept(width, CW), (width, CW), low),
        ],
        [
            pltpu.VMEM((Q + RIM, width), low),
            pltpu.VMEM((Q + RIM, CH), f32),
            pltpu.VMEM((N, DI), f32),
            pltpu.VMEM((8, DI), f32),
        ],
        2.0 * rows * width * CW,
        "conv",
    )

    incoming = relay(ends, totals, True)

    (intra,) = call(
        intra_kernel,
        blocks,
        [
            (tokens(2 * N, forth), bc),
            (tokens(DI, forth), xs),
            (tokens(HL, forth), cum),
            (per_block(H, Q, forth), cumt),
        ],
        [(tokens(DI, forth), (rows, DI), f32)],
        [pltpu.VMEM((Q, Q), f32)],
        2.0 * rows * Q * DI * 2,
        "intra",
    )

    (z, dn, db, wz, wo) = call(
        functools.partial(project_kernel, groups),
        blocks,
        [
            (scalars, scal),
            (tokens(width, forth), nrm),
            (tokens(width, forth), flat_cot),
            (fixed(*za.shape), za),
            (fixed(*za.shape), zb),
        ],
        [
            (tokens(DI, forth), (rows, DI), f32),
            (tokens(DI, forth), (rows, DI), f32),
            (tokens(width, forth), (rows, width), low),
            (kept(width, DI), (width, DI), low),
            (kept(DI, width), (DI, width), low),
        ],
        [],
        4.0 * rows * width * DI,
        "project",
    )

    (out, dz, dy, gdy, gn, sbf, rs1, dloc, suf, back_ends, back_totals, gacc, kacc) = call(
        functools.partial(gate_kernel, groups),
        blocks,
        [
            (scalars, scal),
            (tokens(DI, back), intra),
            (tokens(DI, back), xh),
            (tokens(2 * N, back), bc),
            (tokens(HL, back), cum),
            (per_block(N, DI, back), sloc),
            (per_block(8, DI, back), pre),
            (per_seq(N, DI), incoming),
            (tokens(DI, back), z),
            (tokens(DI, back), dn),
            (tokens(width, back), flat_hidden),
            (fixed(DI, width), wo),
            (fixed(1, DI), gain_gate),
            (fixed(1, DI), skip),
            (fixed(HL, DI), e),
            (fixed(DI, HL), et),
        ],
        [
            (tokens(width, back), (rows, width), low),
            (tokens(DI, back), (rows, DI), low),
            (tokens(DI, back), (rows, DI), low),
            (tokens(DI, back), (rows, DI), low),
            (tokens(DI, back), (rows, DI), low),
            (per_block(N, DI, back), (blocks, N, DI), low),
            (tokens(HL, back), (rows, HL), f32),
            (per_block(N, DI, back), (blocks, N, DI), f32),
            (per_block(8, DI, back), (blocks, 8, DI), f32),
            (per_seq(N, DI), (seqs, N, DI), f32),
            (per_seq(8, DI), (seqs, 8, DI), f32),
            (kept(16, DI), (16, DI), f32),
            (kept(16, DI), (16, DI), f32),
        ],
        [
            pltpu.VMEM((Q, DI), f32),
            pltpu.VMEM((Q, DI), f32),
            pltpu.VMEM((Q, DI), f32),
            pltpu.VMEM((16, DI), f32),
            pltpu.VMEM((16, DI), f32),
            pltpu.VMEM((16, DI), f32),
            pltpu.VMEM((N, DI), f32),
            pltpu.VMEM((8, DI), f32),
        ],
        4.0 * rows * width * DI,
        "gate",
    )

    back_incoming = relay(back_ends, back_totals, False)

    (dx, dbc, rs2) = call(
        intra_back_kernel,
        blocks,
        [
            (tokens(2 * N, forth), bc),
            (tokens(DI, forth), xs),
            (tokens(DI, forth), xh),
            (tokens(DI, forth), dy),
            (tokens(HL, forth), step),
            (tokens(HL, forth), cum),
            (per_block(H, Q, forth), cumt),
            (fixed(1, DI), skip),
            (fixed(HL, DI), e),
            (fixed(DI, HL), et),
        ],
        [
            (tokens(DI, forth), (rows, DI), f32),
            (tokens(2 * N, forth), (rows, 2 * N), f32),
            (tokens(HL, forth), (rows, HL), f32),
        ],
        [pltpu.VMEM((Q, Q), f32), pltpu.VMEM((Q, Q), f32)],
        4.0 * rows * Q * DI * 2,
        "intra_back",
    )

    share = rows // 4
    piece = (PIECES // 2, 2, width // PIECES, DI)
    (e0, e1, dnz) = call(
        early_grad_kernel,
        4,
        [
            (scalars, scal),
            (fixed(width, rows), nrmt),
            (pl.BlockSpec((rows, DI // 4), lambda i: (0, i)), dz),
            (pl.BlockSpec((share, DI), lambda i: (i, 0)), dz),
            (pl.BlockSpec((rows, DI // 4), lambda i: (0, i)), gn),
            (fixed(rows, width), db),
            (fixed(width, DI), wz),
        ],
        [
            (kept(*piece), piece, low),
            (kept(*piece), piece, low),
            (pl.BlockSpec((share, width), lambda i: (i, 0)), (rows, width), f32),
        ],
        [pltpu.VMEM((width, DI // 4), f32), pltpu.VMEM((DI // 4, width), f32)],
        6.0 * rows * width * DI,
        "early_grad",
    )

    (dcv, cacc, hacc, heads_out, tails_out) = call(
        functools.partial(conv_back_kernel, groups),
        blocks,
        [
            (per_block(N, DI, back), dloc),
            (per_block(8, DI, back), suf),
            (per_seq(N, DI), back_incoming),
            (per_block(N, DI, back), sbf),
            (tokens(DI, back), xh),
            (tokens(DI, back), wx),
            (tokens(DI, back), gdy),
            (tokens(DI, back), dx),
            (tokens(2 * N, back), dbc),
            (tokens(2 * N, back), bc),
            (tokens(HL, back), cum),
            (tokens(HL, back), step),
            (tokens(HL, back), dtb),
            (tokens(HL, back), rs1),
            (tokens(HL, back), rs2),
            (per_block(Q + RIM, CD, back), cie),
            (fixed(KW, CD), taps),
            (fixed(1, CD), bias),
            (fixed(1, HL), rate_row),
            (fixed(HL, DI), e),
            (fixed(DI, HL), et),
        ],
        [
            (tokens(CW, back), (rows, CW), low),
            (kept(8 * (KW + 1), CD), (8 * (KW + 1), CD), f32),
            (kept(16, HL), (16, HL), f32),
            (per_seq(8, CD), (seqs, 8, CD), f32),
            (per_seq(16, CD), (seqs, 16, CD), f32),
        ],
        [
            pltpu.VMEM((Q + RIM, CH), f32),
            pltpu.VMEM((Q + 16, CH), f32),
            pltpu.VMEM((8, CD), f32),
        ],
        6.0 * rows * N * DI,
        "conv_back",
    )

    returned = lax.ppermute(
        heads_out.astype(low), "seq", [(i, i - 1) for i in range(1, seq_size)]
    ).astype(f32)
    fixed_tail = jnp.concatenate(
        [tails_out[:, :8], tails_out[:, 8:] + returned], axis=1
    ).astype(low)
    dcv = dcv.reshape(seqs, piece_len, CW)
    dcv = dcv.at[:, piece_len - 16 :, :CD].set(fixed_tail).reshape(rows, CW)

    late = (PIECES // 2, width // PIECES, CW)
    late_spec = pl.BlockSpec((PIECES // 2, width // PIECES, CW // 5), lambda i: (0, 0, i))
    (l0, l1) = call(
        late_grad_kernel,
        5,
        [
            (scalars, scal),
            (fixed(width, rows), nrmt),
            (pl.BlockSpec((rows, CW // 5), lambda i: (0, i)), dcv),
        ],
        [(late_spec, late, low), (late_spec, late, low)],
        [pltpu.VMEM((width, CW // 5), f32)],
        2.0 * rows * width * CW,
        "late_grad",
    )

    (gh, nacc) = call(
        input_kernel,
        blocks,
        [
            (tokens(CW, forth), dcv),
            (tokens(width, forth), dnz),
            (fixed(width, CW), wc),
            (tokens(width, forth), flat_hidden),
            (tokens(width, forth), flat_cot),
            (fixed(1, width), gain_in),
        ],
        [
            (tokens(width, forth), (rows, width), low),
            (kept(8, width), (8, width), f32),
        ],
        [pltpu.VMEM((Q, width), f32)],
        2.0 * rows * width * CW,
        "input",
    )

    conv_sums = cacc.reshape(KW + 1, 8, CD).sum(axis=1)
    skips = kacc.sum(axis=0).reshape(H, P_SIZE).sum(axis=1)
    scalar_sums = jnp.concatenate(
        [hacc[0:8].sum(axis=0)[:H], -hacc[8:16].sum(axis=0)[:H] * rate, skips]
    )
    vector = jnp.concatenate(
        [nacc.sum(axis=0), conv_sums.reshape(-1), gacc.sum(axis=0), scalar_sums]
    )
    if quick:
        length = vector.shape[0]
        vector = total_over(jnp.pad(vector, (0, -length % (8 * HALF))).reshape(-1, HALF))
        vector = vector.reshape(-1)[:length]
        early = unweave(e0, e1)
        own_late = unweave(l0, l1)
        own_z, own_out = early[0], early[1]
        own_out = jnp.concatenate([own_out[:, : DI // 2], own_out[:, DI // 2 :]], axis=0)
    else:
        vector = lax.psum(vector, axes)
        order = jnp.array(order_of_pieces(), jnp.int32)
        inverse = jnp.argsort(jnp.concatenate([order, order + 1]))
        whole = jnp.concatenate([e0, e1])[inverse].astype(f32)
        outs = whole[:, 1].reshape(PIECES, -1, 2, width).transpose(0, 2, 1, 3).reshape(DI, width)
        own_z = lax.psum_scatter(
            whole[:, 0].reshape(width, DI), axes, scatter_dimension=0, tiled=True
        )
        own_out = lax.psum_scatter(outs, axes, scatter_dimension=0, tiled=True)
        whole = jnp.concatenate([l0, l1])[inverse].astype(f32).reshape(width, CW)
        own_late = lax.psum_scatter(whole, axes, scatter_dimension=0, tiled=True)

    def own(value, size, axis):
        return lax.dynamic_slice_in_dim(value, place * size, size, axis)

    at = width
    g_norm = own(vector[:at], cuts[0], 0)
    g_taps = own(vector[at : at + KW * CD].reshape(KW, CD), CD // devices, 1)
    at += KW * CD
    g_bias = own(vector[at : at + CD], CD // devices, 0)
    at += CD
    g_gate = own(vector[at : at + DI], cuts[3], 0)
    at += DI
    g_in = jnp.concatenate([own_z, own_late[:, : CD + H]], axis=1)
    return (
        out.reshape(hidden.shape),
        gh.reshape(hidden.shape),
        g_norm,
        g_in,
        g_taps,
        g_bias,
        vector[at : at + H],
        vector[at + H : at + 2 * H],
        vector[at + 2 * H : at + 3 * H],
        g_gate,
        own_out,
    )


def solution(mesh):
    return jax.shard_map(
        per_device,
        mesh=mesh,
        in_specs=(
            P("dp", "seq", None),
            P("dp"),
            P(("dp", "seq")),
            P(("dp", "seq"), None),
            P(None, ("dp", "seq")),
            P(("dp", "seq")),
            P(),
            P(),
            P(),
            P(("dp", "seq")),
            P(("dp", "seq"), None),
            P("dp", "seq", None),
        ),
        out_specs=(
            P("dp", "seq", None),
            P("dp", "seq", None),
            P(("dp", "seq")),
            P(("dp", "seq"), None),
            P(None, ("dp", "seq")),
            P(("dp", "seq")),
            P(),
            P(),
            P(),
            P(("dp", "seq")),
            P(("dp", "seq"), None),
        ),
        check_vma=False,
    )
```

```python
import functools

import jax
import jax.numpy as jnp
import numpy as np
from jax import lax
from jax.experimental import pallas as pl
from jax.experimental.pallas import tpu as pltpu
from jax.sharding import PartitionSpec as P

H = 24
P_SIZE = 64
N = 128
KW = 4
Q = 256
E = 3352
DI = 1536
CD = 1792
HL = 128
CW = CD + HL
CH = 256
HALF = 128
RIM = 16
PIECES = 32
NEG = -1e30

epsilon = 1e-05
low = jnp.bfloat16
f32 = jnp.float32
axes = ("dp", "seq")


def onehot(rows, cols, first, period):
    table = np.zeros((rows, cols), np.float32)
    at = np.arange(cols)
    table[first + at % period, at] = 1.0
    return jnp.asarray(table, low)


def head_table():
    table = np.zeros((HL, DI), np.float32)
    at = np.arange(DI)
    table[at // P_SIZE, at] = 1.0
    table[HL // 2 + at // P_SIZE, at] = 1.0
    return table


def dot(left, right, dims):
    return lax.dot_general(left, right, (dims, ((), ())), preferred_element_type=f32)


def nn(left, right):
    return dot(left, right, ((1,), (0,)))


def nt(left, right):
    return dot(left, right, ((1,), (1,)))


def tn(left, right):
    return dot(left, right, ((0,), (0,)))


def pack(value):
    top = value.astype(low).astype(f32)
    rest = pltpu.roll(value - top, HL // 2, 1)
    lane = lax.broadcasted_iota(jnp.int32, value.shape, 1)
    return jnp.where(lane < HL // 2, top, rest).astype(low)


def spread(packed, table):
    return nn(packed, table)


def gather_heads(value, table):
    top = value.astype(low)
    return nn(top, table) + nn((value - top.astype(f32)).astype(low), table)


def running_sum(value, reverse):
    rows = value.shape[0]
    at = lax.broadcasted_iota(jnp.int32, value.shape, 0)
    step = 1
    while step < rows:
        if reverse:
            value = value + jnp.where(at < rows - step, pltpu.roll(value, rows - step, 0), 0.0)
        else:
            value = value + jnp.where(at >= step, pltpu.roll(value, step, 0), 0.0)
        step *= 2
    return value


def softplus(value):
    tail = jnp.exp(-jnp.abs(value))
    series = tail * (1.0 - tail * (0.5 - tail * (1.0 / 3.0 - tail * (0.25 - tail * 0.2))))
    return jnp.maximum(value, 0.0) + jnp.where(tail < 0.03125, series, jnp.log(1.0 + tail))


def fold8(value):
    return jnp.sum(value.reshape(value.shape[0] // 8, 8, value.shape[1]), axis=0)


def pair_rows(me, own, other):
    first = (me & 1) == 0
    return jnp.concatenate([jnp.where(first, own, other), jnp.where(first, other, own)], axis=0)


def source_of(me, place):
    return me ^ ((place // 4) * 2) ^ ((place % 4) * 8)


def place_of(piece):
    return ((piece >> 1) & 3) * 4 + (piece >> 3)


def conv_kernel(
    groups, scal, x, halo, wa, wb, t56, t48, t24, sb, rate, e,
    nrm_o, nrmt_o, cie_o, sp_o, xh_o, xs_o, wx_o, bc_o, step_o, cum_o, dtb_o, cumt_o,
    sloc_o, pre_o, r_o, tot_o, wc_o, taps_o, gain_o, gate_o,
    nrm, cs, run, dec, small,
):
    block = pl.program_id(0)
    fresh = block % groups == 0

    @pl.when(block == 0)
    def assemble():
        me = scal[0]

        def one(place, carry):
            chip = source_of(me, place) >> 1
            own, other = wa[place].astype(f32), wb[place].astype(f32)
            wc_o[pl.ds(pl.multiple_of(chip * 48, 16), 48), :] = pair_rows(me, own, other).astype(low)
            rows = pl.ds(pl.multiple_of(place * 8, 8), 8)
            small[0, rows, :] = own[0:8, CD:CW]
            small[1, rows, :] = other[0:8, CD:CW]
            return carry

        lax.fori_loop(0, PIECES // 2, one, 0)
        at = lax.broadcasted_iota(jnp.int32, (PIECES, 1), 0)
        slot = at & (PIECES // 2 - 1)
        ids = me ^ ((slot >> 2) << 1) ^ ((slot & 3) << 3) ^ (at >> 4)

        def row_of(k, table, size):
            pieces = [small[which, pl.ds(k, PIECES // 2, stride=8), :] for which in range(2)]
            wide = nn(jnp.concatenate(pieces, axis=0).astype(low), table)
            lane = lax.broadcasted_iota(jnp.int32, wide.shape, 1)
            inside = jnp.logical_and(lane >= ids * size, lane < (ids + 1) * size)
            return jnp.sum(jnp.where(inside, wide, 0.0), axis=0, keepdims=True)

        for k in range(KW + 1):
            taps_o[k : k + 1, :] = row_of(k, t56[...], CD // PIECES)
        gate_o[0:1, :] = row_of(0, t48[...], DI // PIECES)
        gain_o[0:1, :] = row_of(1, t24[...], gain_o.shape[1] // PIECES)

    def normed(rows):
        wide = rows.astype(f32)
        scale = lax.rsqrt(jnp.mean(wide * wide, axis=-1, keepdims=True) + epsilon)
        return (wide * scale * gain_o[0:1, :]).astype(low)

    nrm[0:RIM, :] = normed(halo[...])
    for r in range(0, Q, 32):
        nrm[RIM + r : RIM + r + 32, :] = normed(x[r : r + 32, :])
    nrm_o[...] = nrm[RIM:, :]
    nrmt_o[...] = nrm[RIM:, :].T

    for c in range(0, CD, CH):
        cols = slice(c, c + CH)
        conv_in = nn(nrm[...], wc_o[:, cols]).astype(low)
        cie_o[:, cols] = conv_in
        cs[...] = conv_in.astype(f32)
        for r in range(0, Q, 32):
            taps = taps_o[0:1, cols] * cs[RIM - 3 + r : RIM + 29 + r, :]
            for k in range(1, KW):
                taps = taps + taps_o[k : k + 1, cols] * cs[RIM - 3 + k + r : RIM + 29 + k + r, :]
            pre = taps_o[KW : KW + 1, cols] + taps
            sig = jax.nn.sigmoid(pre)
            act = (pre * sig).astype(low)
            sp_o[r : r + 32, cols] = sig * (1.0 + pre * (1.0 - sig))
            if c < DI:
                xh_o[r : r + 32, cols] = act
            else:
                bc_o[r : r + 32, :] = act

    dtb = nn(nrm[RIM:, :], wc_o[:, CD:CW]) + sb[...]
    step = softplus(dtb)
    cum = running_sum(-step * rate[...], False)
    step_o[...] = step
    cum_o[...] = cum
    dtb_o[...] = dtb
    cumt_o[...] = cum.T[0:H, :]
    last = cum[Q - 1 : Q, :]
    steps = pack(step)
    tails = pack(jnp.exp2(last - cum) * step)
    decays = pack(jnp.broadcast_to(jnp.exp2(last), (8, HL)))
    for c in range(0, DI, CH):
        cols = slice(c, c + CH)
        table = e[:, cols]
        wide = xh_o[:, cols].astype(f32)
        xs_o[:, cols] = (spread(steps, table) * wide).astype(low)
        weighted = (spread(tails, table) * wide).astype(low)
        wx_o[:, cols] = weighted
        local = tn(bc_o[:, 0:N], weighted)
        decay = spread(decays, table)
        before = jnp.where(fresh, 0.0, run[:, cols])
        sloc_o[:, cols] = before
        after = decay[0:1, :] * before + local
        run[:, cols] = after
        r_o[:, cols] = after
        product = jnp.where(fresh, 1.0, dec[:, cols])
        pre_o[:, cols] = product
        product = product * decay
        dec[:, cols] = product
        tot_o[:, cols] = product[0:1, :]


def intra_kernel(bc, xs, cum, cumt, o, sc):
    sc[...] = nt(bc[:, N : 2 * N], bc[:, 0:N])
    at = lax.broadcasted_iota(jnp.int32, (HALF, HALF), 0)
    to = lax.broadcasted_iota(jnp.int32, (HALF, HALF), 1)
    lower = at >= to
    left = lax.broadcasted_iota(jnp.int32, (Q, HALF), 1) < P_SIZE
    for pair in range(H // 2):
        cols = slice(pair * HALF, (pair + 1) * HALF)
        x_pair = xs[:, cols]
        tops, bottoms = [], []
        for h in (2 * pair, 2 * pair + 1):
            row = cumt[h : h + 1, :]
            upper_col, lower_col = cum[0:HALF, h : h + 1], cum[HALF:, h : h + 1]
            m00 = sc[0:HALF, 0:HALF] * jnp.exp2(jnp.where(lower, upper_col - row[:, 0:HALF], NEG))
            m10 = sc[HALF:, 0:HALF] * jnp.exp2(lower_col - row[:, 0:HALF])
            m11 = sc[HALF:, HALF:] * jnp.exp2(jnp.where(lower, lower_col - row[:, HALF:], NEG))
            tops.append(nn(m00.astype(low), x_pair[0:HALF, :]))
            bottoms.append(nn(jnp.concatenate([m10.astype(low), m11.astype(low)], axis=1), x_pair))
        o[0:HALF, cols] = jnp.where(left[0:HALF], tops[0], tops[1])
        o[HALF:, cols] = jnp.where(left[0:HALF], bottoms[0], bottoms[1])


def valid_column(scal, groups, block):
    seq, group = block // groups, block % groups
    at = scal[1] * (groups * Q) + group * Q + lax.broadcasted_iota(jnp.int32, (Q, 1), 0)
    return (at < scal[2 + seq]).astype(f32)


def project_kernel(groups, scal, nrm, cot, wa, wb, z_o, dn_o, db_o, wz_o, wo_o):
    block = pl.program_id(0)

    @pl.when(block == 0)
    def assemble():
        me = scal[0]

        def halves(packed):
            return jnp.concatenate([packed[:, 0 : DI // 2], packed[:, DI // 2 :]], axis=0)

        def one(place, carry):
            chip = source_of(me, place) >> 1
            own, other = wa[place, 0].astype(f32), wb[place, 0].astype(f32)
            wz_o[pl.ds(pl.multiple_of(chip * 48, 16), 48), :] = pair_rows(me, own, other).astype(low)
            own, other = halves(wa[place, 1].astype(f32)), halves(wb[place, 1].astype(f32))
            wo_o[pl.ds(pl.multiple_of(chip * 96, 16), 96), :] = pair_rows(me, own, other).astype(low)
            return carry

        lax.fori_loop(0, PIECES // 2, one, 0)

    db_o[...] = (cot[...].astype(f32) * valid_column(scal, groups, block)).astype(low)
    for c in range(0, DI, CH):
        z_o[:, c : c + CH] = nn(nrm[...], wz_o[:, c : c + CH])
        dn_o[:, c : c + CH] = nt(db_o[...], wo_o[c : c + CH, :])


def gate_kernel(
    groups, scal, intra, xh, bc, cum, sloc, pre, inc, z, dn, hid, wo, gg, skip, e, et,
    out_o, dz_o, dy_o, gdy_o, gn_o, sbf_o, rs_o, dloc_o, suf_o, rd_o, tot_o, gacc_o, kacc_o,
    yi_s, ge_s, pr_s, y_s, sg_s, gt_s, run, dec,
):
    at = pl.program_id(0)
    fresh = at % groups == 0
    block = (at // groups) * groups + groups - 1 - at % groups

    @pl.when(at == 0)
    def start():
        gacc_o[...] = jnp.zeros_like(gacc_o)
        kacc_o[...] = jnp.zeros_like(kacc_o)

    c_rows = bc[:, N : 2 * N]
    growth = pack(jnp.exp2(cum[...]))
    for c in range(0, DI, CH):
        cols = slice(c, c + CH)
        begin = (sloc[:, cols] + pre[0:1, cols] * inc[:, cols].astype(f32)).astype(low)
        sbf_o[:, cols] = begin
        wide = spread(growth, e[:, cols])
        ge_s[:, cols] = wide
        yi_s[:, cols] = intra[:, cols] + wide * nn(c_rows, begin)

    def body(i, carry):
        rows = pl.ds(pl.multiple_of(i * 32, 32), 32)
        squares = jnp.zeros((32, HALF), f32)
        crosses = jnp.zeros((32, HALF), f32)
        for c in range(0, DI, HALF):
            cols = slice(c, c + HALF)
            zv = z[rows, cols]
            y = yi_s[rows, cols] + skip[:, cols] * xh[rows, cols].astype(f32)
            sig = jax.nn.sigmoid(zv)
            gated = y * (zv * sig)
            squares = squares + gated * gated
            crosses = crosses + (dn[rows, cols] * gg[0:1, cols]) * gated
            y_s[:, cols] = y
            sg_s[:, cols] = sig
            gt_s[:, cols] = gated
        scale = lax.rsqrt(jnp.sum(squares, axis=1, keepdims=True) / DI + epsilon)
        shift = scale * scale * scale * (jnp.sum(crosses, axis=1, keepdims=True) / DI)
        for c in range(0, DI, HALF):
            cols = slice(c, c + HALF)
            zv, y, sig, gated = z[rows, cols], y_s[:, cols], sg_s[:, cols], gt_s[:, cols]
            wide = dn[rows, cols]
            normal = gated * scale
            gn_o[rows, cols] = (normal * gg[0:1, cols]).astype(low)
            gacc_o[:, cols] += fold8(wide * normal)
            d_gated = scale * (wide * gg[0:1, cols]) - gated * shift
            d_sig = d_gated * sig
            dz_o[rows, cols] = (d_sig * y * (1.0 + zv * (1.0 - sig))).astype(low)
            d_low = (d_sig * zv).astype(low)
            dy_o[rows, cols] = d_low
            d_y = d_low.astype(f32)
            kacc_o[:, cols] += fold8(d_y * xh[rows, cols].astype(f32))
            gdy_o[rows, cols] = (ge_s[rows, cols] * d_y).astype(low)
            pr_s[rows, cols] = d_y * yi_s[rows, cols]
        return carry

    lax.fori_loop(0, Q // 32, body, 0)

    valid = valid_column(scal, groups, block)
    for c in range(0, DI // 2, CH):
        branch = nn(gn_o[...], wo[:, c : c + CH])
        out_o[:, c : c + CH] = (hid[:, c : c + CH].astype(f32) + valid * branch).astype(low)
    decays = pack(jnp.broadcast_to(jnp.exp2(cum[Q - 1 : Q, :]), (8, HL)))
    sums = jnp.zeros((Q, HL), f32)
    for c in range(0, DI, CH):
        cols = slice(c, c + CH)
        sums = sums + gather_heads(pr_s[:, cols], et[cols, :])
        decay = spread(decays, e[:, cols])
        before = jnp.where(fresh, 0.0, run[:, cols])
        dloc_o[:, cols] = before
        after = decay[0:1, :] * before + tn(c_rows, gdy_o[:, cols])
        run[:, cols] = after
        rd_o[:, cols] = after
        product = jnp.where(fresh, 1.0, dec[:, cols])
        suf_o[:, cols] = product
        product = product * decay
        dec[:, cols] = product
        tot_o[:, cols] = product[0:1, :]
    rs_o[...] = sums


def intra_back_kernel(bc, xs, xh, dy, step, cum, cumt, skip, e, et, dx_o, dbc_o, rs_o, sc, acc):
    sc[...] = nt(bc[:, 0:N], bc[:, N : 2 * N])
    acc[...] = jnp.zeros_like(acc)
    at = lax.broadcasted_iota(jnp.int32, (HALF, HALF), 0)
    to = lax.broadcasted_iota(jnp.int32, (HALF, HALF), 1)
    upper = at <= to
    left = lax.broadcasted_iota(jnp.int32, (Q, HALF), 1) < P_SIZE
    steps = pack(step[...])
    sums = jnp.zeros((Q, HL), f32)
    for pair in range(H // 2):
        cols = slice(pair * HALF, (pair + 1) * HALF)
        dy_pair = dy[:, cols]
        x_pair = xs[:, cols]
        tops, bottoms, parts = [], [], []
        for h in (2 * pair, 2 * pair + 1):
            keep = left if h % 2 == 0 else jnp.logical_not(left)
            x_half = jnp.where(keep, x_pair, jnp.zeros_like(x_pair))
            row = cumt[h : h + 1, :]
            first_col, second_col = cum[0:HALF, h : h + 1], cum[HALF:, h : h + 1]
            l00 = jnp.exp2(jnp.where(upper, row[:, 0:HALF] - first_col, NEG))
            l01 = jnp.exp2(row[:, HALF:] - first_col)
            l11 = jnp.exp2(jnp.where(upper, row[:, HALF:] - second_col, NEG))
            m00 = (sc[0:HALF, 0:HALF] * l00).astype(low)
            m01 = (sc[0:HALF, HALF:] * l01).astype(low)
            m11 = (sc[HALF:, HALF:] * l11).astype(low)
            tops.append(nn(jnp.concatenate([m00, m01], axis=1), dy_pair))
            bottoms.append(nn(m11, dy_pair[HALF:, :]))
            grown = nt(x_half[0:HALF, :], dy_pair)
            last = nt(x_half[HALF:, :], dy_pair[HALF:, :])
            parts.append((grown[:, 0:HALF] * l00, grown[:, HALF:] * l01, last * l11))
        acc[0:HALF, 0:HALF] += parts[0][0] + parts[1][0]
        acc[0:HALF, HALF:] += parts[0][1] + parts[1][1]
        acc[HALF:, HALF:] += parts[0][2] + parts[1][2]
        flow = jnp.concatenate(
            [
                jnp.where(left[0:HALF], tops[0], tops[1]),
                jnp.where(left[0:HALF], bottoms[0], bottoms[1]),
            ],
            axis=0,
        )
        sums = sums + gather_heads(flow * xh[:, cols].astype(f32), et[cols, :])
        dx_o[:, cols] = spread(steps, e[:, cols]) * flow + skip[:, cols] * dy_pair.astype(f32)
    rs_o[...] = sums
    scores = acc[...].astype(low)
    dbc_o[:, 0:N] = nn(scores, bc[:, N : 2 * N])
    dbc_o[:, N : 2 * N] = tn(scores, bc[:, 0:N])


def conv_back_kernel(
    groups, dloc, suf, inc, sbf, xh, wx, gdy, dx, dbc, bc, cum, step, dtb, rs1, rs2,
    cie, sp, cw, rate, e, et,
    dcv_o, kacc_o, hacc_o, head_o, tail_o,
    ds, nxt,
):
    at = pl.program_id(0)
    fresh = at % groups == 0
    opening = at % groups == groups - 1

    @pl.when(at == 0)
    def start():
        kacc_o[...] = jnp.zeros_like(kacc_o)
        hacc_o[...] = jnp.zeros_like(hacc_o)

    def conv_back(flow, c):
        cols = slice(c, c + CH)
        ds[0:8, :] = jnp.zeros((8, CH), f32)
        ds[8 + Q :, :] = jnp.where(fresh, 0.0, nxt[:, cols])
        ds[8 : 8 + Q, :] = flow * sp[:, cols]
        nxt[:, cols] = ds[8:16, :]
        taps = [cw[k : k + 1, cols] for k in range(KW)]
        sums = [jnp.zeros((8, CH), f32) for _ in range(KW + 1)]

        def views_at(begin, count):
            return [ds[begin + 11 - k : begin + 11 - k + count, :] for k in range(KW)]

        def back(views):
            total = taps[0] * views[0]
            for k in range(1, KW):
                total = total + taps[k] * views[k]
            return total

        for r in range(0, Q, 32):
            views = views_at(r, 32)
            dcv_o[r : r + 32, cols] = back(views).astype(low)
            conv_in = cie[RIM + r : RIM + r + 32, cols].astype(f32)
            for k in range(KW):
                sums[k] = sums[k] + fold8(views[k] * conv_in)
            sums[KW] = sums[KW] + fold8(views[KW - 1])
        views = views_at(-8, 8)
        head_o[:, cols] = back(views).astype(low)
        conv_in = cie[0:RIM, cols].astype(f32)[8:16, :]
        for k in range(KW):
            kacc_o[8 * k : 8 * k + 8, cols] += sums[k] + jnp.where(opening, views[k] * conv_in, 0.0)
        kacc_o[8 * KW : 8 * KW + 8, cols] += sums[KW]

        @pl.when(fresh)
        def keep():
            tail_o[:, cols] = back(views_at(Q - 16, 16))

    cumv = cum[...]
    stepv = step[...]
    last = cumv[Q - 1 : Q, :]
    fade = jnp.exp2(last - cumv)
    tail = fade * stepv
    tails = pack(tail)
    b_rows = bc[:, 0:N]
    d_b = dbc[:, 0:N]
    d_c = dbc[:, N : 2 * N]
    sums = jnp.zeros((Q, HL), f32)
    lasts = jnp.zeros((8, HL), f32)
    for c in range(0, DI, CH):
        cols = slice(c, c + CH)
        end = dloc[:, cols] + suf[0:1, cols] * inc[:, cols].astype(f32)
        end_low = end.astype(low)
        begin = sbf[:, cols]
        lasts = lasts + gather_heads(fold8(end * begin.astype(f32)), et[cols, :])
        reach = nn(b_rows, end_low)
        sums = sums + gather_heads(reach * xh[:, cols].astype(f32), et[cols, :])
        d_b = d_b + nt(wx[:, cols], end_low)
        d_c = d_c + nt(gdy[:, cols], begin)
        conv_back(dx[:, cols] + spread(tails, e[:, cols]) * reach, c)
    conv_back(jnp.concatenate([d_b, d_c], axis=1), DI)

    flow = sums * tail
    d_cum = rs1[...] - stepv * rs2[...] - flow
    d_last = jnp.exp2(last) * jnp.sum(lasts, axis=0, keepdims=True)
    d_last = d_last + jnp.sum(flow, axis=0, keepdims=True)
    d_log = running_sum(d_cum, True) + d_last
    d_step = rs2[...] + sums * fade - d_log * rate[...]
    d_dt = d_step * jax.nn.sigmoid(dtb[...])
    lane = lax.broadcasted_iota(jnp.int32, d_dt.shape, 1)
    d_dt = jnp.where(lane < H, d_dt, 0.0)
    dcv_o[:, CD:CW] = d_dt.astype(low)
    head_o[:, CD:CW] = jnp.zeros((8, HL), low)

    @pl.when(fresh)
    def keep_step():
        tail_o[:, CD:CW] = d_dt[Q - 16 :, :]

    hacc_o[0:8, :] += fold8(d_dt)
    hacc_o[8:16, :] += fold8(d_log * stepv)


def piece_at(me, place, which):
    return source_of(me, place) ^ which


def early_grad_kernel(scal, nrmt, dz, dzr, gn, db, wz, g0_o, g1_o, dn_o, part, wide):
    at = pl.program_id(0)
    me = scal[0]
    refs = (g0_o, g1_o)
    quarter = DI // 4
    cols = pl.ds(pl.multiple_of(at * quarter, HALF), quarter)
    part[...] = nn(nrmt[...], dz[...])
    for place in range(PIECES // 2):
        for which in range(2):
            start = pl.multiple_of(piece_at(me, place, which) * 24, 8)
            refs[which][place, 0, :, cols] = part[pl.ds(start, 24), :].astype(low)
    wide[pl.ds(pl.multiple_of(at * quarter, HALF), quarter), :] = tn(gn[...], db[...])
    dn_o[...] = nt(dzr[...], wz[...])

    @pl.when(at == 3)
    def finish():
        for place in range(PIECES // 2):
            for which in range(2):
                start = pl.multiple_of(piece_at(me, place, which) * 48, 8)
                for half in range(2):
                    rows = pl.ds(start + 24 * half, 24)
                    span = slice(half * DI // 2, (half + 1) * DI // 2)
                    refs[which][place, 1, :, span] = wide[rows, :].astype(low)


def late_grad_kernel(scal, nrmt, dcv, tails, returned, g0_o, g1_o, fix_o, part):
    refs = (g0_o, g1_o)
    fix_o[...] = dcv[...]
    seqs = tails.shape[0]
    piece_len = dcv.shape[0] // seqs
    for seq in range(seqs):
        back = jnp.concatenate(
            [tails[seq, 0:8, :], tails[seq, 8:16, :] + returned[seq].astype(f32)], axis=0
        )
        fix_o[(seq + 1) * piece_len - 16 : (seq + 1) * piece_len, :] = back.astype(low)
    part[...] = nn(nrmt[...], fix_o[...])
    for place in range(PIECES // 2):
        for which in range(2):
            start = pl.multiple_of(piece_at(scal[0], place, which) * 24, 8)
            refs[which][place, :, :] = part[pl.ds(start, 24), :].astype(low)


def input_kernel(dcv, dnz, wc, x, cot, gain, past, gh_o, acc_o, total):
    @pl.when(pl.program_id(0) == 0)
    def start():
        acc_o[...] = jnp.zeros_like(acc_o)

    total[...] = dnz[...] + nt(dcv[...], wc[...])
    width = x.shape[1]
    for r in range(0, Q, 16):
        rows = slice(r, r + 16)
        wide = x[rows, :].astype(f32)
        scale = lax.rsqrt(jnp.mean(wide * wide, axis=-1, keepdims=True) + epsilon)
        flow = total[rows, :]
        acc_o[...] += fold8(flow * wide * scale)
        scaled = flow * gain[0:1, :]
        mean = jnp.sum(scaled * wide, axis=-1, keepdims=True) / width
        d_x = scale * scaled - wide * (scale * scale * scale * mean)
        gh_o[rows, :] = (cot[rows, :].astype(f32) + d_x).astype(low)


def call(kernel, grid, inputs, outputs, scratch, flops, name, aliases=None):
    in_specs = [spec for spec, _ in inputs]
    out_specs = [spec for spec, _, _ in outputs]
    out_shape = [jax.ShapeDtypeStruct(shape, kind) for _, shape, kind in outputs]
    moved = sum(value.size * value.dtype.itemsize for _, value in inputs)
    return pl.pallas_call(
        kernel,
        grid=(grid,),
        in_specs=in_specs,
        out_specs=out_specs,
        out_shape=out_shape,
        scratch_shapes=scratch,
        input_output_aliases=aliases or {},
        cost_estimate=pl.CostEstimate(flops=int(flops), transcendentals=0, bytes_accessed=moved),
        compiler_params=pltpu.CompilerParams(
            dimension_semantics=("arbitrary",), vmem_limit_bytes=56 * 1024 * 1024
        ),
        name=name,
    )(*[value for _, value in inputs])


def swap(value, mask):
    return lax.ppermute(value, axes, [(i, i ^ mask) for i in range(PIECES)])


def tie(value, *after):
    return lax.optimization_barrier((value,) + after)[0]


def along(value, masks):
    return jnp.stack([value] + [swap(value, mask) for mask in masks])


def ends_of(plane, value):
    flat = (PIECES // 2,) + value.shape
    return plane.reshape(flat), swap(plane, 1).reshape(flat)


def weave_first(first, second, rim):
    line = tie(along(first, (8, 16, 24)), rim)
    later = along(tie(second, line), (8, 16, 24))
    got = [tie(swap(line, mask), later) for mask in (2, 4, 6)]
    plane = jnp.stack([line] + got)
    return ends_of(plane, first), tie(later, plane)


def weave_second(line, value, token):
    got = [tie(swap(line, mask), token) for mask in (2, 4, 6)]
    plane = jnp.stack([line] + got)
    return ends_of(plane, value), plane


def parts_of(total):
    return total[0], [total[j].astype(low) for j in range(1, 4)]


def merge_core(kept, got):
    total = kept.astype(f32) + got.astype(f32)
    return parts_of(total.reshape((4, 4) + kept.shape[1:]))


def merge(keep, sends, masks, *after):
    got = [swap(value, mask) for value, mask in zip(sends, masks)]
    if after:
        got = lax.optimization_barrier((*got,) + after)[:3]
    got = [value.astype(f32) for value in got]
    return (keep + got[0]) + (got[1] + got[2])


def tie_all(keep, sends, *after):
    out = lax.optimization_barrier((keep, *sends) + after)
    return out[0], list(out[1:4])


def total_over(value):
    value = value + swap(value, 1)
    for masks in ((2, 4, 6), (8, 16, 24)):
        got = [swap(value, mask) for mask in masks]
        value = (value + got[0]) + (got[1] + got[2])
    return value


def extras(taps, bias, gate, norm):
    left = jnp.concatenate([taps, bias[:, None, :]], axis=1)
    norm = jnp.pad(norm, ((0, 0), (0, gate.shape[1] - norm.shape[1])))
    right = jnp.stack([gate, norm], axis=1)
    left = jnp.pad(left, ((0, 0), (0, 24 - left.shape[1]), (0, 0)))
    right = jnp.pad(right, ((0, 0), (0, 24 - right.shape[1]), (0, 0)))
    return jnp.concatenate([left, right], axis=2)


def order_of_pieces():
    return [(j << 1) | (k << 3) for j in range(4) for k in range(4)]


def relay(ends, totals, forward, fillers):
    count = lax.axis_size("seq")
    incoming = jnp.zeros(ends.shape, f32)
    results, got = [], None
    for hop in range(1, count):
        value = (totals * incoming + ends).astype(low)
        route = [(hop - 1, hop)] if forward else [(count - hop, count - hop - 1)]
        arrived = lax.ppermute(value, "seq", route)
        if fillers:
            made = fillers.pop(0)(got)
            results.append(made)
            arrived = tie(arrived, made[-1])
        got = arrived
        incoming = incoming + got.astype(f32)
    while fillers:
        results.append(fillers.pop(0)(got))
    return incoming.astype(low), results


def per_device(
    hidden,
    lengths,
    norm_gain,
    in_weight,
    conv_weight,
    conv_bias,
    step_bias,
    decay_log,
    skip_gain,
    gate_gain,
    out_weight,
    cotangent,
):
    seqs, piece_len, width = hidden.shape
    groups = piece_len // Q
    blocks = seqs * groups
    rows = seqs * piece_len
    devices = lax.axis_size(axes)
    quick = devices == PIECES
    place = lax.axis_index(axes).astype(jnp.int32)
    me = place if quick else jnp.zeros((), jnp.int32)
    seq_at = lax.axis_index("seq").astype(jnp.int32)
    scal = jnp.concatenate([me[None], seq_at[None], lengths.astype(jnp.int32)])

    rims = hidden[:, piece_len - RIM :, :]
    seq_size = lax.axis_size("seq")
    rim_in = lax.ppermute(rims, "seq", [(i, i + 1) for i in range(seq_size - 1)])
    inner = hidden.reshape(seqs, groups, Q, width)[:, : groups - 1, Q - RIM :, :]
    halo = jnp.concatenate([rim_in[:, None], inner], axis=1).reshape(blocks, RIM, width)

    w_low = in_weight.astype(low)
    o_low = out_weight.astype(low)
    if quick:
        half = o_low.shape[0] // 2
        packed = jnp.concatenate([o_low[:half], o_low[half:]], axis=1)
        second = jnp.stack([w_low[:, :DI], packed])
        first = jnp.concatenate(
            [
                in_weight[:, DI:],
                extras(
                    conv_weight[None], conv_bias[None], gate_gain[None], norm_gain[None]
                )[0],
            ],
            axis=1,
        ).astype(low)
        (ca, cb_pieces), second_line = weave_first(first, second, rim_in)
        begin = tie(scal, second_line)
    else:
        begin = scal
        order = jnp.array(order_of_pieces(), jnp.int32)
        rows_w = lax.all_gather(w_low, axes, axis=0, tiled=True).reshape(PIECES, -1, E)
        full_taps = lax.all_gather(conv_weight.astype(low), axes, axis=1, tiled=True)
        full = [
            lax.all_gather(value.astype(low), axes, axis=0, tiled=True).reshape(PIECES, -1)
            for value in (conv_bias, gate_gain, norm_gain)
        ]
        extra = extras(full_taps.reshape(KW, PIECES, -1).transpose(1, 0, 2), *full)
        whole = jnp.concatenate([rows_w[:, :, DI:], extra], axis=2)
        ca, cb_pieces = whole[order], whole[order + 1]
        outs = lax.all_gather(o_low, axes, axis=0, tiled=True)
        outs = outs.reshape(PIECES, 2, -1, width).transpose(0, 2, 1, 3).reshape(PIECES, -1, DI)
        whole = jnp.stack([rows_w[:, :, :DI], outs], axis=1)
        za, zb = whole[order], whole[order + 1]

    rate = jnp.exp(decay_log)
    log2_rate = rate * 1.4426950408889634
    sb = jnp.pad(step_bias, (0, HL - H)).reshape(1, HL)
    rate_row = jnp.pad(rate, (0, HL - H)).reshape(1, HL)
    log2_row = jnp.pad(log2_rate, (0, HL - H)).reshape(1, HL)
    skip = jnp.repeat(skip_gain, P_SIZE).reshape(1, DI)
    e = jnp.asarray(head_table(), low)
    et = jnp.asarray(np.pad(head_table()[: HL // 2].T, ((0, 0), (0, HL // 2))), low)
    t56 = onehot(HL, CD, H, CD // PIECES)
    t48 = onehot(HL, DI, 80, DI // PIECES)
    t24 = onehot(HL, width, 80, width // PIECES)

    def forth(i):
        return i

    def back(i):
        return (i // groups) * groups + groups - 1 - i % groups

    def tokens(cols, order):
        return pl.BlockSpec((Q, cols), lambda i: (order(i), 0))

    def per_block(height, cols, order):
        return pl.BlockSpec((None, height, cols), lambda i: (order(i), 0, 0))

    def per_seq(height, cols):
        return pl.BlockSpec((None, height, cols), lambda i: (i // groups, 0, 0))

    def fixed(*shape):
        zeros = (0,) * len(shape)
        return pl.BlockSpec(shape, lambda i: zeros, pipeline_mode=pl.Buffered(1))

    def kept(*shape):
        zeros = (0,) * len(shape)
        return pl.BlockSpec(shape, lambda i: zeros)

    scalars = pl.BlockSpec(memory_space=pltpu.SMEM)
    flat_hidden = hidden.reshape(rows, width)
    flat_cot = cotangent.reshape(rows, width)

    (nrm, nrmt, cie, sp, xh, xs, wx, bc, step, cum, dtb, cumt, sloc, pre, ends, totals, wc, taps, gain_in, gain_gate) = call(
        functools.partial(conv_kernel, groups),
        blocks,
        [
            (scalars, begin),
            (tokens(width, forth), flat_hidden),
            (per_block(RIM, width, forth), halo),
            (fixed(*ca.shape), ca),
            (fixed(*ca.shape), cb_pieces),
            (fixed(HL, CD), t56),
            (fixed(HL, DI), t48),
            (fixed(HL, width), t24),
            (fixed(1, HL), sb),
            (fixed(1, HL), log2_row),
            (fixed(HL, DI), e),
        ],
        [
            (tokens(width, forth), (rows, width), low),
            (pl.BlockSpec((width, Q), lambda i: (0, i)), (width, rows), low),
            (per_block(Q + RIM, CD, forth), (blocks, Q + RIM, CD), low),
            (tokens(CD, forth), (rows, CD), f32),
            (tokens(DI, forth), (rows, DI), low),
            (tokens(DI, forth), (rows, DI), low),
            (tokens(DI, forth), (rows, DI), low),
            (tokens(2 * N, forth), (rows, 2 * N), low),
            (tokens(HL, forth), (rows, HL), f32),
            (tokens(HL, forth), (rows, HL), f32),
            (tokens(HL, forth), (rows, HL), f32),
            (per_block(H, Q, forth), (blocks, H, Q), f32),
            (per_block(N, DI, forth), (blocks, N, DI), f32),
            (per_block(8, DI, forth), (blocks, 8, DI), f32),
            (per_seq(N, DI), (seqs, N, DI), f32),
            (per_seq(1, DI), (seqs, 1, DI), f32),
            (kept(width, CW), (width, CW), low),
            (kept(8, CD), (8, CD), f32),
            (kept(8, width), (8, width), f32),
            (kept(8, DI), (8, DI), f32),
        ],
        [
            pltpu.VMEM((Q + RIM, width), low),
            pltpu.VMEM((Q + RIM, CH), f32),
            pltpu.VMEM((N, DI), f32),
            pltpu.VMEM((8, DI), f32),
            pltpu.VMEM((2, HL, HL), f32),
        ],
        2.0 * rows * width * CW,
        "conv",
    )
    if quick:
        (za, zb), token = weave_second(second_line, second, cum)
        bc_after = tie(bc, token)
    else:
        bc_after = bc

    def intra_part(got):
        return call(
            intra_kernel,
            blocks,
            [
                (tokens(2 * N, forth), bc_after),
                (tokens(DI, forth), xs),
                (tokens(HL, forth), cum),
                (per_block(H, Q, forth), cumt),
            ],
            [(tokens(DI, forth), (rows, DI), f32)],
            [pltpu.VMEM((Q, Q), f32)],
            2.0 * rows * Q * DI * 2,
            "intra",
        )

    def after(value, got):
        return value if got is None else tie(value, got)

    def project_part(got):
        return call(
            functools.partial(project_kernel, groups),
            blocks,
            [
                (scalars, after(scal, got)),
                (tokens(width, forth), nrm),
                (tokens(width, forth), flat_cot),
                (fixed(*za.shape), za),
                (fixed(*za.shape), zb),
            ],
            [
                (tokens(DI, forth), (rows, DI), f32),
                (tokens(DI, forth), (rows, DI), f32),
                (tokens(width, forth), (rows, width), low),
                (kept(width, DI), (width, DI), low),
                (kept(DI, width), (DI, width), low),
            ],
            [],
            4.0 * rows * width * DI,
            "project",
        )

    incoming, ((intra,), (z, dn, db, wz, wo)) = relay(
        ends, totals, True, [intra_part, project_part]
    )

    (out, dz, dy, gdy, gn, sbf, rs1, dloc, suf, back_ends, back_totals, gacc, kacc) = call(
        functools.partial(gate_kernel, groups),
        blocks,
        [
            (scalars, scal),
            (tokens(DI, back), intra),
            (tokens(DI, back), xh),
            (tokens(2 * N, back), bc),
            (tokens(HL, back), cum),
            (per_block(N, DI, back), sloc),
            (per_block(8, DI, back), pre),
            (per_seq(N, DI), incoming),
            (tokens(DI, back), z),
            (tokens(DI, back), dn),
            (tokens(width, back), flat_hidden),
            (fixed(DI, width), wo),
            (fixed(8, DI), gain_gate),
            (fixed(1, DI), skip),
            (fixed(HL, DI), e),
            (fixed(DI, HL), et),
        ],
        [
            (tokens(width, back), (rows, width), low),
            (tokens(DI, back), (rows, DI), low),
            (tokens(DI, back), (rows, DI), low),
            (tokens(DI, back), (rows, DI), low),
            (tokens(DI, back), (rows, DI), low),
            (per_block(N, DI, back), (blocks, N, DI), low),
            (tokens(HL, back), (rows, HL), f32),
            (per_block(N, DI, back), (blocks, N, DI), f32),
            (per_block(8, DI, back), (blocks, 8, DI), f32),
            (per_seq(N, DI), (seqs, N, DI), f32),
            (per_seq(1, DI), (seqs, 1, DI), f32),
            (kept(8, DI), (8, DI), f32),
            (kept(8, DI), (8, DI), f32),
        ],
        [
            pltpu.VMEM((Q, DI), f32),
            pltpu.VMEM((Q, DI), f32),
            pltpu.VMEM((Q, DI), f32),
            pltpu.VMEM((32, DI), f32),
            pltpu.VMEM((32, DI), f32),
            pltpu.VMEM((32, DI), f32),
            pltpu.VMEM((N, DI), f32),
            pltpu.VMEM((8, DI), f32),
        ],
        4.0 * rows * width * DI,
        "gate",
    )

    def intra_back_part(got):
        return call(
            intra_back_kernel,
            blocks,
            [
                (tokens(2 * N, forth), after(bc, got)),
                (tokens(DI, forth), xs),
                (tokens(DI, forth), xh),
                (tokens(DI, forth), dy),
                (tokens(HL, forth), step),
                (tokens(HL, forth), cum),
                (per_block(H, Q, forth), cumt),
                (fixed(1, DI), skip),
                (fixed(HL, DI), e),
                (fixed(DI, HL), et),
            ],
            [
                (tokens(DI, forth), (rows, DI), f32),
                (tokens(2 * N, forth), (rows, 2 * N), f32),
                (tokens(HL, forth), (rows, HL), f32),
            ],
            [pltpu.VMEM((Q, Q), f32), pltpu.VMEM((Q, Q), f32)],
            4.0 * rows * Q * DI * 2,
            "intra_back",
        )

    share = rows // 4
    piece = (PIECES // 2, 2, width // PIECES, DI)

    def early_part(got):
        return call(
            early_grad_kernel,
            4,
            [
                (scalars, after(scal, got)),
                (fixed(width, rows), nrmt),
                (pl.BlockSpec((rows, DI // 4), lambda i: (0, i)), dz),
                (pl.BlockSpec((share, DI), lambda i: (i, 0)), dz),
                (pl.BlockSpec((rows, DI // 4), lambda i: (0, i)), gn),
                (fixed(rows, width), db),
                (fixed(width, DI), wz),
            ],
            [
                (kept(*piece), piece, low),
                (kept(*piece), piece, low),
                (pl.BlockSpec((share, width), lambda i: (i, 0)), (rows, width), f32),
            ],
            [pltpu.VMEM((width, DI // 4), f32), pltpu.VMEM((DI, width), f32)],
            6.0 * rows * width * DI,
            "early_grad",
        )

    back_incoming, ((e0, e1, dnz), (dx, dbc, rs2)) = relay(
        back_ends, back_totals, False, [early_part, intra_back_part]
    )
    if quick:
        early = merge_core(e0, tie(swap(e1, 1), rs2))
        back_incoming = tie(back_incoming, *early[1])

    (dcv, cacc, hacc, heads_out, tails_out) = call(
        functools.partial(conv_back_kernel, groups),
        blocks,
        [
            (per_block(N, DI, back), dloc),
            (per_block(8, DI, back), suf),
            (per_seq(N, DI), back_incoming),
            (per_block(N, DI, back), sbf),
            (tokens(DI, back), xh),
            (tokens(DI, back), wx),
            (tokens(DI, back), gdy),
            (tokens(DI, back), dx),
            (tokens(2 * N, back), dbc),
            (tokens(2 * N, back), bc),
            (tokens(HL, back), cum),
            (tokens(HL, back), step),
            (tokens(HL, back), dtb),
            (tokens(HL, back), rs1),
            (tokens(HL, back), rs2),
            (per_block(Q + RIM, CD, back), cie),
            (tokens(CD, back), sp),
            (fixed(8, CD), taps),
            (fixed(1, HL), rate_row),
            (fixed(HL, DI), e),
            (fixed(DI, HL), et),
        ],
        [
            (tokens(CW, back), (rows, CW), low),
            (kept(8 * (KW + 1), CD), (8 * (KW + 1), CD), f32),
            (kept(16, HL), (16, HL), f32),
            (per_seq(8, CW), (seqs, 8, CW), low),
            (per_seq(16, CW), (seqs, 16, CW), f32),
        ],
        [
            pltpu.VMEM((Q + 16, CH), f32),
            pltpu.VMEM((8, CD), f32),
        ],
        6.0 * rows * N * DI,
        "conv_back",
    )
    turn = scal
    if quick:
        early = parts_of(merge(*early, (2, 4, 6), hacc))
        turn = tie(scal, *early[1])
    returned = lax.ppermute(heads_out, "seq", [(i, i - 1) for i in range(1, seq_size)])

    late = (PIECES // 2, width // PIECES, CW)
    late_spec = pl.BlockSpec((PIECES // 2, width // PIECES, CW // 5), lambda i: (0, 0, i))
    (l0, l1, dcv) = call(
        late_grad_kernel,
        5,
        [
            (scalars, turn),
            (fixed(width, rows), nrmt),
            (pl.BlockSpec((rows, CW // 5), lambda i: (0, i)), dcv),
            (pl.BlockSpec((seqs, 16, CW // 5), lambda i: (0, 0, i)), tails_out),
            (pl.BlockSpec((seqs, 8, CW // 5), lambda i: (0, 0, i)), returned),
        ],
        [
            (late_spec, late, low),
            (late_spec, late, low),
            (pl.BlockSpec((rows, CW // 5), lambda i: (0, i)), (rows, CW), low),
        ],
        [pltpu.VMEM((width, CW // 5), f32)],
        2.0 * rows * width * CW,
        "late_grad",
    )

    def input_part(first, count, past, token):
        def order(i):
            return i + first

        return call(
            input_kernel,
            count,
            [
                (tokens(CW, order), dcv),
                (tokens(width, order), dnz),
                (fixed(width, CW), wc),
                (tokens(width, order), flat_hidden),
                (tokens(width, order), flat_cot),
                (fixed(8, width), gain_in if token is None else tie(gain_in, *token)),
                (pl.BlockSpec(memory_space=pl.ANY), past),
            ],
            [
                (tokens(width, order), (rows, width), low),
                (kept(8, width), (8, width), f32),
            ],
            [pltpu.VMEM((Q, width), f32)],
            2.0 * rows * width * CW * count / blocks,
            "input",
            {6: 0} if first else None,
        )

    half_blocks = blocks // 2
    if quick:
        gh, nacc = input_part(0, half_blocks, scal, None)
        late_sum = merge_core(l0, tie(swap(l1, 1), nacc))
        early = tie_all(*early, late_sum[1][0])
        gh, nacc2 = input_part(half_blocks, blocks - half_blocks, gh, late_sum[1])
        late_sum = parts_of(merge(*late_sum, (2, 4, 6), nacc2))
        early = merge(*early, (8, 16, 24), nacc2)
        late_sum = tie_all(*late_sum, early)
        nacc = nacc + nacc2
    else:
        gh, nacc = input_part(0, blocks, scal, None)

    conv_sums = cacc.reshape(KW + 1, 8, CD).sum(axis=1)
    skips = kacc.sum(axis=0).reshape(H, P_SIZE).sum(axis=1)
    scalar_sums = jnp.concatenate(
        [hacc[0:8].sum(axis=0)[:H], -hacc[8:16].sum(axis=0)[:H] * rate, skips]
    )
    vector = jnp.concatenate(
        [nacc.sum(axis=0), conv_sums.reshape(-1), gacc.sum(axis=0), scalar_sums]
    )
    if quick:
        length = vector.shape[0]
        vector = tie(vector, late_sum[1][0])
        vector = total_over(jnp.pad(vector, (0, -length % (8 * HALF))).reshape(-1, HALF))
        vector = vector.reshape(-1)[:length]
        own_late = merge(*late_sum, (8, 16, 24))
        own_z, own_out = early[0], early[1]
        own_out = jnp.concatenate([own_out[:, : DI // 2], own_out[:, DI // 2 :]], axis=0)
    else:
        vector = lax.psum(vector, axes)
        order = jnp.array(order_of_pieces(), jnp.int32)
        inverse = jnp.argsort(jnp.concatenate([order, order + 1]))
        whole = jnp.concatenate([e0, e1])[inverse].astype(f32)
        outs = whole[:, 1].reshape(PIECES, -1, 2, width).transpose(0, 2, 1, 3).reshape(DI, width)
        own_z = lax.psum_scatter(
            whole[:, 0].reshape(width, DI), axes, scatter_dimension=0, tiled=True
        )
        own_out = lax.psum_scatter(outs, axes, scatter_dimension=0, tiled=True)
        whole = jnp.concatenate([l0, l1])[inverse].astype(f32).reshape(width, CW)
        own_late = lax.psum_scatter(whole, axes, scatter_dimension=0, tiled=True)

    def own(value, size, axis):
        return lax.dynamic_slice_in_dim(value, place * size, size, axis)

    at = width
    g_norm = own(vector[:at], norm_gain.shape[0], 0)
    g_taps = own(vector[at : at + KW * CD].reshape(KW, CD), CD // devices, 1)
    at += KW * CD
    g_bias = own(vector[at : at + CD], CD // devices, 0)
    at += CD
    g_gate = own(vector[at : at + DI], gate_gain.shape[0], 0)
    at += DI
    g_in = jnp.concatenate([own_z, own_late[:, : CD + H]], axis=1)
    return (
        out.reshape(hidden.shape),
        gh.reshape(hidden.shape),
        g_norm,
        g_in,
        g_taps,
        g_bias,
        vector[at : at + H],
        vector[at + H : at + 2 * H],
        vector[at + 2 * H : at + 3 * H],
        g_gate,
        own_out,
    )


def solution(mesh):
    return jax.shard_map(
        per_device,
        mesh=mesh,
        in_specs=(
            P("dp", "seq", None),
            P("dp"),
            P(("dp", "seq")),
            P(("dp", "seq"), None),
            P(None, ("dp", "seq")),
            P(("dp", "seq")),
            P(),
            P(),
            P(),
            P(("dp", "seq")),
            P(("dp", "seq"), None),
            P("dp", "seq", None),
        ),
        out_specs=(
            P("dp", "seq", None),
            P("dp", "seq", None),
            P(("dp", "seq")),
            P(("dp", "seq"), None),
            P(None, ("dp", "seq")),
            P(("dp", "seq")),
            P(),
            P(),
            P(),
            P(("dp", "seq")),
            P(("dp", "seq"), None),
        ),
        check_vma=False,
    )
```

```python
import functools

import jax
import jax.numpy as jnp
import numpy as np
from jax import lax
from jax.experimental import pallas as pl
from jax.experimental.pallas import tpu as pltpu
from jax.sharding import PartitionSpec as P

H = 24
P_SIZE = 64
N = 128
KW = 4
Q = 256
E = 3352
DI = 1536
CD = 1792
HL = 128
CW = CD + HL
CH = 256
HALF = 128
RIM = 16
PIECES = 32
NEG = -1e30
LIMITS = {
    "conv": 56,
    "intra": 56,
    "project": 48,
    "gate": 48,
    "early_grad": 56,
    "intra_back": 56,
    "conv_back": 56,
    "late_grad": 56,
    "input": 56,
}

epsilon = 1e-05
low = jnp.bfloat16
f32 = jnp.float32
axes = ("dp", "seq")


def onehot(rows, cols, first, period):
    table = np.zeros((rows, cols), np.float32)
    at = np.arange(cols)
    table[first + at % period, at] = 1.0
    return jnp.asarray(table, low)


def head_table():
    table = np.zeros((HL, DI), np.float32)
    at = np.arange(DI)
    table[at // P_SIZE, at] = 1.0
    table[HL // 2 + at // P_SIZE, at] = 1.0
    return table


def dot(left, right, dims):
    return lax.dot_general(left, right, (dims, ((), ())), preferred_element_type=f32)


def nn(left, right):
    return dot(left, right, ((1,), (0,)))


def nt(left, right):
    return dot(left, right, ((1,), (1,)))


def tn(left, right):
    return dot(left, right, ((0,), (0,)))


def pack(value):
    top = value.astype(low).astype(f32)
    rest = pltpu.roll(value - top, HL // 2, 1)
    lane = lax.broadcasted_iota(jnp.int32, value.shape, 1)
    return jnp.where(lane < HL // 2, top, rest).astype(low)


def spread(packed, table):
    return nn(packed, table)


def spread_all(packed, table):
    wide = nn(jnp.concatenate(packed, axis=0), table)
    parts, at = [], 0
    for value in packed:
        parts.append(wide[at : at + value.shape[0], :])
        at += value.shape[0]
    return parts


def gather_all(values, table):
    tops = [value.astype(low) for value in values]
    rests = [(value - top.astype(f32)).astype(low) for value, top in zip(values, tops)]
    parts = spread_all(tops + rests, table)
    return [parts[i] + parts[i + len(values)] for i in range(len(values))]


def gather_heads(value, table):
    return gather_all([value], table)[0]


def running_sum(value, reverse):
    rows = value.shape[0]
    at = lax.broadcasted_iota(jnp.int32, value.shape, 0)
    step = 1
    while step < rows:
        if reverse:
            value = value + jnp.where(at < rows - step, pltpu.roll(value, rows - step, 0), 0.0)
        else:
            value = value + jnp.where(at >= step, pltpu.roll(value, step, 0), 0.0)
        step *= 2
    return value


def softplus(value):
    tail = jnp.exp(-jnp.abs(value))
    series = tail * (1.0 - tail * (0.5 - tail * (1.0 / 3.0 - tail * (0.25 - tail * 0.2))))
    return jnp.maximum(value, 0.0) + jnp.where(tail < 0.03125, series, jnp.log(1.0 + tail))


def fold8(value):
    return jnp.sum(value.reshape(value.shape[0] // 8, 8, value.shape[1]), axis=0)


def pair_rows(me, own, other):
    first = (me & 1) == 0
    return jnp.concatenate([jnp.where(first, own, other), jnp.where(first, other, own)], axis=0)


def source_of(me, place):
    return me ^ ((place // 4) * 2) ^ ((place % 4) * 8)


def place_of(piece):
    return ((piece >> 1) & 3) * 4 + (piece >> 3)


def conv_kernel(
    groups, scal, x, halo, wa, wb, t56, t48, t24, par, e,
    nrm_o, nrmt_o, cie_o, sp_o, xh_o, xs_o, wx_o, bc_o, step_o, cum_o, dtb_o, cumt_o,
    sloc_o, pre_o, r_o, rl_o, tot_o, wc_o, taps_o, gain_o, gate_o,
    nrm, run, dec, small, *slots,
):
    block = pl.program_id(0)
    fresh = block % groups == 0
    zero = scal[scal.shape[0] - 1]

    @pl.when(block == 0)
    def assemble():
        me = scal[0]

        def one(place, carry):
            chip = source_of(me, place) >> 1
            own, other = wa[place].astype(f32), wb[place].astype(f32)
            wc_o[pl.ds(pl.multiple_of(chip * 48, 16), 48), :] = pair_rows(me, own, other).astype(low)
            rows = pl.ds(pl.multiple_of(place * 8, 8), 8)
            small[0, rows, :] = own[0:8, CD:CW]
            small[1, rows, :] = other[0:8, CD:CW]
            return carry

        lax.fori_loop(0, PIECES // 2, one, 0)
        at = lax.broadcasted_iota(jnp.int32, (PIECES, 1), 0)
        slot = at & (PIECES // 2 - 1)
        ids = me ^ ((slot >> 2) << 1) ^ ((slot & 3) << 3) ^ (at >> 4)

        def row_of(k, table, size):
            pieces = [small[which, pl.ds(k, PIECES // 2, stride=8), :] for which in range(2)]
            wide = nn(jnp.concatenate(pieces, axis=0).astype(low), table)
            lane = lax.broadcasted_iota(jnp.int32, wide.shape, 1)
            inside = jnp.logical_and(lane >= ids * size, lane < (ids + 1) * size)
            return jnp.sum(jnp.where(inside, wide, 0.0), axis=0, keepdims=True)

        for k in range(KW + 1):
            taps_o[k : k + 1, :] = row_of(k, t56[...], CD // PIECES)
        gate_o[0:1, :] = row_of(0, t48[...], DI // PIECES)
        gain_o[0:1, :] = row_of(1, t24[...], gain_o.shape[1] // PIECES)

    def normed(rows):
        wide = rows.astype(f32)
        scale = lax.rsqrt(jnp.mean(wide * wide, axis=-1, keepdims=True) + epsilon)
        return (wide * scale * gain_o[0:1, :]).astype(low)

    nrm[0:RIM, :] = normed(halo[...])
    for r in range(0, Q, 32):
        nrm[RIM + r : RIM + r + 32, :] = normed(x[r : r + 32, :])
    nrm_o[...] = nrm[RIM:, :]
    nrmt_o[...] = nrm[RIM:, :].T

    for c in range(0, CD, CH):
        cols = slice(c, c + CH)
        conv_in = nn(nrm[...], wc_o[:, cols]).astype(low)
        cie_o[:, cols] = conv_in
        wide = conv_in.astype(f32)
        for side in range(2):
            span = slice(c + side * HALF, c + (side + 1) * HALF)
            cs = slots[c // HALF + side]
            cs[...] = wide[:, side * HALF : (side + 1) * HALF]
            for r in range(0, Q, 64):
                taps = taps_o[0:1, span] * cs[pl.ds(zero + (RIM - 3 + r), 64), :]
                for k in range(1, KW):
                    taps = taps + taps_o[k : k + 1, span] * cs[pl.ds(zero + (RIM - 3 + k + r), 64), :]
                pre = taps_o[KW : KW + 1, span] + taps
                sig = jax.nn.sigmoid(pre)
                act = (pre * sig).astype(low)
                sp_o[r : r + 64, span] = sig * (1.0 + pre * (1.0 - sig))
                if c < DI:
                    xh_o[r : r + 64, span] = act
                else:
                    bc_o[r : r + 64, side * HALF : (side + 1) * HALF] = act

    dtb = nn(nrm[RIM:, :], wc_o[:, CD:CW]) + par[0:1, :]
    step = softplus(dtb)
    cum = running_sum(-step * par[1:2, :], False)
    step_o[...] = step
    cum_o[...] = cum
    dtb_o[...] = dtb
    cumt_o[...] = cum.T[0:H, :]
    last = cum[Q - 1 : Q, :]
    steps = pack(step)
    tails = pack(jnp.exp2(last - cum) * step)
    decays = pack(jnp.broadcast_to(jnp.exp2(last), (8, HL)))
    for c in range(0, DI, CH):
        cols = slice(c, c + CH)
        table = e[:, cols]
        wide = xh_o[:, cols].astype(f32)
        xs_o[:, cols] = (spread(steps, table) * wide).astype(low)
        tail_e, decay = spread_all([tails, decays], table)
        weighted = (tail_e * wide).astype(low)
        wx_o[:, cols] = weighted
        local = tn(bc_o[:, 0:N], weighted)
        before = jnp.where(fresh, 0.0, run[:, cols])
        sloc_o[:, cols] = before
        after = decay[0:1, :] * before + local
        run[:, cols] = after
        r_o[:, cols] = after
        rl_o[:, cols] = after.astype(low)
        product = jnp.where(fresh, 1.0, dec[:, cols])
        pre_o[:, cols] = product
        product = product * decay
        dec[:, cols] = product
        tot_o[:, cols] = product[0:1, :]


def block_rows(block):
    return pl.ds(pl.multiple_of(block * Q, Q), Q)


def intra_kernel(bc, xs, cum, cumt, o, sc):
    sc[...] = nt(bc[:, N : 2 * N], bc[:, 0:N])
    at = lax.broadcasted_iota(jnp.int32, (HALF, HALF), 0)
    to = lax.broadcasted_iota(jnp.int32, (HALF, HALF), 1)
    lower = at >= to
    left = lax.broadcasted_iota(jnp.int32, (HALF, HALF), 1) < P_SIZE
    for pair in range(H // 2):
        cols = slice(pair * HALF, (pair + 1) * HALF)
        x_pair = xs[:, cols]
        m00, m10, m11 = [], [], []
        for h in (2 * pair, 2 * pair + 1):
            row = cumt[h : h + 1, :]
            upper_col, lower_col = cum[0:HALF, h : h + 1], cum[HALF:, h : h + 1]
            l00 = jnp.exp2(jnp.where(lower, upper_col - row[:, 0:HALF], NEG))
            m00.append((sc[0:HALF, 0:HALF] * l00).astype(low))
            l10 = jnp.exp2(lower_col - row[:, 0:HALF])
            m10.append((sc[HALF:, 0:HALF] * l10).astype(low))
            l11 = jnp.exp2(jnp.where(lower, lower_col - row[:, HALF:], NEG))
            m11.append((sc[HALF:, HALF:] * l11).astype(low))
        top = nn(jnp.concatenate(m00, axis=0), x_pair[0:HALF, :])
        sides = [jnp.concatenate([m10[i], m11[i]], axis=1) for i in range(2)]
        bottom = nn(jnp.concatenate(sides, axis=0), x_pair)
        o[0:HALF, cols] = jnp.where(left, top[0:HALF, :], top[HALF:, :])
        o[HALF:, cols] = jnp.where(left, bottom[0:HALF, :], bottom[HALF:, :])


def valid_column(scal, groups, block):
    seq, group = block // groups, block % groups
    at = scal[1] * (groups * Q) + group * Q + lax.broadcasted_iota(jnp.int32, (Q, 1), 0)
    return (at < scal[2 + seq]).astype(f32)


def project_kernel(groups, scal, nrm, cot, wa, wb, z_all, dn_all, db_o, wz_o, wo_o):
    block = pl.program_id(0)
    z_o, dn_o = z_all.at[block_rows(block), :], dn_all.at[block_rows(block), :]

    @pl.when(block == 0)
    def assemble():
        me = scal[0]

        def halves(packed):
            return jnp.concatenate([packed[:, 0 : DI // 2], packed[:, DI // 2 :]], axis=0)

        def one(place, carry):
            chip = source_of(me, place) >> 1
            own, other = wa[place, 0].astype(f32), wb[place, 0].astype(f32)
            wz_o[pl.ds(pl.multiple_of(chip * 48, 16), 48), :] = pair_rows(me, own, other).astype(low)
            own, other = halves(wa[place, 1].astype(f32)), halves(wb[place, 1].astype(f32))
            wo_o[pl.ds(pl.multiple_of(chip * 96, 16), 96), :] = pair_rows(me, own, other).astype(low)
            return carry

        lax.fori_loop(0, PIECES // 2, one, 0)

    db_o[...] = (cot[...].astype(f32) * valid_column(scal, groups, block)).astype(low)
    for c in range(0, DI, CH):
        z_o[:, c : c + CH] = nn(nrm[...], wz_o[:, c : c + CH])
        dn_o[:, c : c + CH] = nt(db_o[...], wo_o[c : c + CH, :])


def gate_kernel(
    groups, hops, scal, intra, xh, bc, cum, sloc, pre, *refs
):
    inc = refs[:hops]
    z_all, dn_all, hid, wo, gg, par, e, et = refs[hops : hops + 8]
    (
        out_o, dz_o, dy_o, gdy_o, gn_o, sbf_o, rs_o, dloc_o, suf_o, rd_o, rdl_o, tot_o, kacc_o,
        yi_s, ge_s, pr_s, y_s, sg_s, gt_s, run, dec, skip, fall,
    ) = refs[hops + 8 :]
    at = pl.program_id(0)
    fresh = at % groups == 0
    block = (at // groups) * groups + groups - 1 - at % groups
    here = block_rows(block)
    z, dn = z_all.at[here, :], dn_all.at[here, :]

    @pl.when(at == 0)
    def start():
        kacc_o[...] = jnp.zeros_like(kacc_o)

    c_rows = bc[:, N : 2 * N]
    growth = pack(jnp.exp2(cum[...]))
    params = pack(par[...])
    decays = pack(jnp.broadcast_to(jnp.exp2(cum[Q - 1 : Q, :]), (8, HL)))
    for c in range(0, DI, CH):
        cols = slice(c, c + CH)
        begin = (sloc[:, cols] + pre[0:1, cols] * total_of(inc, cols)).astype(low)
        sbf_o[:, cols] = begin
        wide, skip[:, cols], fall[:, cols] = spread_all([growth, params, decays], e[:, cols])
        ge_s[:, cols] = wide
        yi_s[:, cols] = intra[:, cols] + wide * nn(c_rows, begin)

    def body(r):
        rows = slice(r, r + 32)
        squares = jnp.zeros((32, HALF), f32)
        crosses = jnp.zeros((32, HALF), f32)
        for c in range(0, DI, HALF):
            cols = slice(c, c + HALF)
            zv = z[rows, cols]
            y = yi_s[rows, cols] + skip[3:4, cols] * xh[rows, cols].astype(f32)
            sig = jax.nn.sigmoid(zv)
            gated = y * (zv * sig)
            squares = squares + gated * gated
            crosses = crosses + (dn[rows, cols] * gg[0:1, cols]) * gated
            y_s[rows, cols] = y
            sg_s[rows, cols] = sig
            gt_s[rows, cols] = gated
        scale = lax.rsqrt(jnp.sum(squares, axis=1, keepdims=True) / DI + epsilon)
        shift = scale * scale * scale * (jnp.sum(crosses, axis=1, keepdims=True) / DI)
        for c in range(0, DI, HALF):
            cols = slice(c, c + HALF)
            zv, y, sig, gated = z[rows, cols], y_s[rows, cols], sg_s[rows, cols], gt_s[rows, cols]
            gained = gg[0:1, cols]
            gn_o[rows, cols] = (gated * scale * gained).astype(low)
            d_gated = scale * (dn[rows, cols] * gained) - gated * shift
            d_sig = d_gated * sig
            d_wide = d_sig * zv
            dz_o[rows, cols] = (y * (d_sig + d_wide * (1.0 - sig))).astype(low)
            d_low = d_wide.astype(low)
            dy_o[rows, cols] = d_low
            d_y = d_low.astype(f32)
            kacc_o[:, cols] += fold8(d_y * xh[rows, cols].astype(f32))
            gdy_o[rows, cols] = (ge_s[rows, cols] * d_y).astype(low)
            pr_s[rows, cols] = d_y * yi_s[rows, cols]

    for r in range(0, Q, 32):
        body(r)

    valid = valid_column(scal, groups, block)
    for c in range(0, DI // 2, CH):
        branch = nn(gn_o[...], wo[:, c : c + CH])
        out_o[:, c : c + CH] = (hid[:, c : c + CH].astype(f32) + valid * branch).astype(low)
    sums = jnp.zeros((Q, HL), f32)
    for c in range(0, DI, CH):
        cols = slice(c, c + CH)
        sums = sums + gather_heads(pr_s[:, cols], et[cols, :])
        decay = fall[:, cols]
        before = jnp.where(fresh, 0.0, run[:, cols])
        dloc_o[:, cols] = before
        after = decay[0:1, :] * before + tn(c_rows, gdy_o[:, cols])
        run[:, cols] = after
        rd_o[:, cols] = after
        rdl_o[:, cols] = after.astype(low)
        product = jnp.where(fresh, 1.0, dec[:, cols])
        suf_o[:, cols] = product
        product = product * decay
        dec[:, cols] = product
        tot_o[:, cols] = product[0:1, :]
    rs_o[...] = sums


def intra_back_kernel(bc, xs, xh, dy, step, cum, cumt, par, e, et, dx_o, dbc_o, rs_o, sc, acc):
    sc[...] = nt(bc[:, 0:N], bc[:, N : 2 * N])
    acc[...] = jnp.zeros_like(acc)
    at = lax.broadcasted_iota(jnp.int32, (HALF, HALF), 0)
    to = lax.broadcasted_iota(jnp.int32, (HALF, HALF), 1)
    upper = at <= to
    left = lax.broadcasted_iota(jnp.int32, (Q, HALF), 1) < P_SIZE
    steps = pack(step[...])
    params = pack(par[...])
    sums = jnp.zeros((Q, HL), f32)
    for quad in range(H // 4):
        flows = []
        for pair in (2 * quad, 2 * quad + 1):
            cols = slice(pair * HALF, (pair + 1) * HALF)
            dy_pair = dy[:, cols]
            x_pair = xs[:, cols]
            heads = (2 * pair, 2 * pair + 1)
            zeros = jnp.zeros_like(x_pair)
            x_a, x_b = jnp.where(left, x_pair, zeros), jnp.where(left, zeros, x_pair)
            rows = [cumt[h : h + 1, :] for h in heads]
            x_top = jnp.concatenate([x_a[0:HALF, :], x_b[0:HALF, :]], axis=0)
            grown = nt(x_top, dy_pair)
            m00, m01, m11 = [], [], []
            total = 0.0
            for i, h in enumerate(heads):
                first_col = cum[0:HALF, h : h + 1]
                l00 = jnp.exp2(jnp.where(upper, rows[i][:, 0:HALF] - first_col, NEG))
                m00.append((sc[0:HALF, 0:HALF] * l00).astype(low))
                total = total + grown[i * HALF : (i + 1) * HALF, 0:HALF] * l00
            acc[0:HALF, 0:HALF] += total
            total = 0.0
            for i, h in enumerate(heads):
                first_col = cum[0:HALF, h : h + 1]
                l01 = jnp.exp2(rows[i][:, HALF:] - first_col)
                m01.append((sc[0:HALF, HALF:] * l01).astype(low))
                total = total + grown[i * HALF : (i + 1) * HALF, HALF:] * l01
            acc[0:HALF, HALF:] += total
            sides = [jnp.concatenate([m00[i], m01[i]], axis=1) for i in range(2)]
            top = nn(jnp.concatenate(sides, axis=0), dy_pair)
            x_bottom = jnp.concatenate([x_a[HALF:, :], x_b[HALF:, :]], axis=0)
            grown = nt(x_bottom, dy_pair[HALF:, :])
            total = 0.0
            for i, h in enumerate(heads):
                second_col = cum[HALF:, h : h + 1]
                l11 = jnp.exp2(jnp.where(upper, rows[i][:, HALF:] - second_col, NEG))
                m11.append((sc[HALF:, HALF:] * l11).astype(low))
                total = total + grown[i * HALF : (i + 1) * HALF, :] * l11
            acc[HALF:, HALF:] += total
            bottom = nn(jnp.concatenate(m11, axis=0), dy_pair[HALF:, :])
            half_left = left[0:HALF]
            flows.append(
                jnp.concatenate(
                    [
                        jnp.where(half_left, top[0:HALF, :], top[HALF:, :]),
                        jnp.where(half_left, bottom[0:HALF, :], bottom[HALF:, :]),
                    ],
                    axis=0,
                )
            )
        cols = slice(quad * CH, (quad + 1) * CH)
        flow = jnp.concatenate(flows, axis=1)
        sums = sums + gather_heads(flow * xh[:, cols].astype(f32), et[cols, :])
        step_e, skip = spread_all([steps, params], e[:, cols])
        dx_o[:, cols] = step_e * flow + skip[3:4, :] * dy[:, cols].astype(f32)
    rs_o[...] = sums
    scores = acc[...].astype(low)
    dbc_o[:, 0:N] = nn(scores, bc[:, N : 2 * N])
    dbc_o[:, N : 2 * N] = tn(scores, bc[:, 0:N])


def conv_back_kernel(
    groups, hops, scal, dloc, suf, sbf, xh, wx, gdy, dx, dbc, bc, cum, step, dtb, rs1, rs2, *refs
):
    inc = refs[:hops]
    cie, sp, cw, par, e, et, dcv_o, kacc_o, hacc_o, head_o, tail_o, nxt, *slots = refs[hops:]
    at = pl.program_id(0)
    fresh = at % groups == 0
    opening = at % groups == groups - 1
    zero = scal[scal.shape[0] - 1]

    @pl.when(at == 0)
    def start():
        kacc_o[...] = jnp.zeros_like(kacc_o)
        hacc_o[...] = jnp.zeros_like(hacc_o)

    def conv_back(flow, c):
        for side in range(2):
            half_back(flow[:, side * HALF : (side + 1) * HALF], c + side * HALF)

    def half_back(flow, c):
        ds = slots[c // HALF]
        cols = slice(c, c + HALF)
        ds[0:8, :] = jnp.zeros((8, HALF), f32)
        ds[8 + Q :, :] = jnp.where(fresh, 0.0, nxt[:, cols])
        ds[8 : 8 + Q, :] = flow * sp[:, cols]
        nxt[:, cols] = ds[8:16, :]
        taps = [cw[k : k + 1, cols] for k in range(KW)]
        sums = [jnp.zeros((8, HALF), f32) for _ in range(KW + 1)]

        def views_at(begin, count):
            return [ds[pl.ds(zero + (begin + 11 - k), count), :] for k in range(KW)]

        def back(views):
            total = taps[0] * views[0]
            for k in range(1, KW):
                total = total + taps[k] * views[k]
            return total

        for r in range(0, Q, 64):
            views = views_at(r, 64)
            dcv_o[r : r + 64, cols] = back(views).astype(low)
            conv_in = cie[RIM + r : RIM + r + 64, cols].astype(f32)
            for k in range(KW):
                sums[k] = sums[k] + fold8(views[k] * conv_in)
            sums[KW] = sums[KW] + fold8(views[KW - 1])
        views = views_at(-8, 8)
        head_o[:, cols] = back(views).astype(low)
        conv_in = cie[0:RIM, cols].astype(f32)[8:16, :]
        for k in range(KW):
            kacc_o[8 * k : 8 * k + 8, cols] += sums[k] + jnp.where(opening, views[k] * conv_in, 0.0)
        kacc_o[8 * KW : 8 * KW + 8, cols] += sums[KW]

    cumv = cum[...]
    stepv = step[...]
    last = cumv[Q - 1 : Q, :]
    fade = jnp.exp2(last - cumv)
    tail = fade * stepv
    tails = pack(tail)
    b_rows = bc[:, 0:N]
    d_b = dbc[:, 0:N]
    d_c = dbc[:, N : 2 * N]
    sums = jnp.zeros((Q, HL), f32)
    lasts = jnp.zeros((8, HL), f32)
    for c in range(0, DI, CH):
        cols = slice(c, c + CH)
        end = dloc[:, cols] + suf[0:1, cols] * total_of(inc, cols)
        end_low = end.astype(low)
        begin = sbf[:, cols]
        reach = nn(b_rows, end_low)
        held = [reach * xh[:, cols].astype(f32), fold8(end * begin.astype(f32))]
        held = gather_all(held, et[cols, :])
        sums, lasts = sums + held[0], lasts + held[1]
        d_b = d_b + nt(wx[:, cols], end_low)
        d_c = d_c + nt(gdy[:, cols], begin)
        conv_back(dx[:, cols] + spread(tails, e[:, cols]) * reach, c)
    conv_back(jnp.concatenate([d_b, d_c], axis=1), DI)

    flow = sums * tail
    d_cum = rs1[...] - stepv * rs2[...] - flow
    d_last = jnp.exp2(last) * jnp.sum(lasts, axis=0, keepdims=True)
    d_last = d_last + jnp.sum(flow, axis=0, keepdims=True)
    d_log = running_sum(d_cum, True) + d_last
    d_step = rs2[...] + sums * fade - d_log * par[2:3, :]
    d_dt = d_step * jax.nn.sigmoid(dtb[...])
    lane = lax.broadcasted_iota(jnp.int32, d_dt.shape, 1)
    d_dt = jnp.where(lane < H, d_dt, 0.0)
    dcv_o[:, CD:CW] = d_dt.astype(low)
    head_o[:, CD:CW] = jnp.zeros((8, HL), low)

    @pl.when(fresh)
    def keep():
        tail_o[:, CD:CW] = d_dt[Q - 16 :, :]
        for slot, ds in enumerate(slots):
            cols = slice(slot * HALF, (slot + 1) * HALF)
            total = jnp.zeros((16, HALF), f32)
            for k in range(KW):
                total = total + cw[k : k + 1, cols] * ds[pl.ds(zero + (Q - 5 - k), 16), :]
            tail_o[:, cols] = total

    hacc_o[0:8, :] += fold8(d_dt)
    hacc_o[8:16, :] += fold8(d_log * stepv)


def piece_at(me, place, which):
    return source_of(me, place) ^ which


def fold_lanes(value):
    total = value[:, 0:HALF]
    for c in range(HALF, value.shape[1], HALF):
        total = total + value[:, c : c + HALF]
    return total


def early_grad_kernel(scal, nrmt, dz, gn, db, wzc, wo, g0_o, g1_o, na_o, ga_o, part, wide):
    at = pl.program_id(0)

    @pl.when(at == 0)
    def start():
        na_o[...] = jnp.zeros_like(na_o)

    me = scal[0]
    refs = (g0_o, g1_o)
    quarter = DI // 4
    cols = pl.ds(pl.multiple_of(at * quarter, HALF), quarter)
    part[...] = nn(nrmt[...], dz[...])
    na_o[...] += fold_lanes(part[...] * wzc[...].astype(f32))
    for place in range(PIECES // 2):
        for which in range(2):
            start = pl.multiple_of(piece_at(me, place, which) * 24, 8)
            refs[which][place, 0, :, cols] = part[pl.ds(start, 24), :].astype(low)
    rows = pl.ds(pl.multiple_of(at * quarter, HALF), quarter)
    wide[rows, :] = tn(gn[...], db[...])
    ga_o[...] = fold_lanes(wide[rows, :] * wo[...].astype(f32))

    @pl.when(at == 3)
    def finish():
        for place in range(PIECES // 2):
            for which in range(2):
                start = pl.multiple_of(piece_at(me, place, which) * 48, 8)
                for half in range(2):
                    rows = pl.ds(start + 24 * half, 24)
                    span = slice(half * DI // 2, (half + 1) * DI // 2)
                    refs[which][place, 1, :, span] = wide[rows, :].astype(low)


def row_sums(value):
    ones = jnp.ones((8, value.shape[1]), low)
    total = 0.0
    for _ in range(3):
        top = value.astype(low)
        total = total + nt(ones, top)
        value = value - top.astype(f32)
    return total[0:1, :]


def late_grad_kernel(
    scal, nrmt, dcv, wc, na, tails, returned, cacc, hacc, kacc, ga, par, et,
    g0_o, g1_o, fix_o, vec_o, part, nl,
):
    at = pl.program_id(0)

    @pl.when(at == 0)
    def start():
        nl[...] = na[...]

    refs = (g0_o, g1_o)
    fix_o[...] = dcv[...]
    seqs = tails.shape[0]
    piece_len = dcv.shape[0] // seqs
    for seq in range(seqs):
        back = jnp.concatenate(
            [tails[seq, 0:8, :], tails[seq, 8:16, :] + returned[seq].astype(f32)], axis=0
        )
        fix_o[(seq + 1) * piece_len - 16 : (seq + 1) * piece_len, :] = back.astype(low)
    part[...] = nn(nrmt[...], fix_o[...])
    columns = at * fix_o.shape[1] + lax.broadcasted_iota(jnp.int32, (1, fix_o.shape[1]), 1)
    weight = jnp.where(columns < CD + H, wc[...].astype(f32), 0.0)
    nl[...] += fold_lanes(part[...] * weight)
    for place in range(PIECES // 2):
        for which in range(2):
            start = pl.multiple_of(piece_at(scal[0], place, which) * 24, 8)
            refs[which][place, :, :] = part[pl.ds(start, 24), :].astype(low)

    @pl.when(at == pl.num_programs(0) - 1)
    def finish():
        def put(first, row):
            for c in range(0, row.shape[1], HALF):
                vec_o[first + c // HALF : first + c // HALF + 1, :] = row[:, c : c + HALF]
            return first + row.shape[1] // HALF

        def column_sum(value):
            return jnp.sum(value, axis=0, keepdims=True)

        first = 0
        for k in range(KW + 1):
            first = put(first, column_sum(cacc[8 * k : 8 * k + 8, :]))
        first = put(first, row_sums(ga[...]))
        first = put(first, row_sums(nl[...]))
        first = put(first, column_sum(hacc[0:8, :]))
        first = put(first, -column_sum(hacc[8:16, :]) * par[2:3, :])
        first = put(first, column_sum(gather_heads(kacc[...], et[...])))
        vec_o[first:, :] = jnp.zeros((vec_o.shape[0] - first, HALF), f32)


def input_kernel(dcv, dz, wc, wz, x, cot, gain, past, token, gh_o, done_o, total):
    done_o[...] = jnp.zeros_like(done_o)
    total[...] = nt(dz[...], wz[...]) + nt(dcv[...], wc[...])
    width = x.shape[1]
    for r in range(0, Q, 16):
        rows = slice(r, r + 16)
        wide = x[rows, :].astype(f32)
        scale = lax.rsqrt(jnp.mean(wide * wide, axis=-1, keepdims=True) + epsilon)
        flow = total[rows, :]
        scaled = flow * gain[0:1, :]
        mean = jnp.sum(scaled * wide, axis=-1, keepdims=True) / width
        d_x = scale * scaled - wide * (scale * scale * scale * mean)
        gh_o[rows, :] = (cot[rows, :].astype(f32) + d_x).astype(low)


def call(kernel, grid, inputs, outputs, scratch, flops, name, aliases=None):
    in_specs = [spec for spec, _ in inputs]
    out_specs = [item[0] for item in outputs]
    out_shape = [
        pltpu.VMEM(item[1], item[2]) if len(item) > 3 else jax.ShapeDtypeStruct(item[1], item[2])
        for item in outputs
    ]
    moved = 1 if flops == 1.0 else sum(value.size * value.dtype.itemsize for _, value in inputs)
    return pl.pallas_call(
        kernel,
        grid=(grid,),
        in_specs=in_specs,
        out_specs=out_specs,
        out_shape=out_shape,
        scratch_shapes=scratch,
        input_output_aliases=aliases or {},
        cost_estimate=pl.CostEstimate(flops=int(flops), transcendentals=0, bytes_accessed=moved),
        compiler_params=pltpu.CompilerParams(
            dimension_semantics=("arbitrary",), vmem_limit_bytes=LIMITS[name] * 1024 * 1024
        ),
        name=name,
    )(*[value for _, value in inputs])


def near(value):
    return pltpu.with_memory_space_constraint(value, pltpu.VMEM)


def swap(value, mask):
    return lax.ppermute(value, axes, [(i, i ^ mask) for i in range(PIECES)])


def tie(value, *after):
    return lax.optimization_barrier((value,) + after)[0]


def along(value, masks):
    return jnp.stack([value] + [swap(value, mask) for mask in masks])


def ends_of(plane, value):
    flat = (PIECES // 2,) + value.shape
    return plane.reshape(flat), swap(plane, 1).reshape(flat)


def weave_first(first, second, rim):
    line = tie(along(first, (8, 16, 24)), rim)
    later = along(tie(second, line), (8, 16, 24))
    got = [tie(swap(line, mask), later) for mask in (2, 4, 6)]
    plane = jnp.stack([line] + got)
    return ends_of(plane, first), tie(later, plane)


def weave_second(line, value, token):
    got = [tie(swap(line, mask), token) for mask in (2, 4, 6)]
    plane = jnp.stack([line] + got)
    return ends_of(plane, value), plane


def parts_of(total):
    return total[0], [total[j].astype(low) for j in range(1, 4)]


def merge_core(kept, got):
    total = kept.astype(f32) + got.astype(f32)
    return parts_of(total.reshape((4, 4) + kept.shape[1:]))


def merge(keep, sends, masks, *after):
    got = [swap(value, mask) for value, mask in zip(sends, masks)]
    if after:
        got = lax.optimization_barrier((*got,) + after)[:3]
    got = [value.astype(f32) for value in got]
    return (keep + got[0]) + (got[1] + got[2])


def tie_all(keep, sends, *after):
    out = lax.optimization_barrier((keep, *sends) + after)
    return out[0], list(out[1:4])


def rounded(value):
    return value.astype(low).astype(f32)


def extras(taps, bias, gate, norm):
    left = jnp.concatenate([taps, bias[:, None, :]], axis=1)
    norm = jnp.pad(norm, ((0, 0), (0, gate.shape[1] - norm.shape[1])))
    right = jnp.stack([gate, norm], axis=1)
    left = jnp.pad(left, ((0, 0), (0, 24 - left.shape[1]), (0, 0)))
    right = jnp.pad(right, ((0, 0), (0, 24 - right.shape[1]), (0, 0)))
    return jnp.concatenate([left, right], axis=2)


def order_of_pieces():
    return [(j << 1) | (k << 3) for j in range(4) for k in range(4)]


def relay(ends, ends_low, totals, forward, fillers):
    count = lax.axis_size("seq")
    incoming = None
    results, arrivals, got = [], [], None
    for hop in range(1, count):
        value = ends_low
        if incoming is not None:
            value = (totals * incoming + ends).astype(low)
        route = [(hop - 1, hop)] if forward else [(count - hop, count - hop - 1)]
        arrived = lax.ppermute(value, "seq", route)
        if fillers:
            made = fillers.pop(0)(got)
            results.append(made)
            arrived = tie(arrived, made[-1])
        got = arrived
        arrivals.append(got)
        wide = got.astype(f32)
        incoming = wide if incoming is None else incoming + wide
    while fillers:
        results.append(fillers.pop(0)(got))
    return arrivals or [jnp.zeros_like(ends_low)], results


def total_of(refs, cols):
    total = refs[0][:, cols].astype(f32)
    for ref in refs[1:]:
        total = total + ref[:, cols].astype(f32)
    return total


def per_device(
    hidden,
    lengths,
    norm_gain,
    in_weight,
    conv_weight,
    conv_bias,
    step_bias,
    decay_log,
    skip_gain,
    gate_gain,
    out_weight,
    cotangent,
):
    seqs, piece_len, width = hidden.shape
    groups = piece_len // Q
    blocks = seqs * groups
    rows = seqs * piece_len
    devices = lax.axis_size(axes)
    quick = devices == PIECES
    place = lax.axis_index(axes).astype(jnp.int32)
    me = place if quick else jnp.zeros((), jnp.int32)
    seq_at = lax.axis_index("seq").astype(jnp.int32)
    scal = jnp.concatenate([me[None], seq_at[None], lengths.astype(jnp.int32), me[None] * 0])

    rims = hidden[:, piece_len - RIM :, :]
    seq_size = lax.axis_size("seq")
    rim_in = lax.ppermute(rims, "seq", [(i, i + 1) for i in range(seq_size - 1)])
    inner = hidden.reshape(seqs, groups, Q, width)[:, : groups - 1, Q - RIM :, :]
    halo = jnp.concatenate([rim_in[:, None], inner], axis=1).reshape(blocks, RIM, width)

    w_low = in_weight.astype(low)
    o_low = out_weight.astype(low)
    if quick:
        half = o_low.shape[0] // 2
        packed = jnp.concatenate([o_low[:half], o_low[half:]], axis=1)
        second = jnp.stack([w_low[:, :DI], packed])
        first = jnp.concatenate(
            [
                in_weight[:, DI:],
                extras(
                    conv_weight[None], conv_bias[None], gate_gain[None], norm_gain[None]
                )[0],
            ],
            axis=1,
        ).astype(low)
        (ca, cb_pieces), second_line = weave_first(first, second, rim_in)
        begin = tie(scal, second_line)
    else:
        begin = scal
        order = jnp.array(order_of_pieces(), jnp.int32)
        rows_w = lax.all_gather(w_low, axes, axis=0, tiled=True).reshape(PIECES, -1, E)
        full_taps = lax.all_gather(conv_weight.astype(low), axes, axis=1, tiled=True)
        full = [
            lax.all_gather(value.astype(low), axes, axis=0, tiled=True).reshape(PIECES, -1)
            for value in (conv_bias, gate_gain, norm_gain)
        ]
        extra = extras(full_taps.reshape(KW, PIECES, -1).transpose(1, 0, 2), *full)
        whole = jnp.concatenate([rows_w[:, :, DI:], extra], axis=2)
        ca, cb_pieces = whole[order], whole[order + 1]
        outs = lax.all_gather(o_low, axes, axis=0, tiled=True)
        outs = outs.reshape(PIECES, 2, -1, width).transpose(0, 2, 1, 3).reshape(PIECES, -1, DI)
        whole = jnp.stack([rows_w[:, :, :DI], outs], axis=1)
        za, zb = whole[order], whole[order + 1]

    rate = jnp.exp(decay_log)
    par = jnp.pad(
        jnp.stack([step_bias, rate * 1.4426950408889634, rate, skip_gain]), ((0, 4), (0, HL - H))
    )
    e = jnp.asarray(head_table(), low)
    et = jnp.asarray(np.pad(head_table()[: HL // 2].T, ((0, 0), (0, HL // 2))), low)
    t56 = onehot(HL, CD, H, CD // PIECES)
    t48 = onehot(HL, DI, 80, DI // PIECES)
    t24 = onehot(HL, width, 80, width // PIECES)

    def forth(i):
        return i

    def back(i):
        return (i // groups) * groups + groups - 1 - i % groups

    def tokens(cols, order):
        return pl.BlockSpec((Q, cols), lambda i: (order(i), 0))

    def per_block(height, cols, order):
        return pl.BlockSpec((None, height, cols), lambda i: (order(i), 0, 0))

    def per_seq(height, cols):
        return pl.BlockSpec((None, height, cols), lambda i: (i // groups, 0, 0))

    def fixed(*shape):
        zeros = (0,) * len(shape)
        return pl.BlockSpec(shape, lambda i: zeros, pipeline_mode=pl.Buffered(1))

    def kept(*shape):
        zeros = (0,) * len(shape)
        return pl.BlockSpec(shape, lambda i: zeros)

    scalars = pl.BlockSpec(memory_space=pltpu.SMEM)
    whole = pl.BlockSpec(memory_space=pltpu.VMEM)
    flat_hidden = hidden.reshape(rows, width)
    flat_cot = cotangent.reshape(rows, width)

    (nrm, nrmt, cie, sp, xh, xs, wx, bc, step, cum, dtb, cumt, sloc, pre, ends, ends_low, totals, wc, taps, gain_in, gain_gate) = call(
        functools.partial(conv_kernel, groups),
        blocks,
        [
            (scalars, begin),
            (tokens(width, forth), flat_hidden),
            (per_block(RIM, width, forth), halo),
            (fixed(*ca.shape), ca),
            (fixed(*ca.shape), cb_pieces),
            (fixed(HL, CD), t56),
            (fixed(HL, DI), t48),
            (fixed(HL, width), t24),
            (fixed(8, HL), par),
            (fixed(HL, DI), e),
        ],
        [
            (tokens(width, forth), (rows, width), low),
            (pl.BlockSpec((width, Q), lambda i: (0, i)), (width, rows), low),
            (per_block(Q + RIM, CD, forth), (blocks, Q + RIM, CD), low),
            (tokens(CD, forth), (rows, CD), f32),
            (tokens(DI, forth), (rows, DI), low),
            (tokens(DI, forth), (rows, DI), low),
            (tokens(DI, forth), (rows, DI), low),
            (tokens(2 * N, forth), (rows, 2 * N), low),
            (tokens(HL, forth), (rows, HL), f32),
            (tokens(HL, forth), (rows, HL), f32),
            (tokens(HL, forth), (rows, HL), f32),
            (per_block(H, Q, forth), (blocks, H, Q), f32),
            (per_block(N, DI, forth), (blocks, N, DI), f32),
            (per_block(8, DI, forth), (blocks, 8, DI), f32),
            (per_seq(N, DI), (seqs, N, DI), f32),
            (per_seq(N, DI), (seqs, N, DI), low),
            (per_seq(1, DI), (seqs, 1, DI), f32),
            (kept(width, CW), (width, CW), low),
            (kept(8, CD), (8, CD), f32),
            (kept(8, width), (8, width), f32),
            (kept(8, DI), (8, DI), f32),
        ],
        [
            pltpu.VMEM((Q + RIM, width), low),
            pltpu.VMEM((N, DI), f32),
            pltpu.VMEM((8, DI), f32),
            pltpu.VMEM((2, HL, HL), f32),
            *[pltpu.VMEM((Q + RIM, HALF), f32)] * (CD // HALF),
        ],
        2.0 * rows * width * CW,
        "conv",
    )
    if quick:
        (za, zb), token = weave_second(second_line, second, cum)
        bc_after = tie(bc, token)
    else:
        bc_after = bc

    def intra_part(got):
        return call(
            intra_kernel,
            blocks,
            [
                (tokens(2 * N, forth), bc_after),
                (tokens(DI, forth), xs),
                (tokens(HL, forth), cum),
                (per_block(H, Q, forth), cumt),
            ],
            [(tokens(DI, forth), (rows, DI), f32)],
            [pltpu.VMEM((Q, Q), f32)],
            2.0 * rows * Q * DI * 2,
            "intra",
        )

    def after(value, got):
        return value if got is None else tie(value, got)

    def project_part(got):
        return call(
            functools.partial(project_kernel, groups),
            blocks,
            [
                (scalars, after(scal, got)),
                (tokens(width, forth), nrm),
                (tokens(width, forth), flat_cot),
                (fixed(*za.shape), za),
                (fixed(*za.shape), zb),
            ],
            [
                (whole, (rows, DI), f32, near),
                (whole, (rows, DI), f32, near),
                (tokens(width, forth), (rows, width), low),
                (kept(width, DI), (width, DI), low),
                (kept(DI, width), (DI, width), low),
            ],
            [],
            4.0 * rows * width * DI,
            "project",
        )

    incoming, ((intra,), (z, dn, db, wz, wo)) = relay(
        ends, ends_low, totals, True, [intra_part, project_part]
    )

    (out, dz, dy, gdy, gn, sbf, rs1, dloc, suf, back_ends, back_ends_low, back_totals, kacc) = call(
        functools.partial(gate_kernel, groups, len(incoming)),
        blocks,
        [
            (scalars, scal),
            (tokens(DI, back), intra),
            (tokens(DI, back), xh),
            (tokens(2 * N, back), bc),
            (tokens(HL, back), cum),
            (per_block(N, DI, back), sloc),
            (per_block(8, DI, back), pre),
            *[(per_seq(N, DI), value) for value in incoming],
            (whole, near(z)),
            (whole, near(dn)),
            (tokens(width, back), flat_hidden),
            (fixed(DI, width), wo),
            (fixed(8, DI), gain_gate),
            (fixed(8, HL), par),
            (fixed(HL, DI), e),
            (fixed(DI, HL), et),
        ],
        [
            (tokens(width, back), (rows, width), low),
            (tokens(DI, back), (rows, DI), low),
            (tokens(DI, back), (rows, DI), low),
            (tokens(DI, back), (rows, DI), low),
            (tokens(DI, back), (rows, DI), low),
            (per_block(N, DI, back), (blocks, N, DI), low),
            (tokens(HL, back), (rows, HL), f32),
            (per_block(N, DI, back), (blocks, N, DI), f32),
            (per_block(8, DI, back), (blocks, 8, DI), f32),
            (per_seq(N, DI), (seqs, N, DI), f32),
            (per_seq(N, DI), (seqs, N, DI), low),
            (per_seq(1, DI), (seqs, 1, DI), f32),
            (kept(8, DI), (8, DI), f32),
        ],
        [
            pltpu.VMEM((Q, DI), f32),
            pltpu.VMEM((Q, DI), f32),
            pltpu.VMEM((Q, DI), f32),
            pltpu.VMEM((Q, DI), f32),
            pltpu.VMEM((Q, DI), f32),
            pltpu.VMEM((Q, DI), f32),
            pltpu.VMEM((N, DI), f32),
            pltpu.VMEM((8, DI), f32),
            pltpu.VMEM((8, DI), f32),
            pltpu.VMEM((8, DI), f32),
        ],
        4.0 * rows * width * DI,
        "gate",
    )

    def intra_back_part(got):
        return call(
            intra_back_kernel,
            blocks,
            [
                (tokens(2 * N, forth), after(bc, got)),
                (tokens(DI, forth), xs),
                (tokens(DI, forth), xh),
                (tokens(DI, forth), dy),
                (tokens(HL, forth), step),
                (tokens(HL, forth), cum),
                (per_block(H, Q, forth), cumt),
                (fixed(8, HL), par),
                (fixed(HL, DI), e),
                (fixed(DI, HL), et),
            ],
            [
                (tokens(DI, forth), (rows, DI), f32),
                (tokens(2 * N, forth), (rows, 2 * N), f32),
                (tokens(HL, forth), (rows, HL), f32),
            ],
            [pltpu.VMEM((Q, Q), f32), pltpu.VMEM((Q, Q), f32)],
            4.0 * rows * Q * DI * 2,
            "intra_back",
        )

    piece = (PIECES // 2, 2, width // PIECES, DI)

    def early_part(got):
        return call(
            early_grad_kernel,
            4,
            [
                (scalars, after(scal, got)),
                (fixed(width, rows), nrmt),
                (pl.BlockSpec((rows, DI // 4), lambda i: (0, i)), dz),
                (pl.BlockSpec((rows, DI // 4), lambda i: (0, i)), gn),
                (fixed(rows, width), db),
                (pl.BlockSpec((width, DI // 4), lambda i: (0, i)), wz),
                (pl.BlockSpec((DI // 4, width), lambda i: (i, 0)), wo),
            ],
            [
                (kept(*piece), piece, low),
                (kept(*piece), piece, low),
                (kept(width, HALF), (width, HALF), f32),
                (pl.BlockSpec((DI // 4, HALF), lambda i: (i, 0)), (DI, HALF), f32),
            ],
            [pltpu.VMEM((width, DI // 4), f32), pltpu.VMEM((DI, width), f32)],
            6.0 * rows * width * DI,
            "early_grad",
        )

    back_incoming, ((e0, e1, na, ga), (dx, dbc, rs2)) = relay(
        back_ends, back_ends_low, back_totals, False, [early_part, intra_back_part]
    )
    if quick:
        early = merge_core(e0, tie(swap(e1, 1), rs2))
        back_incoming[-1] = tie(back_incoming[-1], *early[1])

    (dcv, cacc, hacc, heads_out, tails_out) = call(
        functools.partial(conv_back_kernel, groups, len(back_incoming)),
        blocks,
        [
            (scalars, scal),
            (per_block(N, DI, back), dloc),
            (per_block(8, DI, back), suf),
            (per_block(N, DI, back), sbf),
            (tokens(DI, back), xh),
            (tokens(DI, back), wx),
            (tokens(DI, back), gdy),
            (tokens(DI, back), dx),
            (tokens(2 * N, back), dbc),
            (tokens(2 * N, back), bc),
            (tokens(HL, back), cum),
            (tokens(HL, back), step),
            (tokens(HL, back), dtb),
            (tokens(HL, back), rs1),
            (tokens(HL, back), rs2),
            *[(per_seq(N, DI), value) for value in back_incoming],
            (per_block(Q + RIM, CD, back), cie),
            (tokens(CD, back), sp),
            (fixed(8, CD), taps),
            (fixed(8, HL), par),
            (fixed(HL, DI), e),
            (fixed(DI, HL), et),
        ],
        [
            (tokens(CW, back), (rows, CW), low),
            (kept(8 * (KW + 1), CD), (8 * (KW + 1), CD), f32),
            (kept(16, HL), (16, HL), f32),
            (per_seq(8, CW), (seqs, 8, CW), low),
            (per_seq(16, CW), (seqs, 16, CW), f32),
        ],
        [
            pltpu.VMEM((8, CD), f32),
            *[pltpu.VMEM((Q + 16, HALF), f32)] * (CD // HALF),
        ],
        6.0 * rows * N * DI,
        "conv_back",
    )
    turn = scal
    if quick:
        early = parts_of(merge(*early, (2, 4, 6), hacc))
        turn = tie(scal, *early[1])
    returned = lax.ppermute(heads_out, "seq", [(i, i - 1) for i in range(1, seq_size)])

    late = (PIECES // 2, width // PIECES, CW)
    late_spec = pl.BlockSpec((PIECES // 2, width // PIECES, CW // 5), lambda i: (0, 0, i))
    (l0, l1, dcv, vector) = call(
        late_grad_kernel,
        5,
        [
            (scalars, turn),
            (fixed(width, rows), nrmt),
            (pl.BlockSpec((rows, CW // 5), lambda i: (0, i)), dcv),
            (pl.BlockSpec((width, CW // 5), lambda i: (0, i)), wc),
            (fixed(width, HALF), na),
            (pl.BlockSpec((seqs, 16, CW // 5), lambda i: (0, 0, i)), tails_out),
            (pl.BlockSpec((seqs, 8, CW // 5), lambda i: (0, 0, i)), returned),
            (fixed(8 * (KW + 1), CD), cacc),
            (fixed(16, HL), hacc),
            (fixed(8, DI), kacc),
            (fixed(DI, HALF), ga),
            (fixed(8, HL), par),
            (fixed(DI, HL), et),
        ],
        [
            (late_spec, late, low),
            (late_spec, late, low),
            (pl.BlockSpec((rows, CW // 5), lambda i: (0, i)), (rows, CW), low),
            (kept(96, HALF), (96, HALF), f32),
        ],
        [pltpu.VMEM((width, CW // 5), f32), pltpu.VMEM((width, HALF), f32)],
        2.0 * rows * width * CW,
        "late_grad",
    )

    def input_part(first, count, past, before, token):
        def order(i):
            return i + first

        return call(
            input_kernel,
            count,
            [
                (tokens(CW, order), dcv),
                (tokens(DI, order), dz),
                (fixed(width, CW), wc),
                (fixed(width, DI), wz),
                (tokens(width, order), flat_hidden),
                (tokens(width, order), flat_cot),
                (fixed(8, width), gain_in if token is None else tie(gain_in, *token)),
                (pl.BlockSpec(memory_space=pl.ANY), past),
                (pl.BlockSpec(memory_space=pl.ANY), before),
            ],
            [
                (tokens(width, order), (rows, width), low),
                (kept(8, HALF), (8, HALF), f32),
            ],
            [pltpu.VMEM((Q, width), f32)],
            1.0,
            "input",
            {7: 0} if first else None,
        )

    half_blocks = max(blocks // 4, 1)
    if quick:
        late_got = swap(l1, 1)
        vector_got = swap(vector, 1)
        gh, done = input_part(0, half_blocks, scal, scal, None)
        late_sum = merge_core(l0, tie(late_got, done))
        vector = vector + tie(vector_got, done)
        early = tie_all(*early, late_sum[1][0])
        gh, done2 = input_part(half_blocks, blocks - half_blocks, gh, done, late_sum[1])
        late_sum = parts_of(merge(*late_sum, (2, 4, 6), done2))
        early = merge(*early, (8, 16, 24), late_sum[1][0])
        late_sum = tie_all(*late_sum, early)
        vector = tie(vector, late_sum[1][0])
        got = [swap(vector, mask) for mask in (2, 4, 6)]
        vector = (vector + got[0]) + (got[1] + got[2])
    else:
        gh, done = input_part(0, blocks, scal, scal, None)

    if quick:
        got = [swap(vector, mask) for mask in (8, 16, 24)]
        vector = (vector + got[0]) + (got[1] + got[2])
        own_late = merge(*late_sum, (8, 16, 24))
        own_z, own_out = early[0], early[1]
        own_out = jnp.concatenate([own_out[:, : DI // 2], own_out[:, DI // 2 :]], axis=0)
    else:
        vector = lax.psum(vector, axes)
        order = jnp.array(order_of_pieces(), jnp.int32)
        inverse = jnp.argsort(jnp.concatenate([order, order + 1]))
        whole = jnp.concatenate([e0, e1])[inverse].astype(f32)
        outs = whole[:, 1].reshape(PIECES, -1, 2, width).transpose(0, 2, 1, 3).reshape(DI, width)
        own_z = lax.psum_scatter(
            whole[:, 0].reshape(width, DI), axes, scatter_dimension=0, tiled=True
        )
        own_out = lax.psum_scatter(outs, axes, scatter_dimension=0, tiled=True)
        whole = jnp.concatenate([l0, l1])[inverse].astype(f32).reshape(width, CW)
        own_late = lax.psum_scatter(whole, axes, scatter_dimension=0, tiled=True)

    def own(value, size, axis):
        return lax.dynamic_slice_in_dim(value, place * size, size, axis)

    tile = CD // HALF
    g_taps = own(vector[: KW * tile].reshape(KW, CD), CD // devices, 1)
    at = KW * tile
    g_bias = own(vector[at : at + tile].reshape(-1), CD // devices, 0)
    at += tile
    g_gate = own(vector[at : at + DI // HALF].reshape(-1), gate_gain.shape[0], 0)
    at += DI // HALF
    g_norm = own(vector[at : at + width // HALF].reshape(-1), norm_gain.shape[0], 0)
    at += width // HALF
    g_gate, g_norm = g_gate / rounded(gate_gain), g_norm / rounded(norm_gain)
    g_in = jnp.concatenate([own_z, own_late[:, : CD + H]], axis=1)
    return (
        out.reshape(hidden.shape),
        gh.reshape(hidden.shape),
        g_norm,
        g_in,
        g_taps,
        g_bias,
        vector[at, :H],
        vector[at + 1, :H],
        vector[at + 2, :H],
        g_gate,
        own_out,
    )


def solution(mesh):
    return jax.shard_map(
        per_device,
        mesh=mesh,
        in_specs=(
            P("dp", "seq", None),
            P("dp"),
            P(("dp", "seq")),
            P(("dp", "seq"), None),
            P(None, ("dp", "seq")),
            P(("dp", "seq")),
            P(),
            P(),
            P(),
            P(("dp", "seq")),
            P(("dp", "seq"), None),
            P("dp", "seq", None),
        ),
        out_specs=(
            P("dp", "seq", None),
            P("dp", "seq", None),
            P(("dp", "seq")),
            P(("dp", "seq"), None),
            P(None, ("dp", "seq")),
            P(("dp", "seq")),
            P(),
            P(),
            P(),
            P(("dp", "seq")),
            P(("dp", "seq"), None),
        ),
        check_vma=False,
    )
```

```python
import functools

import jax
import jax.numpy as jnp
import numpy as np
from jax import lax
from jax.experimental import pallas as pl
from jax.experimental.pallas import tpu as pltpu
from jax.sharding import PartitionSpec as P

H = 24
P_SIZE = 64
N = 128
KW = 4
Q = 256
E = 3352
DI = 1536
CD = 1792
HL = 128
CW = CD + HL
CH = 256
HALF = 128
RIM = 16
EARLY = 3
LATE = 3
PIECES = 32
NEG = -1e30
LIMITS = {
    "conv": 56,
    "intra": 56,
    "project": 48,
    "gate": 48,
    "early_grad": 56,
    "intra_back": 56,
    "conv_back": 56,
    "late_grad": 56,
    "input": 56,
}

epsilon = 1e-05
low = jnp.bfloat16
f32 = jnp.float32
axes = ("dp", "seq")


def onehot(rows, cols, first, period):
    table = np.zeros((rows, cols), np.float32)
    at = np.arange(cols)
    table[first + at % period, at] = 1.0
    return jnp.asarray(table, low)


def head_table():
    table = np.zeros((HL, DI), np.float32)
    at = np.arange(DI)
    table[at // P_SIZE, at] = 1.0
    table[HL // 2 + at // P_SIZE, at] = 1.0
    return table


def dot(left, right, dims):
    return lax.dot_general(left, right, (dims, ((), ())), preferred_element_type=f32)


def nn(left, right):
    return dot(left, right, ((1,), (0,)))


def nt(left, right):
    return dot(left, right, ((1,), (1,)))


def tn(left, right):
    return dot(left, right, ((0,), (0,)))


def pack(value):
    top = value.astype(low).astype(f32)
    rest = pltpu.roll(value - top, HL // 2, 1)
    lane = lax.broadcasted_iota(jnp.int32, value.shape, 1)
    return jnp.where(lane < HL // 2, top, rest).astype(low)


def spread(packed, table):
    return nn(packed, table)


def spread_all(packed, table):
    wide = nn(jnp.concatenate(packed, axis=0), table)
    parts, at = [], 0
    for value in packed:
        parts.append(wide[at : at + value.shape[0], :])
        at += value.shape[0]
    return parts


def gather_all(values, table):
    tops = [value.astype(low) for value in values]
    rests = [(value - top.astype(f32)).astype(low) for value, top in zip(values, tops)]
    parts = spread_all(tops + rests, table)
    return [parts[i] + parts[i + len(values)] for i in range(len(values))]


def gather_heads(value, table):
    return gather_all([value], table)[0]


def running_sum(value, reverse):
    rows = value.shape[0]
    at = lax.broadcasted_iota(jnp.int32, value.shape, 0)
    step = 1
    while step < rows:
        if reverse:
            value = value + jnp.where(at < rows - step, pltpu.roll(value, rows - step, 0), 0.0)
        else:
            value = value + jnp.where(at >= step, pltpu.roll(value, step, 0), 0.0)
        step *= 2
    return value


def softplus(value):
    tail = jnp.exp(-jnp.abs(value))
    series = tail * (1.0 - tail * (0.5 - tail * (1.0 / 3.0 - tail * (0.25 - tail * 0.2))))
    return jnp.maximum(value, 0.0) + jnp.where(tail < 0.03125, series, jnp.log(1.0 + tail))


def fold8(value):
    return jnp.sum(value.reshape(value.shape[0] // 8, 8, value.shape[1]), axis=0)


def pair_rows(me, own, other):
    first = (me & 1) == 0
    return jnp.concatenate([jnp.where(first, own, other), jnp.where(first, other, own)], axis=0)


def source_of(me, place):
    return me ^ ((place // 4) * 2) ^ ((place % 4) * 8)


def place_of(piece):
    return ((piece >> 1) & 3) * 4 + (piece >> 3)


def conv_kernel(
    groups, scal, x, halo, wa, wb, t56, t48, t24, par, e,
    nrm_o, nrmt_o, cie_o, sp_o, xh_o, xs_o, wx_o, bc_o, step_o, cum_o, dtb_o, cumt_o,
    sloc_o, pre_o, r_o, rl_o, tot_o, wc_o, taps_o, gain_o, gate_o,
    nrm, run, dec, small, wc_s, sem, *slots,
):
    block = pl.program_id(0)
    fresh = block % groups == 0
    zero = scal[scal.shape[0] - 1]

    @pl.when(block == 0)
    def assemble():
        me = scal[0]

        def one(place, carry):
            chip = source_of(me, place) >> 1
            own, other = wa[place].astype(f32), wb[place].astype(f32)
            wc_s[pl.ds(pl.multiple_of(chip * 48, 16), 48), :] = pair_rows(me, own, other).astype(low)
            rows = pl.ds(pl.multiple_of(place * 8, 8), 8)
            small[0, rows, :] = own[0:8, CD:CW]
            small[1, rows, :] = other[0:8, CD:CW]
            return carry

        lax.fori_loop(0, PIECES // 2, one, 0)
        pltpu.make_async_copy(wc_s, wc_o, sem).start()
        at = lax.broadcasted_iota(jnp.int32, (PIECES, 1), 0)
        slot = at & (PIECES // 2 - 1)
        ids = me ^ ((slot >> 2) << 1) ^ ((slot & 3) << 3) ^ (at >> 4)

        def row_of(k, table, size):
            pieces = [small[which, pl.ds(k, PIECES // 2, stride=8), :] for which in range(2)]
            wide = nn(jnp.concatenate(pieces, axis=0).astype(low), table)
            lane = lax.broadcasted_iota(jnp.int32, wide.shape, 1)
            inside = jnp.logical_and(lane >= ids * size, lane < (ids + 1) * size)
            return jnp.sum(jnp.where(inside, wide, 0.0), axis=0, keepdims=True)

        for k in range(KW + 1):
            taps_o[k : k + 1, :] = row_of(k, t56[...], CD // PIECES)
        gate_o[0:1, :] = row_of(0, t48[...], DI // PIECES)
        gain_o[0:1, :] = row_of(1, t24[...], gain_o.shape[1] // PIECES)

    def normed(rows):
        wide = rows.astype(f32)
        scale = lax.rsqrt(jnp.mean(wide * wide, axis=-1, keepdims=True) + epsilon)
        return (wide * scale * gain_o[0:1, :]).astype(low)

    nrm[0:RIM, :] = normed(halo[...])
    for r in range(0, Q, 32):
        nrm[RIM + r : RIM + r + 32, :] = normed(x[r : r + 32, :])
    nrm_o[...] = nrm[RIM:, :]
    nrmt_o[...] = nrm[RIM:, :].T

    for c in range(0, CD, CH):
        cols = slice(c, c + CH)
        conv_in = nn(nrm[...], wc_s[:, cols]).astype(low)
        cie_o[:, cols] = conv_in
        wide = conv_in.astype(f32)
        for side in range(2):
            span = slice(c + side * HALF, c + (side + 1) * HALF)
            cs = slots[c // HALF + side]
            cs[...] = wide[:, side * HALF : (side + 1) * HALF]
            for r in range(0, Q, 64):
                taps = taps_o[0:1, span] * cs[pl.ds(zero + (RIM - 3 + r), 64), :]
                for k in range(1, KW):
                    taps = taps + taps_o[k : k + 1, span] * cs[pl.ds(zero + (RIM - 3 + k + r), 64), :]
                pre = taps_o[KW : KW + 1, span] + taps
                sig = jax.nn.sigmoid(pre)
                act = (pre * sig).astype(low)
                sp_o[r : r + 64, span] = sig * (1.0 + pre * (1.0 - sig))
                if c < DI:
                    xh_o[r : r + 64, span] = act
                else:
                    bc_o[r : r + 64, side * HALF : (side + 1) * HALF] = act

    dtb = nn(nrm[RIM:, :], wc_s[:, CD:CW]) + par[0:1, :]
    step = softplus(dtb)
    cum = running_sum(-step * par[1:2, :], False)
    step_o[...] = step
    cum_o[...] = cum
    dtb_o[...] = dtb
    cumt_o[...] = cum.T[0:H, :]
    last = cum[Q - 1 : Q, :]
    steps = pack(step)
    tails = pack(jnp.exp2(last - cum) * step)
    decays = pack(jnp.broadcast_to(jnp.exp2(last), (8, HL)))
    for c in range(0, DI, CH):
        cols = slice(c, c + CH)
        table = e[:, cols]
        wide = xh_o[:, cols].astype(f32)
        xs_o[:, cols] = (spread(steps, table) * wide).astype(low)
        tail_e, decay = spread_all([tails, decays], table)
        weighted = (tail_e * wide).astype(low)
        wx_o[:, cols] = weighted
        local = tn(bc_o[:, 0:N], weighted)
        before = jnp.where(fresh, 0.0, run[:, cols])
        sloc_o[:, cols] = before
        after = decay[0:1, :] * before + local
        run[:, cols] = after
        r_o[:, cols] = after
        rl_o[:, cols] = after.astype(low)
        product = jnp.where(fresh, 1.0, dec[:, cols])
        pre_o[:, cols] = product
        product = product * decay
        dec[:, cols] = product
        tot_o[:, cols] = product[0:1, :]

    @pl.when(block == pl.num_programs(0) - 1)
    def finish():
        pltpu.make_async_copy(wc_s, wc_o, sem).wait()


def block_rows(block):
    return pl.ds(pl.multiple_of(block * Q, Q), Q)


def intra_kernel(bc, xs, cum, cumt, o, sc):
    sc[...] = nt(bc[:, N : 2 * N], bc[:, 0:N])
    at = lax.broadcasted_iota(jnp.int32, (HALF, HALF), 0)
    to = lax.broadcasted_iota(jnp.int32, (HALF, HALF), 1)
    lower = at >= to
    left = lax.broadcasted_iota(jnp.int32, (HALF, HALF), 1) < P_SIZE
    for pair in range(H // 2):
        cols = slice(pair * HALF, (pair + 1) * HALF)
        x_pair = xs[:, cols]
        m00, m10, m11 = [], [], []
        for h in (2 * pair, 2 * pair + 1):
            row = cumt[h : h + 1, :]
            upper_col, lower_col = cum[0:HALF, h : h + 1], cum[HALF:, h : h + 1]
            l00 = jnp.exp2(jnp.where(lower, upper_col - row[:, 0:HALF], NEG))
            m00.append((sc[0:HALF, 0:HALF] * l00).astype(low))
            l10 = jnp.exp2(lower_col - row[:, 0:HALF])
            m10.append((sc[HALF:, 0:HALF] * l10).astype(low))
            l11 = jnp.exp2(jnp.where(lower, lower_col - row[:, HALF:], NEG))
            m11.append((sc[HALF:, HALF:] * l11).astype(low))
        top = nn(jnp.concatenate(m00, axis=0), x_pair[0:HALF, :])
        sides = [jnp.concatenate([m10[i], m11[i]], axis=1) for i in range(2)]
        bottom = nn(jnp.concatenate(sides, axis=0), x_pair)
        o[0:HALF, cols] = jnp.where(left, top[0:HALF, :], top[HALF:, :])
        o[HALF:, cols] = jnp.where(left, bottom[0:HALF, :], bottom[HALF:, :])


def valid_column(scal, groups, block):
    seq, group = block // groups, block % groups
    at = scal[1] * (groups * Q) + group * Q + lax.broadcasted_iota(jnp.int32, (Q, 1), 0)
    return (at < scal[2 + seq]).astype(f32)


def project_kernel(
    groups, scal, nrm, cot, wa, wb, z_all, dn_all, db_o, wz_o, wo_o, wz_s, wo_s, sems
):
    block = pl.program_id(0)
    z_o, dn_o = z_all.at[block_rows(block), :], dn_all.at[block_rows(block), :]

    copies = [
        pltpu.make_async_copy(wz_s, wz_o, sems.at[0]),
        pltpu.make_async_copy(wo_s, wo_o, sems.at[1]),
    ]

    @pl.when(block == 0)
    def assemble():
        me = scal[0]

        def halves(packed):
            return jnp.concatenate([packed[:, 0 : DI // 2], packed[:, DI // 2 :]], axis=0)

        def one(place, carry):
            chip = source_of(me, place) >> 1
            own, other = wa[place, 0].astype(f32), wb[place, 0].astype(f32)
            wz_s[pl.ds(pl.multiple_of(chip * 48, 16), 48), :] = pair_rows(me, own, other).astype(low)
            own, other = halves(wa[place, 1].astype(f32)), halves(wb[place, 1].astype(f32))
            wo_s[pl.ds(pl.multiple_of(chip * 96, 16), 96), :] = pair_rows(me, own, other).astype(low)
            return carry

        lax.fori_loop(0, PIECES // 2, one, 0)
        for copy in copies:
            copy.start()

    db_o[...] = (cot[...].astype(f32) * valid_column(scal, groups, block)).astype(low)
    for c in range(0, DI, CH):
        z_o[:, c : c + CH] = nn(nrm[...], wz_s[:, c : c + CH])
        dn_o[:, c : c + CH] = nt(db_o[...], wo_s[c : c + CH, :])

    @pl.when(block == pl.num_programs(0) - 1)
    def finish():
        for copy in copies:
            copy.wait()


def gate_kernel(
    groups, hops, scal, intra, xh, bc, cum, sloc, pre, *refs
):
    inc = refs[:hops]
    z_all, dn_all, hid, wo, gg, par, e, et = refs[hops : hops + 8]
    (
        out_o, dz_o, dy_o, gdy_o, gn_o, sbf_o, rs_o, dloc_o, suf_o, rd_o, rdl_o, tot_o, kacc_o,
        yi_s, ge_s, pr_s, y_s, sg_s, gt_s, run, dec, skip, fall,
    ) = refs[hops + 8 :]
    at = pl.program_id(0)
    fresh = at % groups == 0
    block = (at // groups) * groups + groups - 1 - at % groups
    here = block_rows(block)
    z, dn = z_all.at[here, :], dn_all.at[here, :]

    @pl.when(at == 0)
    def start():
        kacc_o[...] = jnp.zeros_like(kacc_o)

    c_rows = bc[:, N : 2 * N]
    growth = pack(jnp.exp2(cum[...]))
    params = pack(par[...])
    decays = pack(jnp.broadcast_to(jnp.exp2(cum[Q - 1 : Q, :]), (8, HL)))
    for c in range(0, DI, CH):
        cols = slice(c, c + CH)
        begin = (sloc[:, cols] + pre[0:1, cols] * total_of(inc, cols)).astype(low)
        sbf_o[:, cols] = begin
        wide, skip[:, cols], fall[:, cols] = spread_all([growth, params, decays], e[:, cols])
        ge_s[:, cols] = wide
        yi_s[:, cols] = intra[:, cols] + wide * nn(c_rows, begin)

    def body(r):
        rows = slice(r, r + 32)
        squares = jnp.zeros((32, HALF), f32)
        crosses = jnp.zeros((32, HALF), f32)
        for c in range(0, DI, HALF):
            cols = slice(c, c + HALF)
            zv = z[rows, cols]
            y = yi_s[rows, cols] + skip[3:4, cols] * xh[rows, cols].astype(f32)
            sig = jax.nn.sigmoid(zv)
            gated = y * (zv * sig)
            squares = squares + gated * gated
            crosses = crosses + (dn[rows, cols] * gg[0:1, cols]) * gated
            y_s[rows, cols] = y
            sg_s[rows, cols] = sig
            gt_s[rows, cols] = gated
        scale = lax.rsqrt(jnp.sum(squares, axis=1, keepdims=True) / DI + epsilon)
        shift = scale * scale * scale * (jnp.sum(crosses, axis=1, keepdims=True) / DI)
        for c in range(0, DI, HALF):
            cols = slice(c, c + HALF)
            zv, y, sig, gated = z[rows, cols], y_s[rows, cols], sg_s[rows, cols], gt_s[rows, cols]
            gained = gg[0:1, cols]
            gn_o[rows, cols] = (gated * scale * gained).astype(low)
            d_gated = scale * (dn[rows, cols] * gained) - gated * shift
            d_sig = d_gated * sig
            d_wide = d_sig * zv
            dz_o[rows, cols] = (y * (d_sig + d_wide * (1.0 - sig))).astype(low)
            d_low = d_wide.astype(low)
            dy_o[rows, cols] = d_low
            d_y = d_low.astype(f32)
            kacc_o[:, cols] += fold8(d_y * xh[rows, cols].astype(f32))
            gdy_o[rows, cols] = (ge_s[rows, cols] * d_y).astype(low)
            pr_s[rows, cols] = d_y * yi_s[rows, cols]

    for r in range(0, Q, 32):
        body(r)

    valid = valid_column(scal, groups, block)
    for c in range(0, DI // 2, CH):
        branch = nn(gn_o[...], wo[:, c : c + CH])
        out_o[:, c : c + CH] = (hid[:, c : c + CH].astype(f32) + valid * branch).astype(low)
    sums = jnp.zeros((Q, HL), f32)
    for c in range(0, DI, CH):
        cols = slice(c, c + CH)
        sums = sums + gather_heads(pr_s[:, cols], et[cols, :])
        decay = fall[:, cols]
        before = jnp.where(fresh, 0.0, run[:, cols])
        dloc_o[:, cols] = before
        after = decay[0:1, :] * before + tn(c_rows, gdy_o[:, cols])
        run[:, cols] = after
        rd_o[:, cols] = after
        rdl_o[:, cols] = after.astype(low)
        product = jnp.where(fresh, 1.0, dec[:, cols])
        suf_o[:, cols] = product
        product = product * decay
        dec[:, cols] = product
        tot_o[:, cols] = product[0:1, :]
    rs_o[...] = sums


def intra_back_kernel(bc, xs, xh, dy, step, cum, cumt, par, e, et, dx_o, dbc_o, rs_o, sc, acc):
    sc[...] = nt(bc[:, 0:N], bc[:, N : 2 * N])
    acc[...] = jnp.zeros_like(acc)
    at = lax.broadcasted_iota(jnp.int32, (HALF, HALF), 0)
    to = lax.broadcasted_iota(jnp.int32, (HALF, HALF), 1)
    upper = at <= to
    left = lax.broadcasted_iota(jnp.int32, (Q, HALF), 1) < P_SIZE
    steps = pack(step[...])
    params = pack(par[...])
    sums = jnp.zeros((Q, HL), f32)
    for quad in range(H // 4):
        flows = []
        for pair in (2 * quad, 2 * quad + 1):
            cols = slice(pair * HALF, (pair + 1) * HALF)
            dy_pair = dy[:, cols]
            x_pair = xs[:, cols]
            heads = (2 * pair, 2 * pair + 1)
            zeros = jnp.zeros_like(x_pair)
            x_a, x_b = jnp.where(left, x_pair, zeros), jnp.where(left, zeros, x_pair)
            rows = [cumt[h : h + 1, :] for h in heads]
            x_top = jnp.concatenate([x_a[0:HALF, :], x_b[0:HALF, :]], axis=0)
            grown = nt(x_top, dy_pair)
            m00, m01, m11 = [], [], []
            total = 0.0
            for i, h in enumerate(heads):
                first_col = cum[0:HALF, h : h + 1]
                l00 = jnp.exp2(jnp.where(upper, rows[i][:, 0:HALF] - first_col, NEG))
                m00.append((sc[0:HALF, 0:HALF] * l00).astype(low))
                total = total + grown[i * HALF : (i + 1) * HALF, 0:HALF] * l00
            acc[0:HALF, 0:HALF] += total
            total = 0.0
            for i, h in enumerate(heads):
                first_col = cum[0:HALF, h : h + 1]
                l01 = jnp.exp2(rows[i][:, HALF:] - first_col)
                m01.append((sc[0:HALF, HALF:] * l01).astype(low))
                total = total + grown[i * HALF : (i + 1) * HALF, HALF:] * l01
            acc[0:HALF, HALF:] += total
            sides = [jnp.concatenate([m00[i], m01[i]], axis=1) for i in range(2)]
            top = nn(jnp.concatenate(sides, axis=0), dy_pair)
            x_bottom = jnp.concatenate([x_a[HALF:, :], x_b[HALF:, :]], axis=0)
            grown = nt(x_bottom, dy_pair[HALF:, :])
            total = 0.0
            for i, h in enumerate(heads):
                second_col = cum[HALF:, h : h + 1]
                l11 = jnp.exp2(jnp.where(upper, rows[i][:, HALF:] - second_col, NEG))
                m11.append((sc[HALF:, HALF:] * l11).astype(low))
                total = total + grown[i * HALF : (i + 1) * HALF, :] * l11
            acc[HALF:, HALF:] += total
            bottom = nn(jnp.concatenate(m11, axis=0), dy_pair[HALF:, :])
            half_left = left[0:HALF]
            flows.append(
                jnp.concatenate(
                    [
                        jnp.where(half_left, top[0:HALF, :], top[HALF:, :]),
                        jnp.where(half_left, bottom[0:HALF, :], bottom[HALF:, :]),
                    ],
                    axis=0,
                )
            )
        cols = slice(quad * CH, (quad + 1) * CH)
        flow = jnp.concatenate(flows, axis=1)
        sums = sums + gather_heads(flow * xh[:, cols].astype(f32), et[cols, :])
        step_e, skip = spread_all([steps, params], e[:, cols])
        dx_o[:, cols] = step_e * flow + skip[3:4, :] * dy[:, cols].astype(f32)
    rs_o[...] = sums
    scores = acc[...].astype(low)
    dbc_o[:, 0:N] = nn(scores, bc[:, N : 2 * N])
    dbc_o[:, N : 2 * N] = tn(scores, bc[:, 0:N])


def conv_back_kernel(
    groups, hops, scal, dloc, suf, sbf, xh, wx, gdy, dx, dbc, bc, cum, step, dtb, rs1, rs2, *refs
):
    inc = refs[:hops]
    cie, sp, cw, par, e, et, dcv_o, kacc_o, hacc_o, head_o, tail_o, nxt, *slots = refs[hops:]
    at = pl.program_id(0)
    fresh = at % groups == 0
    opening = at % groups == groups - 1
    zero = scal[scal.shape[0] - 1]

    @pl.when(at == 0)
    def start():
        kacc_o[...] = jnp.zeros_like(kacc_o)
        hacc_o[...] = jnp.zeros_like(hacc_o)

    def conv_back(flow, c):
        for side in range(2):
            half_back(flow[:, side * HALF : (side + 1) * HALF], c + side * HALF)

    def half_back(flow, c):
        ds = slots[c // HALF]
        cols = slice(c, c + HALF)
        ds[0:8, :] = jnp.zeros((8, HALF), f32)
        ds[8 + Q :, :] = jnp.where(fresh, 0.0, nxt[:, cols])
        ds[8 : 8 + Q, :] = flow * sp[:, cols]
        nxt[:, cols] = ds[8:16, :]
        taps = [cw[k : k + 1, cols] for k in range(KW)]
        sums = [jnp.zeros((8, HALF), f32) for _ in range(KW + 1)]

        def views_at(begin, count):
            return [ds[pl.ds(zero + (begin + 11 - k), count), :] for k in range(KW)]

        def back(views):
            total = taps[0] * views[0]
            for k in range(1, KW):
                total = total + taps[k] * views[k]
            return total

        for r in range(0, Q, 64):
            views = views_at(r, 64)
            dcv_o[r : r + 64, cols] = back(views).astype(low)
            conv_in = cie[RIM + r : RIM + r + 64, cols].astype(f32)
            for k in range(KW):
                sums[k] = sums[k] + fold8(views[k] * conv_in)
            sums[KW] = sums[KW] + fold8(views[KW - 1])
        views = views_at(-8, 8)
        head_o[:, cols] = back(views).astype(low)
        conv_in = cie[0:RIM, cols].astype(f32)[8:16, :]
        for k in range(KW):
            kacc_o[8 * k : 8 * k + 8, cols] += sums[k] + jnp.where(opening, views[k] * conv_in, 0.0)
        kacc_o[8 * KW : 8 * KW + 8, cols] += sums[KW]

    cumv = cum[...]
    stepv = step[...]
    last = cumv[Q - 1 : Q, :]
    fade = jnp.exp2(last - cumv)
    tail = fade * stepv
    tails = pack(tail)
    b_rows = bc[:, 0:N]
    d_b = dbc[:, 0:N]
    d_c = dbc[:, N : 2 * N]
    sums = jnp.zeros((Q, HL), f32)
    lasts = jnp.zeros((8, HL), f32)
    for c in range(0, DI, CH):
        cols = slice(c, c + CH)
        end = dloc[:, cols] + suf[0:1, cols] * total_of(inc, cols)
        end_low = end.astype(low)
        begin = sbf[:, cols]
        reach = nn(b_rows, end_low)
        held = [reach * xh[:, cols].astype(f32), fold8(end * begin.astype(f32))]
        held = gather_all(held, et[cols, :])
        sums, lasts = sums + held[0], lasts + held[1]
        d_b = d_b + nt(wx[:, cols], end_low)
        d_c = d_c + nt(gdy[:, cols], begin)
        conv_back(dx[:, cols] + spread(tails, e[:, cols]) * reach, c)
    conv_back(jnp.concatenate([d_b, d_c], axis=1), DI)

    flow = sums * tail
    d_cum = rs1[...] - stepv * rs2[...] - flow
    d_last = jnp.exp2(last) * jnp.sum(lasts, axis=0, keepdims=True)
    d_last = d_last + jnp.sum(flow, axis=0, keepdims=True)
    d_log = running_sum(d_cum, True) + d_last
    d_step = rs2[...] + sums * fade - d_log * par[2:3, :]
    d_dt = d_step * jax.nn.sigmoid(dtb[...])
    lane = lax.broadcasted_iota(jnp.int32, d_dt.shape, 1)
    d_dt = jnp.where(lane < H, d_dt, 0.0)
    dcv_o[:, CD:CW] = d_dt.astype(low)
    head_o[:, CD:CW] = jnp.zeros((8, HL), low)

    @pl.when(fresh)
    def keep():
        tail_o[:, CD:CW] = d_dt[Q - 16 :, :]
        for slot, ds in enumerate(slots):
            cols = slice(slot * HALF, (slot + 1) * HALF)
            total = jnp.zeros((16, HALF), f32)
            for k in range(KW):
                total = total + cw[k : k + 1, cols] * ds[pl.ds(zero + (Q - 5 - k), 16), :]
            tail_o[:, cols] = total

    hacc_o[0:8, :] += fold8(d_dt)
    hacc_o[8:16, :] += fold8(d_log * stepv)


def piece_at(me, place, which):
    return source_of(me, place) ^ which


def fold_lanes(value):
    total = value[:, 0:HALF]
    for c in range(HALF, value.shape[1], HALF):
        total = total + value[:, c : c + HALF]
    return total


def early_grad_kernel(scal, nrmt, dz, gn, db, wzc, wo, g0_o, g1_o, na_o, ga_o, part, wide):
    at = pl.program_id(0)

    @pl.when(at == 0)
    def start():
        na_o[...] = jnp.zeros_like(na_o)

    me = scal[0]
    refs = (g0_o, g1_o)
    quarter = DI // EARLY
    cols = pl.ds(pl.multiple_of(at * quarter, HALF), quarter)
    part[...] = nn(nrmt[...], dz[...])
    na_o[...] += fold_lanes(part[...] * wzc[...].astype(f32))
    for place in range(PIECES // 2):
        for which in range(2):
            start = pl.multiple_of(piece_at(me, place, which) * 24, 8)
            refs[which][place, 0, :, cols] = part[pl.ds(start, 24), :].astype(low)
    rows = pl.ds(pl.multiple_of(at * quarter, HALF), quarter)
    wide[rows, :] = tn(gn[...], db[...])
    ga_o[...] = fold_lanes(wide[rows, :] * wo[...].astype(f32))

    @pl.when(at == EARLY - 1)
    def finish():
        for place in range(PIECES // 2):
            for which in range(2):
                start = pl.multiple_of(piece_at(me, place, which) * 48, 8)
                for half in range(2):
                    rows = pl.ds(start + 24 * half, 24)
                    span = slice(half * DI // 2, (half + 1) * DI // 2)
                    refs[which][place, 1, :, span] = wide[rows, :].astype(low)


def row_sums(value):
    ones = jnp.ones((8, value.shape[1]), low)
    total = 0.0
    for _ in range(3):
        top = value.astype(low)
        total = total + nt(ones, top)
        value = value - top.astype(f32)
    return total[0:1, :]


def late_grad_kernel(
    scal, nrmt, dcv, wc, na, tails, returned, cacc, hacc, kacc, ga, par, et,
    g0_o, g1_o, fix_o, vec_o, part, nl,
):
    at = pl.program_id(0)

    @pl.when(at == 0)
    def start():
        nl[...] = na[...]

    refs = (g0_o, g1_o)
    fix_o[...] = dcv[...]
    seqs = tails.shape[0]
    piece_len = dcv.shape[0] // seqs
    for seq in range(seqs):
        back = jnp.concatenate(
            [tails[seq, 0:8, :], tails[seq, 8:16, :] + returned[seq].astype(f32)], axis=0
        )
        fix_o[(seq + 1) * piece_len - 16 : (seq + 1) * piece_len, :] = back.astype(low)
    part[...] = nn(nrmt[...], fix_o[...])
    columns = at * fix_o.shape[1] + lax.broadcasted_iota(jnp.int32, (1, fix_o.shape[1]), 1)
    weight = jnp.where(columns < CD + H, wc[...].astype(f32), 0.0)
    nl[...] += fold_lanes(part[...] * weight)
    for place in range(PIECES // 2):
        for which in range(2):
            start = pl.multiple_of(piece_at(scal[0], place, which) * 24, 8)
            refs[which][place, :, :] = part[pl.ds(start, 24), :].astype(low)

    @pl.when(at == pl.num_programs(0) - 1)
    def finish():
        def put(first, row):
            for c in range(0, row.shape[1], HALF):
                vec_o[first + c // HALF : first + c // HALF + 1, :] = row[:, c : c + HALF]
            return first + row.shape[1] // HALF

        def column_sum(value):
            return jnp.sum(value, axis=0, keepdims=True)

        first = 0
        for k in range(KW + 1):
            first = put(first, column_sum(cacc[8 * k : 8 * k + 8, :]))
        first = put(first, row_sums(ga[...]))
        first = put(first, row_sums(nl[...]))
        first = put(first, column_sum(hacc[0:8, :]))
        first = put(first, -column_sum(hacc[8:16, :]) * par[2:3, :])
        first = put(first, column_sum(gather_heads(kacc[...], et[...])))
        vec_o[first:, :] = jnp.zeros((vec_o.shape[0] - first, HALF), f32)


def input_kernel(dcv, dz, wc, wz, x, cot, gain, past, token, gh_o, done_o, total):
    done_o[...] = jnp.zeros_like(done_o)
    total[...] = nt(dz[...], wz[...]) + nt(dcv[...], wc[...])
    width = x.shape[1]
    for r in range(0, Q, 16):
        rows = slice(r, r + 16)
        wide = x[rows, :].astype(f32)
        scale = lax.rsqrt(jnp.mean(wide * wide, axis=-1, keepdims=True) + epsilon)
        flow = total[rows, :]
        scaled = flow * gain[0:1, :]
        mean = jnp.sum(scaled * wide, axis=-1, keepdims=True) / width
        d_x = scale * scaled - wide * (scale * scale * scale * mean)
        gh_o[rows, :] = (cot[rows, :].astype(f32) + d_x).astype(low)


def call(kernel, grid, inputs, outputs, scratch, flops, name, aliases=None):
    in_specs = [spec for spec, _ in inputs]
    out_specs = [item[0] for item in outputs]
    out_shape = [
        pltpu.VMEM(item[1], item[2]) if len(item) > 3 else jax.ShapeDtypeStruct(item[1], item[2])
        for item in outputs
    ]
    moved = 1 if flops == 1.0 else sum(value.size * value.dtype.itemsize for _, value in inputs)
    return pl.pallas_call(
        kernel,
        grid=(grid,),
        in_specs=in_specs,
        out_specs=out_specs,
        out_shape=out_shape,
        scratch_shapes=scratch,
        input_output_aliases=aliases or {},
        cost_estimate=pl.CostEstimate(flops=int(flops), transcendentals=0, bytes_accessed=moved),
        compiler_params=pltpu.CompilerParams(
            dimension_semantics=("arbitrary",), vmem_limit_bytes=LIMITS[name] * 1024 * 1024
        ),
        name=name,
    )(*[value for _, value in inputs])


def near(value):
    return pltpu.with_memory_space_constraint(value, pltpu.VMEM)


def swap(value, mask):
    return lax.ppermute(value, axes, [(i, i ^ mask) for i in range(PIECES)])


def tie(value, *after):
    return lax.optimization_barrier((value,) + after)[0]


def along(value, masks):
    return jnp.stack([value] + [swap(value, mask) for mask in masks])


def ends_of(plane, value):
    flat = (PIECES // 2,) + value.shape
    return plane.reshape(flat), swap(plane, 1).reshape(flat)


def weave_first(first, second, rim):
    line = tie(along(first, (8, 16, 24)), rim)
    later = along(tie(second, line), (8, 16, 24))
    got = [tie(swap(line, mask), later) for mask in (2, 4, 6)]
    plane = jnp.stack([line] + got)
    return ends_of(plane, first), tie(later, plane)


def weave_second(line, value, token):
    got = [tie(swap(line, mask), token) for mask in (2, 4, 6)]
    plane = jnp.stack([line] + got)
    return ends_of(plane, value), plane


def parts_of(total):
    return total[0], [total[j].astype(low) for j in range(1, 4)]


def merge_core(kept, got):
    total = kept.astype(f32) + got.astype(f32)
    return parts_of(total.reshape((4, 4) + kept.shape[1:]))


def merge(keep, sends, masks, *after):
    got = [swap(value, mask) for value, mask in zip(sends, masks)]
    if after:
        got = lax.optimization_barrier((*got,) + after)[:3]
    got = [value.astype(f32) for value in got]
    return (keep + got[0]) + (got[1] + got[2])


def tie_all(keep, sends, *after):
    out = lax.optimization_barrier((keep, *sends) + after)
    return out[0], list(out[1:4])


def rounded(value):
    return value.astype(low).astype(f32)


def extras(taps, bias, gate, norm):
    left = jnp.concatenate([taps, bias[:, None, :]], axis=1)
    norm = jnp.pad(norm, ((0, 0), (0, gate.shape[1] - norm.shape[1])))
    right = jnp.stack([gate, norm], axis=1)
    left = jnp.pad(left, ((0, 0), (0, 24 - left.shape[1]), (0, 0)))
    right = jnp.pad(right, ((0, 0), (0, 24 - right.shape[1]), (0, 0)))
    return jnp.concatenate([left, right], axis=2)


def order_of_pieces():
    return [(j << 1) | (k << 3) for j in range(4) for k in range(4)]


def relay(ends, ends_low, totals, forward, fillers):
    count = lax.axis_size("seq")
    incoming = None
    results, arrivals, got = [], [], None
    for hop in range(1, count):
        value = ends_low
        if incoming is not None:
            value = (totals * incoming + ends).astype(low)
        route = [(hop - 1, hop)] if forward else [(count - hop, count - hop - 1)]
        arrived = lax.ppermute(value, "seq", route)
        if fillers:
            made = fillers.pop(0)(got)
            results.append(made)
            arrived = tie(arrived, made[-1])
        got = arrived
        arrivals.append(got)
        wide = got.astype(f32)
        incoming = wide if incoming is None else incoming + wide
    while fillers:
        results.append(fillers.pop(0)(got))
    return arrivals or [jnp.zeros_like(ends_low)], results


def total_of(refs, cols):
    total = refs[0][:, cols].astype(f32)
    for ref in refs[1:]:
        total = total + ref[:, cols].astype(f32)
    return total


def per_device(
    hidden,
    lengths,
    norm_gain,
    in_weight,
    conv_weight,
    conv_bias,
    step_bias,
    decay_log,
    skip_gain,
    gate_gain,
    out_weight,
    cotangent,
):
    seqs, piece_len, width = hidden.shape
    groups = piece_len // Q
    blocks = seqs * groups
    rows = seqs * piece_len
    devices = lax.axis_size(axes)
    quick = devices == PIECES
    place = lax.axis_index(axes).astype(jnp.int32)
    me = place if quick else jnp.zeros((), jnp.int32)
    seq_at = lax.axis_index("seq").astype(jnp.int32)
    scal = jnp.concatenate([me[None], seq_at[None], lengths.astype(jnp.int32), me[None] * 0])

    rims = hidden[:, piece_len - RIM :, :]
    seq_size = lax.axis_size("seq")
    rim_in = lax.ppermute(rims, "seq", [(i, i + 1) for i in range(seq_size - 1)])
    inner = hidden.reshape(seqs, groups, Q, width)[:, : groups - 1, Q - RIM :, :]
    halo = jnp.concatenate([rim_in[:, None], inner], axis=1).reshape(blocks, RIM, width)

    w_low = in_weight.astype(low)
    o_low = out_weight.astype(low)
    if quick:
        half = o_low.shape[0] // 2
        packed = jnp.concatenate([o_low[:half], o_low[half:]], axis=1)
        second = jnp.stack([w_low[:, :DI], packed])
        first = jnp.concatenate(
            [
                in_weight[:, DI:],
                extras(
                    conv_weight[None], conv_bias[None], gate_gain[None], norm_gain[None]
                )[0],
            ],
            axis=1,
        ).astype(low)
        (ca, cb_pieces), second_line = weave_first(first, second, rim_in)
        begin = tie(scal, second_line)
    else:
        begin = scal
        order = jnp.array(order_of_pieces(), jnp.int32)
        rows_w = lax.all_gather(w_low, axes, axis=0, tiled=True).reshape(PIECES, -1, E)
        full_taps = lax.all_gather(conv_weight.astype(low), axes, axis=1, tiled=True)
        full = [
            lax.all_gather(value.astype(low), axes, axis=0, tiled=True).reshape(PIECES, -1)
            for value in (conv_bias, gate_gain, norm_gain)
        ]
        extra = extras(full_taps.reshape(KW, PIECES, -1).transpose(1, 0, 2), *full)
        whole = jnp.concatenate([rows_w[:, :, DI:], extra], axis=2)
        ca, cb_pieces = whole[order], whole[order + 1]
        outs = lax.all_gather(o_low, axes, axis=0, tiled=True)
        outs = outs.reshape(PIECES, 2, -1, width).transpose(0, 2, 1, 3).reshape(PIECES, -1, DI)
        whole = jnp.stack([rows_w[:, :, :DI], outs], axis=1)
        za, zb = whole[order], whole[order + 1]

    rate = jnp.exp(decay_log)
    par = jnp.pad(
        jnp.stack([step_bias, rate * 1.4426950408889634, rate, skip_gain]), ((0, 4), (0, HL - H))
    )
    e = jnp.asarray(head_table(), low)
    et = jnp.asarray(np.pad(head_table()[: HL // 2].T, ((0, 0), (0, HL // 2))), low)
    t56 = onehot(HL, CD, H, CD // PIECES)
    t48 = onehot(HL, DI, 80, DI // PIECES)
    t24 = onehot(HL, width, 80, width // PIECES)

    def forth(i):
        return i

    def back(i):
        return (i // groups) * groups + groups - 1 - i % groups

    def tokens(cols, order):
        return pl.BlockSpec((Q, cols), lambda i: (order(i), 0))

    def per_block(height, cols, order):
        return pl.BlockSpec((None, height, cols), lambda i: (order(i), 0, 0))

    def per_seq(height, cols):
        return pl.BlockSpec((None, height, cols), lambda i: (i // groups, 0, 0))

    def fixed(*shape):
        zeros = (0,) * len(shape)
        return pl.BlockSpec(shape, lambda i: zeros, pipeline_mode=pl.Buffered(1))

    def kept(*shape):
        zeros = (0,) * len(shape)
        return pl.BlockSpec(shape, lambda i: zeros)

    scalars = pl.BlockSpec(memory_space=pltpu.SMEM)
    whole = pl.BlockSpec(memory_space=pltpu.VMEM)
    away = pl.BlockSpec(memory_space=pl.ANY)
    flat_hidden = hidden.reshape(rows, width)
    flat_cot = cotangent.reshape(rows, width)

    (nrm, nrmt, cie, sp, xh, xs, wx, bc, step, cum, dtb, cumt, sloc, pre, ends, ends_low, totals, wc, taps, gain_in, gain_gate) = call(
        functools.partial(conv_kernel, groups),
        blocks,
        [
            (scalars, begin),
            (tokens(width, forth), flat_hidden),
            (per_block(RIM, width, forth), halo),
            (fixed(*ca.shape), ca),
            (fixed(*ca.shape), cb_pieces),
            (fixed(HL, CD), t56),
            (fixed(HL, DI), t48),
            (fixed(HL, width), t24),
            (fixed(8, HL), par),
            (fixed(HL, DI), e),
        ],
        [
            (tokens(width, forth), (rows, width), low),
            (pl.BlockSpec((width, Q), lambda i: (0, i)), (width, rows), low),
            (per_block(Q + RIM, CD, forth), (blocks, Q + RIM, CD), low),
            (tokens(CD, forth), (rows, CD), f32),
            (tokens(DI, forth), (rows, DI), low),
            (tokens(DI, forth), (rows, DI), low),
            (tokens(DI, forth), (rows, DI), low),
            (tokens(2 * N, forth), (rows, 2 * N), low),
            (tokens(HL, forth), (rows, HL), f32),
            (tokens(HL, forth), (rows, HL), f32),
            (tokens(HL, forth), (rows, HL), f32),
            (per_block(H, Q, forth), (blocks, H, Q), f32),
            (per_block(N, DI, forth), (blocks, N, DI), f32),
            (per_block(8, DI, forth), (blocks, 8, DI), f32),
            (per_seq(N, DI), (seqs, N, DI), f32),
            (per_seq(N, DI), (seqs, N, DI), low),
            (per_seq(1, DI), (seqs, 1, DI), f32),
            (away, (width, CW), low),
            (kept(8, CD), (8, CD), f32),
            (kept(8, width), (8, width), f32),
            (kept(8, DI), (8, DI), f32),
        ],
        [
            pltpu.VMEM((Q + RIM, width), low),
            pltpu.VMEM((N, DI), f32),
            pltpu.VMEM((8, DI), f32),
            pltpu.VMEM((2, HL, HL), f32),
            pltpu.VMEM((width, CW), low),
            pltpu.SemaphoreType.DMA,
            *[pltpu.VMEM((Q + RIM, HALF), f32)] * (CD // HALF),
        ],
        2.0 * rows * width * CW,
        "conv",
    )
    if quick:
        (za, zb), token = weave_second(second_line, second, cum)
        bc_after = tie(bc, token)
    else:
        bc_after = bc

    def intra_part(got):
        return call(
            intra_kernel,
            blocks,
            [
                (tokens(2 * N, forth), bc_after),
                (tokens(DI, forth), xs),
                (tokens(HL, forth), cum),
                (per_block(H, Q, forth), cumt),
            ],
            [(tokens(DI, forth), (rows, DI), f32)],
            [pltpu.VMEM((Q, Q), f32)],
            2.0 * rows * Q * DI * 2,
            "intra",
        )

    def after(value, got):
        return value if got is None else tie(value, got)

    def project_part(got):
        return call(
            functools.partial(project_kernel, groups),
            blocks,
            [
                (scalars, after(scal, got)),
                (tokens(width, forth), nrm),
                (tokens(width, forth), flat_cot),
                (fixed(*za.shape), za),
                (fixed(*za.shape), zb),
            ],
            [
                (whole, (rows, DI), f32, near),
                (whole, (rows, DI), f32, near),
                (tokens(width, forth), (rows, width), low),
                (away, (width, DI), low),
                (away, (DI, width), low),
            ],
            [
                pltpu.VMEM((width, DI), low),
                pltpu.VMEM((DI, width), low),
                pltpu.SemaphoreType.DMA((2,)),
            ],
            4.0 * rows * width * DI,
            "project",
        )

    incoming, ((intra,), (z, dn, db, wz, wo)) = relay(
        ends, ends_low, totals, True, [intra_part, project_part]
    )

    (out, dz, dy, gdy, gn, sbf, rs1, dloc, suf, back_ends, back_ends_low, back_totals, kacc) = call(
        functools.partial(gate_kernel, groups, len(incoming)),
        blocks,
        [
            (scalars, scal),
            (tokens(DI, back), intra),
            (tokens(DI, back), xh),
            (tokens(2 * N, back), bc),
            (tokens(HL, back), cum),
            (per_block(N, DI, back), sloc),
            (per_block(8, DI, back), pre),
            *[(per_seq(N, DI), value) for value in incoming],
            (whole, near(z)),
            (whole, near(dn)),
            (tokens(width, back), flat_hidden),
            (fixed(DI, width), wo),
            (fixed(8, DI), gain_gate),
            (fixed(8, HL), par),
            (fixed(HL, DI), e),
            (fixed(DI, HL), et),
        ],
        [
            (tokens(width, back), (rows, width), low),
            (tokens(DI, back), (rows, DI), low),
            (tokens(DI, back), (rows, DI), low),
            (tokens(DI, back), (rows, DI), low),
            (tokens(DI, back), (rows, DI), low),
            (per_block(N, DI, back), (blocks, N, DI), low),
            (tokens(HL, back), (rows, HL), f32),
            (per_block(N, DI, back), (blocks, N, DI), f32),
            (per_block(8, DI, back), (blocks, 8, DI), f32),
            (per_seq(N, DI), (seqs, N, DI), f32),
            (per_seq(N, DI), (seqs, N, DI), low),
            (per_seq(1, DI), (seqs, 1, DI), f32),
            (kept(8, DI), (8, DI), f32),
        ],
        [
            pltpu.VMEM((Q, DI), f32),
            pltpu.VMEM((Q, DI), f32),
            pltpu.VMEM((Q, DI), f32),
            pltpu.VMEM((Q, DI), f32),
            pltpu.VMEM((Q, DI), f32),
            pltpu.VMEM((Q, DI), f32),
            pltpu.VMEM((N, DI), f32),
            pltpu.VMEM((8, DI), f32),
            pltpu.VMEM((8, DI), f32),
            pltpu.VMEM((8, DI), f32),
        ],
        4.0 * rows * width * DI,
        "gate",
    )

    def intra_back_part(got):
        return call(
            intra_back_kernel,
            blocks,
            [
                (tokens(2 * N, forth), after(bc, got)),
                (tokens(DI, forth), xs),
                (tokens(DI, forth), xh),
                (tokens(DI, forth), dy),
                (tokens(HL, forth), step),
                (tokens(HL, forth), cum),
                (per_block(H, Q, forth), cumt),
                (fixed(8, HL), par),
                (fixed(HL, DI), e),
                (fixed(DI, HL), et),
            ],
            [
                (tokens(DI, forth), (rows, DI), f32),
                (tokens(2 * N, forth), (rows, 2 * N), f32),
                (tokens(HL, forth), (rows, HL), f32),
            ],
            [pltpu.VMEM((Q, Q), f32), pltpu.VMEM((Q, Q), f32)],
            4.0 * rows * Q * DI * 2,
            "intra_back",
        )

    piece = (PIECES // 2, 2, width // PIECES, DI)

    def early_part(got):
        return call(
            early_grad_kernel,
            EARLY,
            [
                (scalars, after(scal, got)),
                (fixed(width, rows), nrmt),
                (pl.BlockSpec((rows, DI // EARLY), lambda i: (0, i)), dz),
                (pl.BlockSpec((rows, DI // EARLY), lambda i: (0, i)), gn),
                (fixed(rows, width), db),
                (pl.BlockSpec((width, DI // EARLY), lambda i: (0, i)), wz),
                (pl.BlockSpec((DI // EARLY, width), lambda i: (i, 0)), wo),
            ],
            [
                (kept(*piece), piece, low),
                (kept(*piece), piece, low),
                (kept(width, HALF), (width, HALF), f32),
                (pl.BlockSpec((DI // EARLY, HALF), lambda i: (i, 0)), (DI, HALF), f32),
            ],
            [pltpu.VMEM((width, DI // EARLY), f32), pltpu.VMEM((DI, width), f32)],
            6.0 * rows * width * DI,
            "early_grad",
        )

    back_incoming, ((e0, e1, na, ga), (dx, dbc, rs2)) = relay(
        back_ends, back_ends_low, back_totals, False, [early_part, intra_back_part]
    )
    if quick:
        early = merge_core(e0, tie(swap(e1, 1), rs2))
        back_incoming[-1] = tie(back_incoming[-1], *early[1])

    (dcv, cacc, hacc, heads_out, tails_out) = call(
        functools.partial(conv_back_kernel, groups, len(back_incoming)),
        blocks,
        [
            (scalars, scal),
            (per_block(N, DI, back), dloc),
            (per_block(8, DI, back), suf),
            (per_block(N, DI, back), sbf),
            (tokens(DI, back), xh),
            (tokens(DI, back), wx),
            (tokens(DI, back), gdy),
            (tokens(DI, back), dx),
            (tokens(2 * N, back), dbc),
            (tokens(2 * N, back), bc),
            (tokens(HL, back), cum),
            (tokens(HL, back), step),
            (tokens(HL, back), dtb),
            (tokens(HL, back), rs1),
            (tokens(HL, back), rs2),
            *[(per_seq(N, DI), value) for value in back_incoming],
            (per_block(Q + RIM, CD, back), cie),
            (tokens(CD, back), sp),
            (fixed(8, CD), taps),
            (fixed(8, HL), par),
            (fixed(HL, DI), e),
            (fixed(DI, HL), et),
        ],
        [
            (tokens(CW, back), (rows, CW), low),
            (kept(8 * (KW + 1), CD), (8 * (KW + 1), CD), f32),
            (kept(16, HL), (16, HL), f32),
            (per_seq(8, CW), (seqs, 8, CW), low),
            (per_seq(16, CW), (seqs, 16, CW), f32),
        ],
        [
            pltpu.VMEM((8, CD), f32),
            *[pltpu.VMEM((Q + 16, HALF), f32)] * (CD // HALF),
        ],
        6.0 * rows * N * DI,
        "conv_back",
    )
    turn = scal
    if quick:
        early = parts_of(merge(*early, (2, 4, 6), hacc))
        turn = tie(scal, *early[1])
    returned = lax.ppermute(heads_out, "seq", [(i, i - 1) for i in range(1, seq_size)])

    late = (PIECES // 2, width // PIECES, CW)
    late_spec = pl.BlockSpec((PIECES // 2, width // PIECES, CW // LATE), lambda i: (0, 0, i))
    (l0, l1, dcv, vector) = call(
        late_grad_kernel,
        LATE,
        [
            (scalars, turn),
            (fixed(width, rows), nrmt),
            (pl.BlockSpec((rows, CW // LATE), lambda i: (0, i)), dcv),
            (pl.BlockSpec((width, CW // LATE), lambda i: (0, i)), wc),
            (fixed(width, HALF), na),
            (pl.BlockSpec((seqs, 16, CW // LATE), lambda i: (0, 0, i)), tails_out),
            (pl.BlockSpec((seqs, 8, CW // LATE), lambda i: (0, 0, i)), returned),
            (fixed(8 * (KW + 1), CD), cacc),
            (fixed(16, HL), hacc),
            (fixed(8, DI), kacc),
            (fixed(DI, HALF), ga),
            (fixed(8, HL), par),
            (fixed(DI, HL), et),
        ],
        [
            (late_spec, late, low),
            (late_spec, late, low),
            (pl.BlockSpec((rows, CW // LATE), lambda i: (0, i)), (rows, CW), low),
            (kept(96, HALF), (96, HALF), f32),
        ],
        [pltpu.VMEM((width, CW // LATE), f32), pltpu.VMEM((width, HALF), f32)],
        2.0 * rows * width * CW,
        "late_grad",
    )

    def input_part(first, count, past, before, token):
        def order(i):
            return i + first

        return call(
            input_kernel,
            count,
            [
                (tokens(CW, order), dcv),
                (tokens(DI, order), dz),
                (fixed(width, CW), wc),
                (fixed(width, DI), wz),
                (tokens(width, order), flat_hidden),
                (tokens(width, order), flat_cot),
                (fixed(8, width), gain_in if token is None else tie(gain_in, *token)),
                (pl.BlockSpec(memory_space=pl.ANY), past),
                (pl.BlockSpec(memory_space=pl.ANY), before),
            ],
            [
                (tokens(width, order), (rows, width), low),
                (kept(8, HALF), (8, HALF), f32),
            ],
            [pltpu.VMEM((Q, width), f32)],
            1.0,
            "input",
            {7: 0} if first else None,
        )

    half_blocks = max(blocks // 4, 1)
    if quick:
        late_got = swap(l1, 1)
        vector_got = swap(vector, 1)
        gh, done = input_part(0, half_blocks, scal, scal, None)
        late_sum = merge_core(l0, tie(late_got, done))
        vector = vector + tie(vector_got, done)
        early = tie_all(*early, late_sum[1][0])
        gh, done2 = input_part(half_blocks, blocks - half_blocks, gh, done, late_sum[1])
        late_sum = parts_of(merge(*late_sum, (2, 4, 6), done2))
        early = merge(*early, (8, 16, 24), late_sum[1][0])
        vector = tie(vector, late_sum[1][0])
        got = [swap(vector, mask) for mask in (2, 4, 6)]
        vector = tie((vector + got[0]) + (got[1] + got[2]), early)
    else:
        gh, done = input_part(0, blocks, scal, scal, None)

    if quick:
        got = [swap(vector, mask) for mask in (8, 16, 24)]
        vector = (vector + got[0]) + (got[1] + got[2])
        own_late = merge(*late_sum, (8, 16, 24))
        own_z, own_out = early[0], early[1]
        own_out = jnp.concatenate([own_out[:, : DI // 2], own_out[:, DI // 2 :]], axis=0)
    else:
        vector = lax.psum(vector, axes)
        order = jnp.array(order_of_pieces(), jnp.int32)
        inverse = jnp.argsort(jnp.concatenate([order, order + 1]))
        whole = jnp.concatenate([e0, e1])[inverse].astype(f32)
        outs = whole[:, 1].reshape(PIECES, -1, 2, width).transpose(0, 2, 1, 3).reshape(DI, width)
        own_z = lax.psum_scatter(
            whole[:, 0].reshape(width, DI), axes, scatter_dimension=0, tiled=True
        )
        own_out = lax.psum_scatter(outs, axes, scatter_dimension=0, tiled=True)
        whole = jnp.concatenate([l0, l1])[inverse].astype(f32).reshape(width, CW)
        own_late = lax.psum_scatter(whole, axes, scatter_dimension=0, tiled=True)

    def own(value, size, axis):
        return lax.dynamic_slice_in_dim(value, place * size, size, axis)

    tile = CD // HALF
    g_taps = own(vector[: KW * tile].reshape(KW, CD), CD // devices, 1)
    at = KW * tile
    g_bias = own(vector[at : at + tile].reshape(-1), CD // devices, 0)
    at += tile
    g_gate = own(vector[at : at + DI // HALF].reshape(-1), gate_gain.shape[0], 0)
    at += DI // HALF
    g_norm = own(vector[at : at + width // HALF].reshape(-1), norm_gain.shape[0], 0)
    at += width // HALF
    g_gate, g_norm = g_gate / rounded(gate_gain), g_norm / rounded(norm_gain)
    g_in = jnp.concatenate([own_z, own_late[:, : CD + H]], axis=1)
    return (
        out.reshape(hidden.shape),
        gh.reshape(hidden.shape),
        g_norm,
        g_in,
        g_taps,
        g_bias,
        vector[at, :H],
        vector[at + 1, :H],
        vector[at + 2, :H],
        g_gate,
        own_out,
    )


def solution(mesh):
    return jax.shard_map(
        per_device,
        mesh=mesh,
        in_specs=(
            P("dp", "seq", None),
            P("dp"),
            P(("dp", "seq")),
            P(("dp", "seq"), None),
            P(None, ("dp", "seq")),
            P(("dp", "seq")),
            P(),
            P(),
            P(),
            P(("dp", "seq")),
            P(("dp", "seq"), None),
            P("dp", "seq", None),
        ),
        out_specs=(
            P("dp", "seq", None),
            P("dp", "seq", None),
            P(("dp", "seq")),
            P(("dp", "seq"), None),
            P(None, ("dp", "seq")),
            P(("dp", "seq")),
            P(),
            P(),
            P(),
            P(("dp", "seq")),
            P(("dp", "seq"), None),
        ),
        check_vma=False,
    )
```

```python
import functools

import jax
import jax.numpy as jnp
import numpy as np
from jax import lax
from jax.experimental import pallas as pl
from jax.experimental.pallas import tpu as pltpu
from jax.sharding import PartitionSpec as P

H = 24
P_SIZE = 64
N = 128
KW = 4
Q = 256
E = 3352
DI = 1536
CD = 1792
HL = 128
CW = CD + HL
CH = 256
HALF = 128
RIM = 16
EARLY = 3
LATE = 3
PIECES = 32
NEG = -1e30
LIMITS = {
    "conv": 56,
    "intra": 56,
    "project": 48,
    "gate": 48,
    "early_grad": 56,
    "intra_back": 51,
    "conv_back": 54,
    "late_grad": 56,
    "input": 56,
}

epsilon = 1e-05
low = jnp.bfloat16
f32 = jnp.float32
axes = ("dp", "seq")


def onehot(rows, cols, first, period):
    table = np.zeros((rows, cols), np.float32)
    at = np.arange(cols)
    table[first + at % period, at] = 1.0
    return jnp.asarray(table, low)


def head_table():
    table = np.zeros((HL, DI), np.float32)
    at = np.arange(DI)
    table[at // P_SIZE, at] = 1.0
    table[HL // 2 + at // P_SIZE, at] = 1.0
    return table


def dot(left, right, dims):
    return lax.dot_general(left, right, (dims, ((), ())), preferred_element_type=f32)


def nn(left, right):
    return dot(left, right, ((1,), (0,)))


def nt(left, right):
    return dot(left, right, ((1,), (1,)))


def tn(left, right):
    return dot(left, right, ((0,), (0,)))


def pack(value):
    top = value.astype(low).astype(f32)
    rest = pltpu.roll(value - top, HL // 2, 1)
    lane = lax.broadcasted_iota(jnp.int32, value.shape, 1)
    return jnp.where(lane < HL // 2, top, rest).astype(low)


def spread(packed, table):
    return nn(packed, table)


def spread_all(packed, table):
    wide = nn(jnp.concatenate(packed, axis=0), table)
    parts, at = [], 0
    for value in packed:
        parts.append(wide[at : at + value.shape[0], :])
        at += value.shape[0]
    return parts


def gather_all(values, table):
    tops = [value.astype(low) for value in values]
    rests = [(value - top.astype(f32)).astype(low) for value, top in zip(values, tops)]
    parts = spread_all(tops + rests, table)
    return [parts[i] + parts[i + len(values)] for i in range(len(values))]


def gather_heads(value, table):
    return gather_all([value], table)[0]


def running_sum(value, reverse):
    rows = value.shape[0]
    at = lax.broadcasted_iota(jnp.int32, value.shape, 0)
    step = 1
    while step < rows:
        if reverse:
            value = value + jnp.where(at < rows - step, pltpu.roll(value, rows - step, 0), 0.0)
        else:
            value = value + jnp.where(at >= step, pltpu.roll(value, step, 0), 0.0)
        step *= 2
    return value


def softplus(value):
    tail = jnp.exp(-jnp.abs(value))
    series = tail * (1.0 - tail * (0.5 - tail * (1.0 / 3.0 - tail * (0.25 - tail * 0.2))))
    return jnp.maximum(value, 0.0) + jnp.where(tail < 0.03125, series, jnp.log(1.0 + tail))


def fold8(value):
    return jnp.sum(value.reshape(value.shape[0] // 8, 8, value.shape[1]), axis=0)


def pair_rows(me, own, other):
    first = (me & 1) == 0
    return jnp.concatenate([jnp.where(first, own, other), jnp.where(first, other, own)], axis=0)


def source_of(me, place):
    return me ^ ((place // 4) * 2) ^ ((place % 4) * 8)


def place_of(piece):
    return ((piece >> 1) & 3) * 4 + (piece >> 3)


def conv_kernel(
    groups, scal, x, halo, wa, wb, t56, t48, t24, par, e,
    nrm_o, nrmt_o, cie_o, sp_o, xh_o, xs_o, wx_o, bc_o, step_o, cum_o, dtb_o, cumt_o,
    sloc_o, pre_o, r_o, rl_o, tot_o, wc_o, taps_o, gain_o, gate_o,
    nrm, run, dec, small, wc_s, sem, *slots,
):
    block = pl.program_id(0)
    fresh = block % groups == 0
    zero = scal[scal.shape[0] - 1]

    @pl.when(block == 0)
    def assemble():
        me = scal[0]

        def one(place, carry):
            chip = source_of(me, place) >> 1
            own, other = wa[place].astype(f32), wb[place].astype(f32)
            wc_s[pl.ds(pl.multiple_of(chip * 48, 16), 48), :] = pair_rows(me, own, other).astype(low)
            rows = pl.ds(pl.multiple_of(place * 8, 8), 8)
            small[0, rows, :] = own[0:8, CD:CW]
            small[1, rows, :] = other[0:8, CD:CW]
            return carry

        lax.fori_loop(0, PIECES // 2, one, 0)
        pltpu.make_async_copy(wc_s, wc_o, sem).start()
        at = lax.broadcasted_iota(jnp.int32, (PIECES, 1), 0)
        slot = at & (PIECES // 2 - 1)
        ids = me ^ ((slot >> 2) << 1) ^ ((slot & 3) << 3) ^ (at >> 4)

        def row_of(k, table, size):
            pieces = [small[which, pl.ds(k, PIECES // 2, stride=8), :] for which in range(2)]
            wide = nn(jnp.concatenate(pieces, axis=0).astype(low), table)
            lane = lax.broadcasted_iota(jnp.int32, wide.shape, 1)
            inside = jnp.logical_and(lane >= ids * size, lane < (ids + 1) * size)
            return jnp.sum(jnp.where(inside, wide, 0.0), axis=0, keepdims=True)

        for k in range(KW + 1):
            taps_o[k : k + 1, :] = row_of(k, t56[...], CD // PIECES)
        gate_o[0:1, :] = row_of(0, t48[...], DI // PIECES)
        gain_o[0:1, :] = row_of(1, t24[...], gain_o.shape[1] // PIECES)

    def normed(rows):
        wide = rows.astype(f32)
        scale = lax.rsqrt(jnp.mean(wide * wide, axis=-1, keepdims=True) + epsilon)
        return (wide * scale * gain_o[0:1, :]).astype(low)

    nrm[0:RIM, :] = normed(halo[...])
    for r in range(0, Q, 32):
        nrm[RIM + r : RIM + r + 32, :] = normed(x[r : r + 32, :])
    nrm_o[...] = nrm[RIM:, :]
    nrmt_o[...] = nrm[RIM:, :].T

    for c in range(0, CD, CH):
        cols = slice(c, c + CH)
        conv_in = nn(nrm[...], wc_s[:, cols]).astype(low)
        cie_o[:, cols] = conv_in
        wide = conv_in.astype(f32)
        for side in range(2):
            span = slice(c + side * HALF, c + (side + 1) * HALF)
            cs = slots[c // HALF + side]
            cs[...] = wide[:, side * HALF : (side + 1) * HALF]
            for r in range(0, Q, 64):
                taps = taps_o[0:1, span] * cs[pl.ds(zero + (RIM - 3 + r), 64), :]
                for k in range(1, KW):
                    taps = taps + taps_o[k : k + 1, span] * cs[pl.ds(zero + (RIM - 3 + k + r), 64), :]
                pre = taps_o[KW : KW + 1, span] + taps
                sig = jax.nn.sigmoid(pre)
                act = (pre * sig).astype(low)
                sp_o[r : r + 64, span] = sig * (1.0 + pre * (1.0 - sig))
                if c < DI:
                    xh_o[r : r + 64, span] = act
                else:
                    bc_o[r : r + 64, side * HALF : (side + 1) * HALF] = act

    dtb = nn(nrm[RIM:, :], wc_s[:, CD:CW]) + par[0:1, :]
    step = softplus(dtb)
    cum = running_sum(-step * par[1:2, :], False)
    step_o[...] = step
    cum_o[...] = cum
    dtb_o[...] = dtb
    cumt_o[...] = cum.T[0:H, :]
    last = cum[Q - 1 : Q, :]
    steps = pack(step)
    tails = pack(jnp.exp2(last - cum) * step)
    decays = pack(jnp.broadcast_to(jnp.exp2(last), (8, HL)))
    for c in range(0, DI, CH):
        cols = slice(c, c + CH)
        table = e[:, cols]
        wide = xh_o[:, cols].astype(f32)
        xs_o[:, cols] = (spread(steps, table) * wide).astype(low)
        tail_e, decay = spread_all([tails, decays], table)
        weighted = (tail_e * wide).astype(low)
        wx_o[:, cols] = weighted
        local = tn(bc_o[:, 0:N], weighted)
        before = jnp.where(fresh, 0.0, run[:, cols])
        sloc_o[:, cols] = before
        after = decay[0:1, :] * before + local
        run[:, cols] = after
        r_o[:, cols] = after
        rl_o[:, cols] = after.astype(low)
        product = jnp.where(fresh, 1.0, dec[:, cols])
        pre_o[:, cols] = product
        product = product * decay
        dec[:, cols] = product
        tot_o[:, cols] = product[0:1, :]

    @pl.when(block == pl.num_programs(0) - 1)
    def finish():
        pltpu.make_async_copy(wc_s, wc_o, sem).wait()


def block_rows(block):
    return pl.ds(pl.multiple_of(block * Q, Q), Q)


def intra_kernel(bc, xs, cum, cumt, o, sc):
    sc[...] = nt(bc[:, N : 2 * N], bc[:, 0:N])
    at = lax.broadcasted_iota(jnp.int32, (HALF, HALF), 0)
    to = lax.broadcasted_iota(jnp.int32, (HALF, HALF), 1)
    lower = at >= to
    left = lax.broadcasted_iota(jnp.int32, (HALF, HALF), 1) < P_SIZE
    for pair in range(H // 2):
        cols = slice(pair * HALF, (pair + 1) * HALF)
        x_pair = xs[:, cols]
        m00, m10, m11 = [], [], []
        for h in (2 * pair, 2 * pair + 1):
            row = cumt[h : h + 1, :]
            upper_col, lower_col = cum[0:HALF, h : h + 1], cum[HALF:, h : h + 1]
            l00 = jnp.exp2(jnp.where(lower, upper_col - row[:, 0:HALF], NEG))
            m00.append((sc[0:HALF, 0:HALF] * l00).astype(low))
            l10 = jnp.exp2(lower_col - row[:, 0:HALF])
            m10.append((sc[HALF:, 0:HALF] * l10).astype(low))
            l11 = jnp.exp2(jnp.where(lower, lower_col - row[:, HALF:], NEG))
            m11.append((sc[HALF:, HALF:] * l11).astype(low))
        top = nn(jnp.concatenate(m00, axis=0), x_pair[0:HALF, :])
        sides = [jnp.concatenate([m10[i], m11[i]], axis=1) for i in range(2)]
        bottom = nn(jnp.concatenate(sides, axis=0), x_pair)
        o[0:HALF, cols] = jnp.where(left, top[0:HALF, :], top[HALF:, :])
        o[HALF:, cols] = jnp.where(left, bottom[0:HALF, :], bottom[HALF:, :])


def valid_column(scal, groups, block):
    seq, group = block // groups, block % groups
    at = scal[1] * (groups * Q) + group * Q + lax.broadcasted_iota(jnp.int32, (Q, 1), 0)
    return (at < scal[2 + seq]).astype(f32)


def project_kernel(
    groups, scal, nrm, cot, wa, wb, z_all, dn_all, db_o, wz_o, wo_o, wz_s, wo_s, sems
):
    block = pl.program_id(0)
    z_o, dn_o = z_all.at[block_rows(block), :], dn_all.at[block_rows(block), :]

    copies = [
        pltpu.make_async_copy(wz_s, wz_o, sems.at[0]),
        pltpu.make_async_copy(wo_s, wo_o, sems.at[1]),
    ]

    @pl.when(block == 0)
    def assemble():
        me = scal[0]

        def halves(packed):
            return jnp.concatenate([packed[:, 0 : DI // 2], packed[:, DI // 2 :]], axis=0)

        def one(place, carry):
            chip = source_of(me, place) >> 1
            own, other = wa[place, 0].astype(f32), wb[place, 0].astype(f32)
            wz_s[pl.ds(pl.multiple_of(chip * 48, 16), 48), :] = pair_rows(me, own, other).astype(low)
            own, other = halves(wa[place, 1].astype(f32)), halves(wb[place, 1].astype(f32))
            wo_s[pl.ds(pl.multiple_of(chip * 96, 16), 96), :] = pair_rows(me, own, other).astype(low)
            return carry

        lax.fori_loop(0, PIECES // 2, one, 0)
        for copy in copies:
            copy.start()

    db_o[...] = (cot[...].astype(f32) * valid_column(scal, groups, block)).astype(low)
    for c in range(0, DI, CH):
        z_o[:, c : c + CH] = nn(nrm[...], wz_s[:, c : c + CH])
        dn_o[:, c : c + CH] = nt(db_o[...], wo_s[c : c + CH, :])

    @pl.when(block == pl.num_programs(0) - 1)
    def finish():
        for copy in copies:
            copy.wait()


def gate_kernel(
    groups, hops, scal, intra, xh, bc, cum, sloc, pre, *refs
):
    inc = refs[:hops]
    z_all, dn_all, hid, wo, gg, par, e, et = refs[hops : hops + 8]
    (
        out_o, dz_o, dy_o, gdy_o, gn_o, sbf_o, rs_o, dloc_o, suf_o, rd_o, rdl_o, tot_o, kacc_o,
        yi_s, ge_s, pr_s, y_s, sg_s, gt_s, run, dec, skip, fall,
    ) = refs[hops + 8 :]
    at = pl.program_id(0)
    fresh = at % groups == 0
    block = (at // groups) * groups + groups - 1 - at % groups
    here = block_rows(block)
    z, dn = z_all.at[here, :], dn_all.at[here, :]

    @pl.when(at == 0)
    def start():
        kacc_o[...] = jnp.zeros_like(kacc_o)

    c_rows = bc[:, N : 2 * N]
    growth = pack(jnp.exp2(cum[...]))
    params = pack(par[...])
    decays = pack(jnp.broadcast_to(jnp.exp2(cum[Q - 1 : Q, :]), (8, HL)))
    for c in range(0, DI, CH):
        cols = slice(c, c + CH)
        begin = (sloc[:, cols] + pre[0:1, cols] * total_of(inc, cols)).astype(low)
        sbf_o[:, cols] = begin
        wide, skip[:, cols], fall[:, cols] = spread_all([growth, params, decays], e[:, cols])
        ge_s[:, cols] = wide
        yi_s[:, cols] = intra[:, cols] + wide * nn(c_rows, begin)

    def body(r):
        rows = slice(r, r + 32)
        squares = jnp.zeros((32, HALF), f32)
        crosses = jnp.zeros((32, HALF), f32)
        for c in range(0, DI, HALF):
            cols = slice(c, c + HALF)
            zv = z[rows, cols]
            y = yi_s[rows, cols] + skip[3:4, cols] * xh[rows, cols].astype(f32)
            sig = jax.nn.sigmoid(zv)
            gated = y * (zv * sig)
            squares = squares + gated * gated
            crosses = crosses + (dn[rows, cols] * gg[0:1, cols]) * gated
            y_s[rows, cols] = y
            sg_s[rows, cols] = sig
            gt_s[rows, cols] = gated
        scale = lax.rsqrt(jnp.sum(squares, axis=1, keepdims=True) / DI + epsilon)
        shift = scale * scale * scale * (jnp.sum(crosses, axis=1, keepdims=True) / DI)
        for c in range(0, DI, HALF):
            cols = slice(c, c + HALF)
            zv, y, sig, gated = z[rows, cols], y_s[rows, cols], sg_s[rows, cols], gt_s[rows, cols]
            gained = gg[0:1, cols]
            gn_o[rows, cols] = (gated * scale * gained).astype(low)
            d_gated = scale * (dn[rows, cols] * gained) - gated * shift
            d_sig = d_gated * sig
            d_wide = d_sig * zv
            dz_o[rows, cols] = (y * (d_sig + d_wide * (1.0 - sig))).astype(low)
            d_low = d_wide.astype(low)
            dy_o[rows, cols] = d_low
            d_y = d_low.astype(f32)
            kacc_o[:, cols] += fold8(d_y * xh[rows, cols].astype(f32))
            gdy_o[rows, cols] = (ge_s[rows, cols] * d_y).astype(low)
            pr_s[rows, cols] = d_y * yi_s[rows, cols]

    for r in range(0, Q, 32):
        body(r)

    valid = valid_column(scal, groups, block)
    for c in range(0, DI // 2, CH):
        branch = nn(gn_o[...], wo[:, c : c + CH])
        out_o[:, c : c + CH] = (hid[:, c : c + CH].astype(f32) + valid * branch).astype(low)
    sums = jnp.zeros((Q, HL), f32)
    for c in range(0, DI, CH):
        cols = slice(c, c + CH)
        sums = sums + gather_heads(pr_s[:, cols], et[cols, :])
        decay = fall[:, cols]
        before = jnp.where(fresh, 0.0, run[:, cols])
        dloc_o[:, cols] = before
        after = decay[0:1, :] * before + tn(c_rows, gdy_o[:, cols])
        run[:, cols] = after
        rd_o[:, cols] = after
        rdl_o[:, cols] = after.astype(low)
        product = jnp.where(fresh, 1.0, dec[:, cols])
        suf_o[:, cols] = product
        product = product * decay
        dec[:, cols] = product
        tot_o[:, cols] = product[0:1, :]
    rs_o[...] = sums


def intra_back_kernel(bc, xs, xh, dy, step, cum, cumt, par, e, et, dx_o, dbc_o, rs_o, sc, acc):
    sc[...] = nt(bc[:, 0:N], bc[:, N : 2 * N])
    acc[...] = jnp.zeros_like(acc)
    at = lax.broadcasted_iota(jnp.int32, (HALF, HALF), 0)
    to = lax.broadcasted_iota(jnp.int32, (HALF, HALF), 1)
    upper = at <= to
    left = lax.broadcasted_iota(jnp.int32, (Q, HALF), 1) < P_SIZE
    steps = pack(step[...])
    params = pack(par[...])
    sums = jnp.zeros((Q, HL), f32)
    for quad in range(H // 4):
        flows = []
        for pair in (2 * quad, 2 * quad + 1):
            cols = slice(pair * HALF, (pair + 1) * HALF)
            dy_pair = dy[:, cols]
            x_pair = xs[:, cols]
            heads = (2 * pair, 2 * pair + 1)
            zeros = jnp.zeros_like(x_pair)
            x_a, x_b = jnp.where(left, x_pair, zeros), jnp.where(left, zeros, x_pair)
            rows = [cumt[h : h + 1, :] for h in heads]
            x_top = jnp.concatenate([x_a[0:HALF, :], x_b[0:HALF, :]], axis=0)
            grown = nt(x_top, dy_pair)
            m00, m01, m11 = [], [], []
            total = 0.0
            for i, h in enumerate(heads):
                first_col = cum[0:HALF, h : h + 1]
                l00 = jnp.exp2(jnp.where(upper, rows[i][:, 0:HALF] - first_col, NEG))
                m00.append((sc[0:HALF, 0:HALF] * l00).astype(low))
                total = total + grown[i * HALF : (i + 1) * HALF, 0:HALF] * l00
            acc[0:HALF, 0:HALF] += total
            total = 0.0
            for i, h in enumerate(heads):
                first_col = cum[0:HALF, h : h + 1]
                l01 = jnp.exp2(rows[i][:, HALF:] - first_col)
                m01.append((sc[0:HALF, HALF:] * l01).astype(low))
                total = total + grown[i * HALF : (i + 1) * HALF, HALF:] * l01
            acc[0:HALF, HALF:] += total
            sides = [jnp.concatenate([m00[i], m01[i]], axis=1) for i in range(2)]
            top = nn(jnp.concatenate(sides, axis=0), dy_pair)
            x_bottom = jnp.concatenate([x_a[HALF:, :], x_b[HALF:, :]], axis=0)
            grown = nt(x_bottom, dy_pair[HALF:, :])
            total = 0.0
            for i, h in enumerate(heads):
                second_col = cum[HALF:, h : h + 1]
                l11 = jnp.exp2(jnp.where(upper, rows[i][:, HALF:] - second_col, NEG))
                m11.append((sc[HALF:, HALF:] * l11).astype(low))
                total = total + grown[i * HALF : (i + 1) * HALF, :] * l11
            acc[HALF:, HALF:] += total
            bottom = nn(jnp.concatenate(m11, axis=0), dy_pair[HALF:, :])
            half_left = left[0:HALF]
            flows.append(
                jnp.concatenate(
                    [
                        jnp.where(half_left, top[0:HALF, :], top[HALF:, :]),
                        jnp.where(half_left, bottom[0:HALF, :], bottom[HALF:, :]),
                    ],
                    axis=0,
                )
            )
        cols = slice(quad * CH, (quad + 1) * CH)
        flow = jnp.concatenate(flows, axis=1)
        sums = sums + gather_heads(flow * xh[:, cols].astype(f32), et[cols, :])
        step_e, skip = spread_all([steps, params], e[:, cols])
        dx_o[:, cols] = step_e * flow + skip[3:4, :] * dy[:, cols].astype(f32)
    rs_o[...] = sums
    scores = acc[...].astype(low)
    dbc_o[:, 0:N] = nn(scores, bc[:, N : 2 * N])
    dbc_o[:, N : 2 * N] = tn(scores, bc[:, 0:N])


def conv_back_kernel(
    groups, hops, scal, dloc, suf, sbf, xh, wx, gdy, dx, dbc, bc, cum, step, dtb, rs1, rs2, *refs
):
    inc = refs[:hops]
    cie, sp, cw, par, e, et, dcv_o, kacc_o, hacc_o, head_o, tail_o, nxt, *slots = refs[hops:]
    at = pl.program_id(0)
    fresh = at % groups == 0
    opening = at % groups == groups - 1
    zero = scal[scal.shape[0] - 1]

    @pl.when(at == 0)
    def start():
        kacc_o[...] = jnp.zeros_like(kacc_o)
        hacc_o[...] = jnp.zeros_like(hacc_o)

    def conv_back(flow, c):
        for side in range(2):
            half_back(flow[:, side * HALF : (side + 1) * HALF], c + side * HALF)

    def half_back(flow, c):
        ds = slots[c // HALF]
        cols = slice(c, c + HALF)
        ds[0:8, :] = jnp.zeros((8, HALF), f32)
        ds[8 + Q :, :] = jnp.where(fresh, 0.0, nxt[:, cols])
        ds[8 : 8 + Q, :] = flow * sp[:, cols]
        nxt[:, cols] = ds[8:16, :]
        taps = [cw[k : k + 1, cols] for k in range(KW)]
        sums = [jnp.zeros((8, HALF), f32) for _ in range(KW + 1)]

        def views_at(begin, count):
            return [ds[pl.ds(zero + (begin + 11 - k), count), :] for k in range(KW)]

        def back(views):
            total = taps[0] * views[0]
            for k in range(1, KW):
                total = total + taps[k] * views[k]
            return total

        for r in range(0, Q, 64):
            views = views_at(r, 64)
            dcv_o[r : r + 64, cols] = back(views).astype(low)
            conv_in = cie[RIM + r : RIM + r + 64, cols].astype(f32)
            for k in range(KW):
                sums[k] = sums[k] + fold8(views[k] * conv_in)
            sums[KW] = sums[KW] + fold8(views[KW - 1])
        views = views_at(-8, 8)
        head_o[:, cols] = back(views).astype(low)
        conv_in = cie[0:RIM, cols].astype(f32)[8:16, :]
        for k in range(KW):
            kacc_o[8 * k : 8 * k + 8, cols] += sums[k] + jnp.where(opening, views[k] * conv_in, 0.0)
        kacc_o[8 * KW : 8 * KW + 8, cols] += sums[KW]

    cumv = cum[...]
    stepv = step[...]
    last = cumv[Q - 1 : Q, :]
    fade = jnp.exp2(last - cumv)
    tail = fade * stepv
    tails = pack(tail)
    b_rows = bc[:, 0:N]
    d_b = dbc[:, 0:N]
    d_c = dbc[:, N : 2 * N]
    sums = jnp.zeros((Q, HL), f32)
    lasts = jnp.zeros((8, HL), f32)
    for c in range(0, DI, CH):
        cols = slice(c, c + CH)
        end = dloc[:, cols] + suf[0:1, cols] * total_of(inc, cols)
        end_low = end.astype(low)
        begin = sbf[:, cols]
        reach = nn(b_rows, end_low)
        held = [reach * xh[:, cols].astype(f32), fold8(end * begin.astype(f32))]
        held = gather_all(held, et[cols, :])
        sums, lasts = sums + held[0], lasts + held[1]
        d_b = d_b + nt(wx[:, cols], end_low)
        d_c = d_c + nt(gdy[:, cols], begin)
        conv_back(dx[:, cols] + spread(tails, e[:, cols]) * reach, c)
    conv_back(jnp.concatenate([d_b, d_c], axis=1), DI)

    flow = sums * tail
    d_cum = rs1[...] - stepv * rs2[...] - flow
    d_last = jnp.exp2(last) * jnp.sum(lasts, axis=0, keepdims=True)
    d_last = d_last + jnp.sum(flow, axis=0, keepdims=True)
    d_log = running_sum(d_cum, True) + d_last
    d_step = rs2[...] + sums * fade - d_log * par[2:3, :]
    d_dt = d_step * jax.nn.sigmoid(dtb[...])
    lane = lax.broadcasted_iota(jnp.int32, d_dt.shape, 1)
    d_dt = jnp.where(lane < H, d_dt, 0.0)
    dcv_o[:, CD:CW] = d_dt.astype(low)
    head_o[:, CD:CW] = jnp.zeros((8, HL), low)

    @pl.when(fresh)
    def keep():
        tail_o[:, CD:CW] = d_dt[Q - 16 :, :]
        for slot, ds in enumerate(slots):
            cols = slice(slot * HALF, (slot + 1) * HALF)
            total = jnp.zeros((16, HALF), f32)
            for k in range(KW):
                total = total + cw[k : k + 1, cols] * ds[pl.ds(zero + (Q - 5 - k), 16), :]
            tail_o[:, cols] = total

    hacc_o[0:8, :] += fold8(d_dt)
    hacc_o[8:16, :] += fold8(d_log * stepv)


def piece_at(me, place, which):
    return source_of(me, place) ^ which


def fold_lanes(value):
    total = value[:, 0:HALF]
    for c in range(HALF, value.shape[1], HALF):
        total = total + value[:, c : c + HALF]
    return total


def early_grad_kernel(scal, nrmt, dz, gn, db, wzc, wo, g0_o, g1_o, na_o, ga_o, part, wide):
    at = pl.program_id(0)

    @pl.when(at == 0)
    def start():
        na_o[...] = jnp.zeros_like(na_o)

    me = scal[0]
    refs = (g0_o, g1_o)
    quarter = DI // EARLY
    cols = pl.ds(pl.multiple_of(at * quarter, HALF), quarter)
    part[...] = nn(nrmt[...], dz[...])
    na_o[...] += fold_lanes(part[...] * wzc[...].astype(f32))
    for place in range(PIECES // 2):
        for which in range(2):
            start = pl.multiple_of(piece_at(me, place, which) * 24, 8)
            refs[which][place, 0, :, cols] = part[pl.ds(start, 24), :].astype(low)
    rows = pl.ds(pl.multiple_of(at * quarter, HALF), quarter)
    wide[rows, :] = tn(gn[...], db[...])
    ga_o[...] = fold_lanes(wide[rows, :] * wo[...].astype(f32))

    @pl.when(at == EARLY - 1)
    def finish():
        for place in range(PIECES // 2):
            for which in range(2):
                start = pl.multiple_of(piece_at(me, place, which) * 48, 8)
                for half in range(2):
                    rows = pl.ds(start + 24 * half, 24)
                    span = slice(half * DI // 2, (half + 1) * DI // 2)
                    refs[which][place, 1, :, span] = wide[rows, :].astype(low)


def row_sums(value):
    ones = jnp.ones((8, value.shape[1]), low)
    total = 0.0
    for _ in range(3):
        top = value.astype(low)
        total = total + nt(ones, top)
        value = value - top.astype(f32)
    return total[0:1, :]


def late_grad_kernel(
    scal, nrmt, dcv, wc, na, tails, returned, cacc, hacc, kacc, ga, par, et,
    g0_o, g1_o, fix_o, vec_o, part, nl,
):
    at = pl.program_id(0)

    @pl.when(at == 0)
    def start():
        nl[...] = na[...]

    refs = (g0_o, g1_o)
    fix_o[...] = dcv[...]
    seqs = tails.shape[0]
    piece_len = dcv.shape[0] // seqs
    for seq in range(seqs):
        back = jnp.concatenate(
            [tails[seq, 0:8, :], tails[seq, 8:16, :] + returned[seq].astype(f32)], axis=0
        )
        fix_o[(seq + 1) * piece_len - 16 : (seq + 1) * piece_len, :] = back.astype(low)
    part[...] = nn(nrmt[...], fix_o[...])
    columns = at * fix_o.shape[1] + lax.broadcasted_iota(jnp.int32, (1, fix_o.shape[1]), 1)
    weight = jnp.where(columns < CD + H, wc[...].astype(f32), 0.0)
    nl[...] += fold_lanes(part[...] * weight)
    for place in range(PIECES // 2):
        for which in range(2):
            start = pl.multiple_of(piece_at(scal[0], place, which) * 24, 8)
            refs[which][place, :, :] = part[pl.ds(start, 24), :].astype(low)

    @pl.when(at == pl.num_programs(0) - 1)
    def finish():
        def put(first, row):
            for c in range(0, row.shape[1], HALF):
                vec_o[first + c // HALF : first + c // HALF + 1, :] = row[:, c : c + HALF]
            return first + row.shape[1] // HALF

        def column_sum(value):
            return jnp.sum(value, axis=0, keepdims=True)

        first = 0
        for k in range(KW + 1):
            first = put(first, column_sum(cacc[8 * k : 8 * k + 8, :]))
        first = put(first, row_sums(ga[...]))
        first = put(first, row_sums(nl[...]))
        first = put(first, column_sum(hacc[0:8, :]))
        first = put(first, -column_sum(hacc[8:16, :]) * par[2:3, :])
        first = put(first, column_sum(gather_heads(kacc[...], et[...])))
        vec_o[first:, :] = jnp.zeros((vec_o.shape[0] - first, HALF), f32)


def input_kernel(dcv, dz, wc, wz, x, cot, gain, past, token, gh_o, done_o, total):
    done_o[...] = jnp.zeros_like(done_o)
    total[...] = nt(dz[...], wz[...]) + nt(dcv[...], wc[...])
    width = x.shape[1]
    for r in range(0, Q, 16):
        rows = slice(r, r + 16)
        wide = x[rows, :].astype(f32)
        scale = lax.rsqrt(jnp.mean(wide * wide, axis=-1, keepdims=True) + epsilon)
        flow = total[rows, :]
        scaled = flow * gain[0:1, :]
        mean = jnp.sum(scaled * wide, axis=-1, keepdims=True) / width
        d_x = scale * scaled - wide * (scale * scale * scale * mean)
        gh_o[rows, :] = (cot[rows, :].astype(f32) + d_x).astype(low)


def call(kernel, grid, inputs, outputs, scratch, flops, name, aliases=None):
    in_specs = [spec for spec, _ in inputs]
    out_specs = [item[0] for item in outputs]
    out_shape = [
        pltpu.VMEM(item[1], item[2]) if len(item) > 3 else jax.ShapeDtypeStruct(item[1], item[2])
        for item in outputs
    ]
    moved = 1 if flops == 1.0 else sum(value.size * value.dtype.itemsize for _, value in inputs)
    return pl.pallas_call(
        kernel,
        grid=(grid,),
        in_specs=in_specs,
        out_specs=out_specs,
        out_shape=out_shape,
        scratch_shapes=scratch,
        input_output_aliases=aliases or {},
        cost_estimate=pl.CostEstimate(flops=int(flops), transcendentals=0, bytes_accessed=moved),
        compiler_params=pltpu.CompilerParams(
            dimension_semantics=("arbitrary",), vmem_limit_bytes=LIMITS[name] * 1024 * 1024
        ),
        name=name,
    )(*[value for _, value in inputs])


def near(value):
    return pltpu.with_memory_space_constraint(value, pltpu.VMEM)


def swap(value, mask):
    return lax.ppermute(value, axes, [(i, i ^ mask) for i in range(PIECES)])


def tie(value, *after):
    return lax.optimization_barrier((value,) + after)[0]


def along(value, masks):
    return jnp.stack([value] + [swap(value, mask) for mask in masks])


def ends_of(plane, value):
    flat = (PIECES // 2,) + value.shape
    return plane.reshape(flat), swap(plane, 1).reshape(flat)


def weave_first(first, second, rim):
    line = tie(along(first, (8, 16, 24)), rim)
    later = along(tie(second, line), (8, 16, 24))
    got = [tie(swap(line, mask), later) for mask in (2, 4, 6)]
    plane = jnp.stack([line] + got)
    return ends_of(plane, first), tie(later, plane)


def weave_second(line, value, token):
    got = [tie(swap(line, mask), token) for mask in (2, 4, 6)]
    plane = jnp.stack([line] + got)
    return ends_of(plane, value), plane


def parts_of(total):
    return total[0], [total[j].astype(low) for j in range(1, 4)]


def merge_core(kept, got):
    total = kept.astype(f32) + got.astype(f32)
    return parts_of(total.reshape((4, 4) + kept.shape[1:]))


def merge(keep, sends, masks, *after):
    got = [swap(value, mask) for value, mask in zip(sends, masks)]
    if after:
        got = lax.optimization_barrier((*got,) + after)[:3]
    got = [value.astype(f32) for value in got]
    return (keep + got[0]) + (got[1] + got[2])


def tie_all(keep, sends, *after):
    out = lax.optimization_barrier((keep, *sends) + after)
    return out[0], list(out[1:4])


def rounded(value):
    return value.astype(low).astype(f32)


def extras(taps, bias, gate, norm):
    left = jnp.concatenate([taps, bias[:, None, :]], axis=1)
    norm = jnp.pad(norm, ((0, 0), (0, gate.shape[1] - norm.shape[1])))
    right = jnp.stack([gate, norm], axis=1)
    left = jnp.pad(left, ((0, 0), (0, 24 - left.shape[1]), (0, 0)))
    right = jnp.pad(right, ((0, 0), (0, 24 - right.shape[1]), (0, 0)))
    return jnp.concatenate([left, right], axis=2)


def order_of_pieces():
    return [(j << 1) | (k << 3) for j in range(4) for k in range(4)]


def relay(ends, ends_low, totals, forward, fillers):
    count = lax.axis_size("seq")
    incoming = None
    results, arrivals, got = [], [], None
    for hop in range(1, count):
        value = ends_low
        if incoming is not None:
            value = (totals * incoming + ends).astype(low)
        route = [(hop - 1, hop)] if forward else [(count - hop, count - hop - 1)]
        arrived = lax.ppermute(value, "seq", route)
        if fillers:
            made = fillers.pop(0)(got)
            results.append(made)
            arrived = tie(arrived, made[-1])
        got = arrived
        arrivals.append(got)
        wide = got.astype(f32)
        incoming = wide if incoming is None else incoming + wide
    while fillers:
        results.append(fillers.pop(0)(got))
    return arrivals or [jnp.zeros_like(ends_low)], results


def total_of(refs, cols):
    total = refs[0][:, cols].astype(f32)
    for ref in refs[1:]:
        total = total + ref[:, cols].astype(f32)
    return total


def per_device(
    hidden,
    lengths,
    norm_gain,
    in_weight,
    conv_weight,
    conv_bias,
    step_bias,
    decay_log,
    skip_gain,
    gate_gain,
    out_weight,
    cotangent,
):
    seqs, piece_len, width = hidden.shape
    groups = piece_len // Q
    blocks = seqs * groups
    rows = seqs * piece_len
    devices = lax.axis_size(axes)
    quick = devices == PIECES
    place = lax.axis_index(axes).astype(jnp.int32)
    me = place if quick else jnp.zeros((), jnp.int32)
    seq_at = lax.axis_index("seq").astype(jnp.int32)
    scal = jnp.concatenate([me[None], seq_at[None], lengths.astype(jnp.int32), me[None] * 0])

    rims = hidden[:, piece_len - RIM :, :]
    seq_size = lax.axis_size("seq")
    rim_in = lax.ppermute(rims, "seq", [(i, i + 1) for i in range(seq_size - 1)])
    inner = hidden.reshape(seqs, groups, Q, width)[:, : groups - 1, Q - RIM :, :]
    halo = jnp.concatenate([rim_in[:, None], inner], axis=1).reshape(blocks, RIM, width)

    w_low = in_weight.astype(low)
    o_low = out_weight.astype(low)
    if quick:
        half = o_low.shape[0] // 2
        packed = jnp.concatenate([o_low[:half], o_low[half:]], axis=1)
        second = jnp.stack([w_low[:, :DI], packed])
        first = jnp.concatenate(
            [
                in_weight[:, DI:],
                extras(
                    conv_weight[None], conv_bias[None], gate_gain[None], norm_gain[None]
                )[0],
            ],
            axis=1,
        ).astype(low)
        (ca, cb_pieces), second_line = weave_first(first, second, rim_in)
        begin = tie(scal, second_line)
    else:
        begin = scal
        order = jnp.array(order_of_pieces(), jnp.int32)
        rows_w = lax.all_gather(w_low, axes, axis=0, tiled=True).reshape(PIECES, -1, E)
        full_taps = lax.all_gather(conv_weight.astype(low), axes, axis=1, tiled=True)
        full = [
            lax.all_gather(value.astype(low), axes, axis=0, tiled=True).reshape(PIECES, -1)
            for value in (conv_bias, gate_gain, norm_gain)
        ]
        extra = extras(full_taps.reshape(KW, PIECES, -1).transpose(1, 0, 2), *full)
        whole = jnp.concatenate([rows_w[:, :, DI:], extra], axis=2)
        ca, cb_pieces = whole[order], whole[order + 1]
        outs = lax.all_gather(o_low, axes, axis=0, tiled=True)
        outs = outs.reshape(PIECES, 2, -1, width).transpose(0, 2, 1, 3).reshape(PIECES, -1, DI)
        whole = jnp.stack([rows_w[:, :, :DI], outs], axis=1)
        za, zb = whole[order], whole[order + 1]

    rate = jnp.exp(decay_log)
    par = jnp.pad(
        jnp.stack([step_bias, rate * 1.4426950408889634, rate, skip_gain]), ((0, 4), (0, HL - H))
    )
    e = jnp.asarray(head_table(), low)
    et = jnp.asarray(np.pad(head_table()[: HL // 2].T, ((0, 0), (0, HL // 2))), low)
    t56 = onehot(HL, CD, H, CD // PIECES)
    t48 = onehot(HL, DI, 80, DI // PIECES)
    t24 = onehot(HL, width, 80, width // PIECES)

    def forth(i):
        return i

    def back(i):
        return (i // groups) * groups + groups - 1 - i % groups

    def tokens(cols, order):
        return pl.BlockSpec((Q, cols), lambda i: (order(i), 0))

    def per_block(height, cols, order):
        return pl.BlockSpec((None, height, cols), lambda i: (order(i), 0, 0))

    def per_seq(height, cols):
        return pl.BlockSpec((None, height, cols), lambda i: (i // groups, 0, 0))

    def fixed(*shape):
        zeros = (0,) * len(shape)
        return pl.BlockSpec(shape, lambda i: zeros, pipeline_mode=pl.Buffered(1))

    def kept(*shape):
        zeros = (0,) * len(shape)
        return pl.BlockSpec(shape, lambda i: zeros)

    scalars = pl.BlockSpec(memory_space=pltpu.SMEM)
    whole = pl.BlockSpec(memory_space=pltpu.VMEM)
    away = pl.BlockSpec(memory_space=pl.ANY)
    flat_hidden = hidden.reshape(rows, width)
    flat_cot = cotangent.reshape(rows, width)

    (nrm, nrmt, cie, sp, xh, xs, wx, bc, step, cum, dtb, cumt, sloc, pre, ends, ends_low, totals, wc, taps, gain_in, gain_gate) = call(
        functools.partial(conv_kernel, groups),
        blocks,
        [
            (scalars, begin),
            (tokens(width, forth), flat_hidden),
            (per_block(RIM, width, forth), halo),
            (fixed(*ca.shape), ca),
            (fixed(*ca.shape), cb_pieces),
            (fixed(HL, CD), t56),
            (fixed(HL, DI), t48),
            (fixed(HL, width), t24),
            (fixed(8, HL), par),
            (fixed(HL, DI), e),
        ],
        [
            (tokens(width, forth), (rows, width), low),
            (pl.BlockSpec((width, Q), lambda i: (0, i)), (width, rows), low),
            (per_block(Q + RIM, CD, forth), (blocks, Q + RIM, CD), low),
            (tokens(CD, forth), (rows, CD), f32),
            (tokens(DI, forth), (rows, DI), low),
            (tokens(DI, forth), (rows, DI), low),
            (tokens(DI, forth), (rows, DI), low),
            (tokens(2 * N, forth), (rows, 2 * N), low),
            (tokens(HL, forth), (rows, HL), f32),
            (tokens(HL, forth), (rows, HL), f32),
            (tokens(HL, forth), (rows, HL), f32),
            (per_block(H, Q, forth), (blocks, H, Q), f32),
            (per_block(N, DI, forth), (blocks, N, DI), f32),
            (per_block(8, DI, forth), (blocks, 8, DI), f32),
            (per_seq(N, DI), (seqs, N, DI), f32),
            (per_seq(N, DI), (seqs, N, DI), low),
            (per_seq(1, DI), (seqs, 1, DI), f32),
            (away, (width, CW), low),
            (kept(8, CD), (8, CD), f32),
            (kept(8, width), (8, width), f32),
            (kept(8, DI), (8, DI), f32),
        ],
        [
            pltpu.VMEM((Q + RIM, width), low),
            pltpu.VMEM((N, DI), f32),
            pltpu.VMEM((8, DI), f32),
            pltpu.VMEM((2, HL + 16, HL), f32),
            pltpu.VMEM((width, CW), low),
            pltpu.SemaphoreType.DMA,
            *[pltpu.VMEM((Q + RIM, HALF), f32)] * (CD // HALF),
        ],
        2.0 * rows * width * CW,
        "conv",
    )
    if quick:
        (za, zb), token = weave_second(second_line, second, cum)
        bc_after = tie(bc, token)
    else:
        bc_after = bc

    def intra_part(got):
        return call(
            intra_kernel,
            blocks,
            [
                (tokens(2 * N, forth), bc_after),
                (tokens(DI, forth), xs),
                (tokens(HL, forth), cum),
                (per_block(H, Q, forth), cumt),
            ],
            [(tokens(DI, forth), (rows, DI), f32)],
            [pltpu.VMEM((Q, Q), f32)],
            2.0 * rows * Q * DI * 2,
            "intra",
        )

    def after(value, got):
        return value if got is None else tie(value, got)

    def project_part(got):
        return call(
            functools.partial(project_kernel, groups),
            blocks,
            [
                (scalars, after(scal, got)),
                (tokens(width, forth), nrm),
                (tokens(width, forth), flat_cot),
                (fixed(*za.shape), za),
                (fixed(*za.shape), zb),
            ],
            [
                (whole, (rows, DI), f32, near),
                (whole, (rows, DI), f32, near),
                (tokens(width, forth), (rows, width), low),
                (away, (width, DI), low),
                (away, (DI, width), low),
            ],
            [
                pltpu.VMEM((width, DI), low),
                pltpu.VMEM((DI, width), low),
                pltpu.SemaphoreType.DMA((2,)),
            ],
            4.0 * rows * width * DI,
            "project",
        )

    incoming, ((intra,), (z, dn, db, wz, wo)) = relay(
        ends, ends_low, totals, True, [intra_part, project_part]
    )

    (out, dz, dy, gdy, gn, sbf, rs1, dloc, suf, back_ends, back_ends_low, back_totals, kacc) = call(
        functools.partial(gate_kernel, groups, len(incoming)),
        blocks,
        [
            (scalars, scal),
            (tokens(DI, back), intra),
            (tokens(DI, back), xh),
            (tokens(2 * N, back), bc),
            (tokens(HL, back), cum),
            (per_block(N, DI, back), sloc),
            (per_block(8, DI, back), pre),
            *[(per_seq(N, DI), value) for value in incoming],
            (whole, near(z)),
            (whole, near(dn)),
            (tokens(width, back), flat_hidden),
            (fixed(DI, width), wo),
            (fixed(8, DI), gain_gate),
            (fixed(8, HL), par),
            (fixed(HL, DI), e),
            (fixed(DI, HL), et),
        ],
        [
            (tokens(width, back), (rows, width), low),
            (tokens(DI, back), (rows, DI), low),
            (tokens(DI, back), (rows, DI), low),
            (tokens(DI, back), (rows, DI), low),
            (tokens(DI, back), (rows, DI), low),
            (per_block(N, DI, back), (blocks, N, DI), low),
            (tokens(HL, back), (rows, HL), f32),
            (per_block(N, DI, back), (blocks, N, DI), f32),
            (per_block(8, DI, back), (blocks, 8, DI), f32),
            (per_seq(N, DI), (seqs, N, DI), f32),
            (per_seq(N, DI), (seqs, N, DI), low),
            (per_seq(1, DI), (seqs, 1, DI), f32),
            (kept(8, DI), (8, DI), f32),
        ],
        [
            pltpu.VMEM((Q, DI), f32),
            pltpu.VMEM((Q, DI), f32),
            pltpu.VMEM((Q, DI), f32),
            pltpu.VMEM((Q, DI), f32),
            pltpu.VMEM((Q, DI), f32),
            pltpu.VMEM((Q, DI), f32),
            pltpu.VMEM((N, DI), f32),
            pltpu.VMEM((8, DI), f32),
            pltpu.VMEM((8, DI), f32),
            pltpu.VMEM((8, DI), f32),
        ],
        4.0 * rows * width * DI,
        "gate",
    )

    def intra_back_part(got):
        return call(
            intra_back_kernel,
            blocks,
            [
                (tokens(2 * N, forth), after(bc, got)),
                (tokens(DI, forth), xs),
                (tokens(DI, forth), xh),
                (tokens(DI, forth), dy),
                (tokens(HL, forth), step),
                (tokens(HL, forth), cum),
                (per_block(H, Q, forth), cumt),
                (fixed(8, HL), par),
                (fixed(HL, DI), e),
                (fixed(DI, HL), et),
            ],
            [
                (tokens(DI, forth), (rows, DI), f32),
                (tokens(2 * N, forth), (rows, 2 * N), f32),
                (tokens(HL, forth), (rows, HL), f32),
            ],
            [pltpu.VMEM((Q, Q), f32), pltpu.VMEM((Q, Q), f32)],
            4.0 * rows * Q * DI * 2,
            "intra_back",
        )

    piece = (PIECES // 2, 2, width // PIECES, DI)

    def early_part(got):
        return call(
            early_grad_kernel,
            EARLY,
            [
                (scalars, after(scal, got)),
                (fixed(width, rows), nrmt),
                (pl.BlockSpec((rows, DI // EARLY), lambda i: (0, i)), dz),
                (pl.BlockSpec((rows, DI // EARLY), lambda i: (0, i)), gn),
                (fixed(rows, width), db),
                (pl.BlockSpec((width, DI // EARLY), lambda i: (0, i)), wz),
                (pl.BlockSpec((DI // EARLY, width), lambda i: (i, 0)), wo),
            ],
            [
                (kept(*piece), piece, low),
                (kept(*piece), piece, low),
                (kept(width, HALF), (width, HALF), f32),
                (pl.BlockSpec((DI // EARLY, HALF), lambda i: (i, 0)), (DI, HALF), f32),
            ],
            [pltpu.VMEM((width, DI // EARLY), f32), pltpu.VMEM((DI, width), f32)],
            6.0 * rows * width * DI,
            "early_grad",
        )

    back_incoming, ((e0, e1, na, ga), (dx, dbc, rs2)) = relay(
        back_ends, back_ends_low, back_totals, False, [early_part, intra_back_part]
    )
    if quick:
        early = merge_core(e0, tie(swap(e1, 1), rs2))
        back_incoming[-1] = tie(back_incoming[-1], *early[1])

    (dcv, cacc, hacc, heads_out, tails_out) = call(
        functools.partial(conv_back_kernel, groups, len(back_incoming)),
        blocks,
        [
            (scalars, scal),
            (per_block(N, DI, back), dloc),
            (per_block(8, DI, back), suf),
            (per_block(N, DI, back), sbf),
            (tokens(DI, back), xh),
            (tokens(DI, back), wx),
            (tokens(DI, back), gdy),
            (tokens(DI, back), dx),
            (tokens(2 * N, back), dbc),
            (tokens(2 * N, back), bc),
            (tokens(HL, back), cum),
            (tokens(HL, back), step),
            (tokens(HL, back), dtb),
            (tokens(HL, back), rs1),
            (tokens(HL, back), rs2),
            *[(per_seq(N, DI), value) for value in back_incoming],
            (per_block(Q + RIM, CD, back), cie),
            (tokens(CD, back), sp),
            (fixed(8, CD), taps),
            (fixed(8, HL), par),
            (fixed(HL, DI), e),
            (fixed(DI, HL), et),
        ],
        [
            (tokens(CW, back), (rows, CW), low),
            (kept(8 * (KW + 1), CD), (8 * (KW + 1), CD), f32),
            (kept(16, HL), (16, HL), f32),
            (per_seq(8, CW), (seqs, 8, CW), low),
            (per_seq(16, CW), (seqs, 16, CW), f32),
        ],
        [
            pltpu.VMEM((8, CD), f32),
            *[pltpu.VMEM((Q + 16, HALF), f32)] * (CD // HALF),
        ],
        6.0 * rows * N * DI,
        "conv_back",
    )
    turn = scal
    if quick:
        early = parts_of(merge(*early, (2, 4, 6), hacc))
        turn = tie(scal, *early[1])
    returned = lax.ppermute(heads_out, "seq", [(i, i - 1) for i in range(1, seq_size)])

    late = (PIECES // 2, width // PIECES, CW)
    late_spec = pl.BlockSpec((PIECES // 2, width // PIECES, CW // LATE), lambda i: (0, 0, i))
    (l0, l1, dcv, vector) = call(
        late_grad_kernel,
        LATE,
        [
            (scalars, turn),
            (fixed(width, rows), nrmt),
            (pl.BlockSpec((rows, CW // LATE), lambda i: (0, i)), dcv),
            (pl.BlockSpec((width, CW // LATE), lambda i: (0, i)), wc),
            (fixed(width, HALF), na),
            (pl.BlockSpec((seqs, 16, CW // LATE), lambda i: (0, 0, i)), tails_out),
            (pl.BlockSpec((seqs, 8, CW // LATE), lambda i: (0, 0, i)), returned),
            (fixed(8 * (KW + 1), CD), cacc),
            (fixed(16, HL), hacc),
            (fixed(8, DI), kacc),
            (fixed(DI, HALF), ga),
            (fixed(8, HL), par),
            (fixed(DI, HL), et),
        ],
        [
            (late_spec, late, low),
            (late_spec, late, low),
            (pl.BlockSpec((rows, CW // LATE), lambda i: (0, i)), (rows, CW), low),
            (kept(96, HALF), (96, HALF), f32),
        ],
        [pltpu.VMEM((width, CW // LATE), f32), pltpu.VMEM((width, HALF), f32)],
        2.0 * rows * width * CW,
        "late_grad",
    )

    def input_part(first, count, past, before, token):
        def order(i):
            return i + first

        return call(
            input_kernel,
            count,
            [
                (tokens(CW, order), dcv),
                (tokens(DI, order), dz),
                (fixed(width, CW), wc),
                (fixed(width, DI), wz),
                (tokens(width, order), flat_hidden),
                (tokens(width, order), flat_cot),
                (fixed(8, width), gain_in if token is None else tie(gain_in, *token)),
                (pl.BlockSpec(memory_space=pl.ANY), past),
                (pl.BlockSpec(memory_space=pl.ANY), before),
            ],
            [
                (tokens(width, order), (rows, width), low),
                (kept(8, HALF), (8, HALF), f32),
            ],
            [pltpu.VMEM((Q, width), f32)],
            1.0,
            "input",
            {7: 0} if first else None,
        )

    half_blocks = max(blocks // 4, 1)
    if quick:
        late_got = swap(l1, 1)
        vector_got = swap(vector, 1)
        gh, done = input_part(0, half_blocks, scal, scal, None)
        late_sum = merge_core(l0, tie(late_got, done))
        vector = vector + tie(vector_got, done)
        early = tie_all(*early, late_sum[1][0])
        gh, done2 = input_part(half_blocks, blocks - half_blocks, gh, done, late_sum[1])
        late_sum = parts_of(merge(*late_sum, (2, 4, 6), done2))
        early = merge(*early, (8, 16, 24), late_sum[1][0])
        vector = tie(vector, late_sum[1][0])
        got = [swap(vector, mask) for mask in (2, 4, 6)]
        vector = tie((vector + got[0]) + (got[1] + got[2]), early)
    else:
        gh, done = input_part(0, blocks, scal, scal, None)

    if quick:
        got = [swap(vector, mask) for mask in (8, 16, 24)]
        vector = (vector + got[0]) + (got[1] + got[2])
        own_late = merge(*late_sum, (8, 16, 24))
        own_z, own_out = early[0], early[1]
        own_out = jnp.concatenate([own_out[:, : DI // 2], own_out[:, DI // 2 :]], axis=0)
    else:
        vector = lax.psum(vector, axes)
        order = jnp.array(order_of_pieces(), jnp.int32)
        inverse = jnp.argsort(jnp.concatenate([order, order + 1]))
        whole = jnp.concatenate([e0, e1])[inverse].astype(f32)
        outs = whole[:, 1].reshape(PIECES, -1, 2, width).transpose(0, 2, 1, 3).reshape(DI, width)
        own_z = lax.psum_scatter(
            whole[:, 0].reshape(width, DI), axes, scatter_dimension=0, tiled=True
        )
        own_out = lax.psum_scatter(outs, axes, scatter_dimension=0, tiled=True)
        whole = jnp.concatenate([l0, l1])[inverse].astype(f32).reshape(width, CW)
        own_late = lax.psum_scatter(whole, axes, scatter_dimension=0, tiled=True)

    def own(value, size, axis):
        return lax.dynamic_slice_in_dim(value, place * size, size, axis)

    tile = CD // HALF
    g_taps = own(vector[: KW * tile].reshape(KW, CD), CD // devices, 1)
    at = KW * tile
    g_bias = own(vector[at : at + tile].reshape(-1), CD // devices, 0)
    at += tile
    g_gate = own(vector[at : at + DI // HALF].reshape(-1), gate_gain.shape[0], 0)
    at += DI // HALF
    g_norm = own(vector[at : at + width // HALF].reshape(-1), norm_gain.shape[0], 0)
    at += width // HALF
    g_gate, g_norm = g_gate / rounded(gate_gain), g_norm / rounded(norm_gain)
    g_in = jnp.concatenate([own_z, own_late[:, : CD + H]], axis=1)
    return (
        out.reshape(hidden.shape),
        gh.reshape(hidden.shape),
        g_norm,
        g_in,
        g_taps,
        g_bias,
        vector[at, :H],
        vector[at + 1, :H],
        vector[at + 2, :H],
        g_gate,
        own_out,
    )


def solution(mesh):
    return jax.shard_map(
        per_device,
        mesh=mesh,
        in_specs=(
            P("dp", "seq", None),
            P("dp"),
            P(("dp", "seq")),
            P(("dp", "seq"), None),
            P(None, ("dp", "seq")),
            P(("dp", "seq")),
            P(),
            P(),
            P(),
            P(("dp", "seq")),
            P(("dp", "seq"), None),
            P("dp", "seq", None),
        ),
        out_specs=(
            P("dp", "seq", None),
            P("dp", "seq", None),
            P(("dp", "seq")),
            P(("dp", "seq"), None),
            P(None, ("dp", "seq")),
            P(("dp", "seq")),
            P(),
            P(),
            P(),
            P(("dp", "seq")),
            P(("dp", "seq"), None),
        ),
        check_vma=False,
    )
```
